32 devices in a mesh: seg: 4 (over y, x), blk: 8 (over z, core).
Axes of the slice: x: 2, y: 2, z: 4, core: 2. Of those that a mesh axis runs over, the one named last changes fastest.
Arguments:
- state: float32 [32, 4, 16, 2304], P(('seg', 'blk')), may hold values from -6 to 6
- metric: float32 [32, 9, 16, 2304], P(('seg', 'blk')), may hold values from -0.4 to 3, as said below
- block_map: int32 [32], replicated, may hold values from 0 to 31, as said below
- links: int32 [32, 6, 4], replicated, may hold values from -1 to 31, as said below
Outputs:
- advanced: float32 [32, 4, 16, 2304], P(('seg', 'blk'))
The draws below stay inside these ranges and needn't reach their ends.
Inputs may be any that keep to these rules, and one draw needn't show every extreme that they name: A permutation of the block numbers; device slot d = s * 8 + p (segment s, position p along its chain) holds block block_map[d]. `links`: entries are (partner block or -1, partner face, r_i, r_x). Face 0 of the block at position p > 0 joins face 1 of the block at position p - 1 of the same segment, face 1 at p < 7 joins face 0 at p + 1, both with zero flags; faces 0 at p = 0 and 1 at p = 7 have partner -1. A block has at most one of faces 2 to 5 with a partner, and some blocks have one; that partner lies at the same position p in another segment, names this block and face back with the same flags. Unused fields of a face with partner -1 are 0. `metric`: entries 0, 4 and 8 of the second dimension are positive.
All inputs are finite; a program needn't handle non-finite values.
Results may differ from the reference program's by a relative error of at most 0.0003.
Values sent between devices are 32-bit elements; how exact they have to be, the bound alone decides.
A program may use at most 64 MiB of HBM per device.

```python
import math
import jax
import jax.numpy as jnp
from jax import lax

LEN = 16
CROSS = 48
SEGS = 4
CHAIN = 8
BLOCKS = 32


def tree_layout(key):
    base = jax.random.fold_in(key, 101)
    subkeys = jax.random.split(base, 5)
    device_blocks = jax.random.permutation(subkeys[0], BLOCKS).astype(jnp.int32)
    row_keys = jax.random.split(subkeys[1], CHAIN)
    pairings = jax.vmap(lambda row_key: jax.random.permutation(row_key, SEGS))(row_keys).astype(jnp.int32)
    slot_of = jnp.argsort(pairings, axis=1).astype(jnp.int32)
    joined_draw = jax.random.randint(subkeys[2], (CHAIN, SEGS // 2), 0, 2).astype(jnp.int32)
    joined_draw = joined_draw.at[0, 0].set(1)
    face_draw = jax.random.randint(subkeys[3], (CHAIN, SEGS), 2, 6).astype(jnp.int32)
    flip_draw = jax.random.randint(subkeys[4], (CHAIN, SEGS // 2, 2), 0, 2).astype(jnp.int32)
    devices = jnp.arange(BLOCKS, dtype=jnp.int32)
    segment = devices // CHAIN
    position = devices % CHAIN
    slot_index = slot_of[position, segment]
    mate_slot = jnp.bitwise_xor(slot_index, 1)
    pair_index = slot_index // 2
    mate_device = pairings[position, mate_slot] * CHAIN + position
    joined = joined_draw[position, pair_index] == 1
    my_face = face_draw[position, slot_index]
    mate_face = face_draw[position, mate_slot]
    flip_pair = flip_draw[position, pair_index]
    zeros = jnp.zeros((BLOCKS,), jnp.int32)
    has_before = position > 0
    has_after = position < CHAIN - 1
    before = jnp.where(has_before, device_blocks[jnp.clip(devices - 1, 0, BLOCKS - 1)], -1)
    after = jnp.where(has_after, device_blocks[jnp.clip(devices + 1, 0, BLOCKS - 1)], -1)
    rows = [jnp.stack([before, jnp.where(has_before, 1, 0), zeros, zeros], axis=1), jnp.stack([after, zeros, zeros, zeros], axis=1)]
    for side in range(2, 6):
        active = joined & (my_face == side)
        rows.append(jnp.stack([jnp.where(active, device_blocks[mate_device], -1), jnp.where(active, mate_face, 0), jnp.where(active, flip_pair[:, 0], 0), jnp.where(active, flip_pair[:, 1], 0)], axis=1))
    by_device = jnp.stack(rows, axis=1).astype(jnp.int32)
    links = jnp.zeros((BLOCKS, 6, 4), jnp.int32).at[device_blocks].set(by_device)
    return (device_blocks, links)


def draw_block_map(key, part):
    return tree_layout(key)[0]


def draw_links(key, part):
    return tree_layout(key)[1]


def draw_metric(key, part):
    subkeys = jax.random.split(jax.random.fold_in(key, 202), 2)
    dims = (BLOCKS, 9, LEN, CROSS * CROSS)
    diagonal_mask = jnp.array([1, 0, 0, 0, 1, 0, 0, 0, 1], jnp.float32).reshape(1, 9, 1, 1)
    diagonal = jnp.exp(jax.random.uniform(subkeys[0], dims, jnp.float32, math.log(0.5), math.log(2.0)))
    off_diagonal = jax.random.uniform(subkeys[1], dims, jnp.float32, -0.4, 0.4)
    return diagonal_mask * diagonal + (1.0 - diagonal_mask) * off_diagonal


def steps_of(rng, shape, shards, smallest, largest):
    level, own = 1.0, jax.random.fold_in(rng, 6)
    for dim, blocks in shards:
        steps = jnp.exp(jax.random.uniform(jax.random.fold_in(own, dim), (blocks,), jnp.float32, smallest / len(shards), largest / len(shards)))
        level = level * jnp.repeat(steps, shape[dim] // blocks).reshape([-1 if axis == dim else 1 for axis in range(len(shape))])
    return level


def scatter_about(own_key, shape, scale, bound, shards=(), kind=jnp.bfloat16):
    loudness = steps_of(own_key, shape, shards, -0.22, 0.18) if shards else 1.0
    drawn = jax.random.normal(own_key, shape, jnp.float32) * scale * loudness
    return jnp.minimum(jnp.maximum(drawn, -bound), bound).astype(kind)


def setup_inputs(seed: int = 0) -> dict:
    streams_of = jax.random.split(jax.random.key(seed), 5)
    state = scatter_about(streams_of[0], (BLOCKS, 4, LEN, CROSS * CROSS), 1.0, 6.0, ((0, 32),), jnp.float32)
    metric = draw_metric(jax.random.fold_in(streams_of[4], 71), 0)
    block_map = draw_block_map(jax.random.fold_in(streams_of[4], 71), 0)
    links = draw_links(jax.random.fold_in(streams_of[4], 71), 0)
    return dict(state=state, metric=metric, block_map=block_map, links=links)


time_step = 0.05
viscosity = 0.2
compress = 1.0


def wall_mirror():
    return jnp.array([-1.0, -1.0, -1.0, 1.0], jnp.float32).reshape(4, 1, 1)


def shifted(extended, direction, offset):
    count = extended.shape[direction] - 4
    return lax.slice_in_dim(extended, offset, offset + count, axis=direction)


def slope(extended, direction):
    return (shifted(extended, direction, 0) - 8.0 * shifted(extended, direction, 1)
            + 8.0 * shifted(extended, direction, 3) - shifted(extended, direction, 4)) / 12.0


def curvature(extended, direction):
    return (-shifted(extended, direction, 0) + 16.0 * shifted(extended, direction, 1)
            - 30.0 * shifted(extended, direction, 2) + 16.0 * shifted(extended, direction, 3)
            - shifted(extended, direction, 4)) / 12.0


def rates(block_state, geometry, padded):
    slopes = [slope(padded[direction], direction + 1) for direction in range(3)]
    bends = [curvature(padded[direction], direction + 1) for direction in range(3)]
    contravariant = []
    metric_norms = []
    for direction in range(3):
        base = 3 * direction
        contravariant.append(geometry[base] * block_state[0] + geometry[base + 1] * block_state[1]
                             + geometry[base + 2] * block_state[2])
        metric_norms.append(geometry[base] * geometry[base] + geometry[base + 1] * geometry[base + 1]
                            + geometry[base + 2] * geometry[base + 2])
    results = []
    for component in range(3):
        convect = sum(contravariant[direction] * slopes[direction][component] for direction in range(3))
        gradient = sum(geometry[3 * direction + component] * slopes[direction][3] for direction in range(3))
        diffuse = sum(metric_norms[direction] * bends[direction][component] for direction in range(3))
        results.append(-convect - gradient + viscosity * diffuse)
    divergence = sum(geometry[3 * direction + component] * slopes[direction][component]
                     for direction in range(3) for component in range(3))
    results.append(-compress * divergence)
    return jnp.stack(results)


def lateral_faces(block_state):
    edge = block_state.shape[2]
    lower_j = jnp.stack([block_state[:, :, 0, :], block_state[:, :, 1, :]])
    upper_j = jnp.stack([block_state[:, :, edge - 1, :], block_state[:, :, edge - 2, :]])
    lower_k = jnp.stack([block_state[:, :, :, 0], block_state[:, :, :, 1]])
    upper_k = jnp.stack([block_state[:, :, :, edge - 1], block_state[:, :, :, edge - 2]])
    return jnp.stack([lower_j, upper_j, lower_k, upper_k])


def pad_lateral(block_state, ghost_layers):
    lower_j = jnp.stack([ghost_layers[0][1], ghost_layers[0][0]], axis=2)
    upper_j = jnp.stack([ghost_layers[1][0], ghost_layers[1][1]], axis=2)
    lower_k = jnp.stack([ghost_layers[2][1], ghost_layers[2][0]], axis=3)
    upper_k = jnp.stack([ghost_layers[3][0], ghost_layers[3][1]], axis=3)
    across_first = jnp.concatenate([lower_j, block_state, upper_j], axis=2)
    across_second = jnp.concatenate([lower_k, block_state, upper_k], axis=3)
    return across_first, across_second


def orient(layers, flip_along, flip_across):
    layers = jnp.where(flip_along == 1, jnp.flip(layers, 2), layers)
    return jnp.where(flip_across == 1, jnp.flip(layers, 3), layers)


def open_rows(block_state):
    mirror = -wall_mirror()
    lower = jnp.stack([mirror * block_state[:, 1], mirror * block_state[:, 0]], axis=1)
    upper = jnp.stack([mirror * block_state[:, -1], mirror * block_state[:, -2]], axis=1)
    return lower, upper


def device_of(block_map, block):
    return jnp.argmax(block_map == jnp.maximum(block, 0)).astype(jnp.int32)


def reference(state, metric, block_map, links):
    count = state.shape[0]
    length = state.shape[2]
    whole = state.reshape(count, 4, length, CROSS, CROSS)
    geometry_all = metric.reshape(count, 9, length, CROSS, CROSS)

    def all_rates(current):
        face_layers = jax.vmap(lateral_faces)(current)

        def per_block(device):
            block_state = current[device]
            entries = links[block_map[device]]
            open_lower, open_upper = open_rows(block_state)
            before = current[device_of(block_map, entries[0, 0])][:, length - 2:]
            after = current[device_of(block_map, entries[1, 0])][:, :2]
            lower = jnp.where(entries[0, 0] >= 0, before, open_lower)
            upper = jnp.where(entries[1, 0] >= 0, after, open_upper)
            along_vessel = jnp.concatenate([lower, block_state, upper], axis=1)
            ghost_layers = []
            for side in range(4):
                entry = entries[2 + side]
                partner = face_layers[device_of(block_map, entry[0]), jnp.clip(entry[1] - 2, 0, 3)]
                partner = orient(partner, entry[2], entry[3])
                ghost_layers.append(jnp.where(entry[0] >= 0, partner, wall_mirror() * face_layers[device, side]))
            across_first, across_second = pad_lateral(block_state, ghost_layers)
            return rates(block_state, geometry_all[device], (along_vessel, across_first, across_second))

        return lax.map(per_block, jnp.arange(count, dtype=jnp.int32))

    first_section = whole + time_step * all_rates(whole)
    advanced = 0.5 * whole + 0.5 * (first_section + time_step * all_rates(first_section))
    return advanced.reshape(state.shape)
```

```python
import functools
import math

import jax
import jax.numpy as jnp
from jax import lax
from jax.experimental import pallas as pl
from jax.experimental.pallas import tpu as pltpu
from jax.sharding import PartitionSpec as P

time_step = 0.05
viscosity = 0.2
compress = 1.0
MESH = pl.DeviceIdType.MESH
LANES = 128
HALF = LANES // 2
WALL = (-1.0, -1.0, -1.0, 1.0)


def split_index(index, size, count):
    quotient = jnp.zeros_like(index)
    for step in range(1, count):
        quotient += (index >= size * step).astype(jnp.int32)
    return quotient, index - size * quotient


def flipped_bits(index, bits):
    bit = 1
    while bit <= bits:
        if bits & bit:
            index = index + bit - 2 * bit * lax.rem(lax.div(index, bit), 2)
        bit *= 2
    return index


def halves(value):
    lead = value.astype(jnp.bfloat16)
    return lead, (value - lead.astype(jnp.float32)).astype(jnp.bfloat16)


def select(flag, yes, no):
    return jnp.where(flag, yes, no)


def ghost_terms(scale, sign, near, metric, values):
    carried = sign * (metric[0] * values[0] + metric[1] * values[1] + metric[2] * values[2])
    norm = viscosity * (metric[0] * metric[0] + metric[1] * metric[1] + metric[2] * metric[2])
    edge = (8.0 * scale) * (2.0 * norm + carried) * near
    outer = scale * (norm + carried)
    return edge, outer, [(scale * sign) * m for m in metric]


def ghost_rates(near, terms, ghosts, moved):
    edge, outer, pull = terms
    eight = 8.0 * near
    slopes = [m - eight * g for g, m in zip(ghosts, moved)]
    parts = [edge * ghosts[c] - outer * moved[c] - pull[c] * slopes[3] for c in range(3)]
    parts.append(-compress * (pull[0] * slopes[0] + pull[1] * slopes[1] + pull[2] * slopes[2]))
    return parts


def kernel(segs, chain, cross, state_hbm, metric_hbm, block_map_hbm, links_hbm, out_ref,
           first, second, geometry, face_matrix, split, k_slope_uvw, k_slope_p, k_bend, slope_k, bend_k,
           row_flip, lane_flip, own_face, own_metric, terms_ref, part_ref,
           ghost_rows, face_out, face_in, block_map, links,
           load_sem, chain_send, chain_recv, face_send, face_recv):
    length, width = out_ref.shape[1], out_ref.shape[2]
    rows = 4 * length
    chunk = math.lcm(cross, LANES)
    chunks = width // chunk
    inner = pl.ds(LANES, width)
    seg, pos = lax.axis_index("seg"), lax.axis_index("blk")
    me = seg * chain + pos
    has_before, has_after = pos > 0, pos < chain - 1
    before, after = lax.rem(pos + chain - 1, chain), lax.rem(pos + 1, chain)
    paired = segs & (segs - 1) == 0
    order = range(segs - 1, 0, -1)

    def to_seg(offset):
        return flipped_bits(seg, offset) if paired else lax.rem(seg + offset, segs)

    def from_seg(offset):
        return flipped_bits(seg, offset) if paired else lax.rem(seg + segs - offset, segs)

    barrier = pltpu.get_barrier_semaphore()
    for offset in order:
        pl.semaphore_signal(barrier, inc=1, device_id={"seg": to_seg(offset)}, device_id_type=MESH)

    @pl.when(has_before)
    def _():
        pl.semaphore_signal(barrier, inc=1, device_id={"blk": before}, device_id_type=MESH)

    @pl.when(has_after)
    def _():
        pl.semaphore_signal(barrier, inc=1, device_id={"blk": after}, device_id_type=MESH)

    load_map = pltpu.make_async_copy(block_map_hbm, block_map, load_sem.at[2])
    load_links = pltpu.make_async_copy(links_hbm, links, load_sem.at[3])
    load_state = pltpu.make_async_copy(state_hbm.at[0], first.at[:, :, inner], load_sem.at[0])
    load_metric = pltpu.make_async_copy(metric_hbm.at[0], geometry, load_sem.at[1])
    load_map.start()
    load_links.start()
    load_state.start()
    load_metric.start()

    lane_row = lax.broadcasted_iota(jnp.int32, (1, LANES), 1)
    face_layer = (lane_row >= HALF).astype(jnp.int32)
    face_place = lane_row - HALF * face_layer
    in_face = face_place < cross
    near_lane = (lane_row < HALF).astype(jnp.float32)

    def build_k():
        here = lax.broadcasted_iota(jnp.int32, (cross, LANES), 0)
        column = lax.broadcasted_iota(jnp.int32, (cross, LANES), 1)
        for group in range(chunk // cross):
            first_row = group * cross
            for tile in range(chunk // LANES):
                lanes = slice(tile * LANES, (tile + 1) * LANES)
                if not first_row // LANES <= tile <= (first_row + cross - 1) // LANES:
                    for matrix in (k_slope_uvw, k_slope_p, k_bend):
                        for top in (first_row, chunk + first_row):
                            matrix[top:top + cross, lanes] = jnp.zeros((cross, LANES), jnp.bfloat16)
                    continue
                there = column + (tile * LANES - first_row)
                there = jnp.where(jnp.logical_and(there >= 0, there < cross), there, 4 * width)
                offset, mirrored = here - there, here + there

                def at(index, value, factor):
                    return jnp.where(index == value, factor, 0.0)

                slope = at(offset, -2, 1.0) + at(offset, -1, -8.0) + at(offset, 1, 8.0) + at(offset, 2, -1.0)
                bend = (at(offset, -2, -1.0) + at(offset, -1, 16.0) + at(offset, 0, -30.0)
                        + at(offset, 1, 16.0) + at(offset, 2, -1.0))
                end = 2 * cross - 2
                wall_slope = (at(mirrored, 0, -8.0) + at(mirrored, 1, 1.0)
                              + at(mirrored, end, 8.0) + at(mirrored, end - 1, -1.0))
                wall_bend = (at(mirrored, 0, 16.0) + at(mirrored, 1, -1.0)
                             + at(mirrored, end, 16.0) + at(mirrored, end - 1, -1.0))
                for matrix, value in ((k_slope_uvw, slope + WALL[0] * wall_slope),
                                      (k_slope_p, slope + WALL[3] * wall_slope),
                                      (k_bend, bend + WALL[0] * wall_bend)):
                    value = value.astype(jnp.bfloat16)
                    matrix[first_row:first_row + cross, lanes] = value
                    matrix[chunk + first_row:chunk + first_row + cross, lanes] = value

    pads = jnp.zeros((4, length, LANES), jnp.float32)
    for padded in (first, second):
        padded[:, :, :LANES] = pads
        padded[:, :, LANES + width:] = pads
    build_k()

    load_map.wait()
    load_links.wait()
    block = block_map[me]
    joins = [links[2 + side, 0, block] >= 0 for side in range(4)]
    partner, flip_along, flip_across = jnp.int32(-1), jnp.int32(0), jnp.int32(0)
    for side in range(4):
        partner = select(joins[side], links[2 + side, 0, block], partner)
        flip_along = select(joins[side], links[2 + side, 2, block], flip_along)
        flip_across = select(joins[side], links[2 + side, 3, block], flip_across)
    any_join = partner >= 0
    on_first = jnp.logical_or(joins[0], joins[1])
    on_second = jnp.logical_or(joins[2], joins[3])
    on_high = jnp.logical_or(joins[1], joins[3])
    comes_from = {offset: block_map[from_seg(offset) * chain + pos] == partner for offset in order}
    face_sign = select(on_high, -1.0, 1.0)

    def build_faces():
        place = jnp.where(in_face, face_place, 0)
        source = place * cross + select(on_high, cross - 1 - face_layer, face_layer)
        source = jnp.where(jnp.logical_and(in_face, on_second), source, -1)
        piece = 2 * LANES
        cells = lax.broadcasted_iota(jnp.int32, (piece, LANES), 0)
        for part in range(width // piece):
            hit = cells == source - part * piece
            face_matrix[part * piece:(part + 1) * piece, :] = hit.astype(jnp.float32).astype(jnp.bfloat16)

    def build_flips():
        target = lax.broadcasted_iota(jnp.int32, (rows, 1), 0)
        component, along_index = split_index(target, length, 4)
        along_index = select(flip_along == 1, length - 1 - along_index, along_index)
        target = component * length + along_index
        hit = lax.broadcasted_iota(jnp.int32, (rows, rows), 1) == target
        row_flip[...] = hit.astype(jnp.float32).astype(jnp.bfloat16)
        place = select(flip_across == 1, cross - 1 - face_place, face_place)
        origin = jnp.where(in_face, face_layer * HALF + place, -1)
        hit = lax.broadcasted_iota(jnp.int32, (LANES, LANES), 0) == origin
        hit = hit.astype(jnp.float32).astype(jnp.bfloat16)
        lane_flip[:LANES, :] = hit
        lane_flip[LANES:, :] = hit

    def flipped(value):
        count = value.shape[0]
        both = jnp.concatenate(halves(value), axis=1)
        both = jnp.dot(row_flip[:count, :count], both, preferred_element_type=jnp.float32)
        return jnp.dot(both.astype(jnp.bfloat16), lane_flip[...], preferred_element_type=jnp.float32)

    def split_up(value):
        count = value.shape[0]
        lead, trail = halves(value)
        split[:count] = lead
        split[count:2 * count] = trail

    def gathered(low, high, count):
        packed = jnp.dot(split[:2 * count], face_matrix[...], preferred_element_type=jnp.float32)
        packed = packed[:count] + packed[count:]
        near, far = LANES - cross, LANES - 2 * cross
        lower = jnp.where(lane_row < HALF, low, pltpu.roll(low, HALF - cross, 1))
        upper = jnp.where(lane_row < HALF, pltpu.roll(high, LANES - near, 1), pltpu.roll(high, HALF - far, 1))
        return jnp.where(on_first, jnp.where(on_high, upper, lower), packed)

    def gather_face(padded):
        low = padded[:, :, LANES:2 * LANES].reshape(rows, LANES)
        high = padded[:, :, width:width + LANES].reshape(rows, LANES)
        return gathered(low, high, rows)

    def spread(value, read, write):
        lead, trail = halves(value)
        both = jnp.concatenate([lead, trail], axis=0)
        near, far = LANES - cross, LANES - 2 * cross
        lower = jnp.where(lane_row < cross, value, pltpu.roll(value, LANES - (HALF - cross), 1))
        lower = jnp.where(jnp.logical_and(lane_row < 2 * cross, jnp.logical_and(on_first, jnp.logical_not(on_high))),
                          lower, 0.0)
        upper = jnp.where(lane_row >= near, pltpu.roll(value, near, 1), pltpu.roll(value, LANES - (HALF - far), 1))
        upper = jnp.where(jnp.logical_and(lane_row >= far, jnp.logical_and(on_first, on_high)), upper, 0.0)
        piece = 2 * LANES
        for part in range(width // piece):
            out = lax.dot_general(both, face_matrix[part * piece:(part + 1) * piece, :],
                                  (((1,), (1,)), ((), ())), preferred_element_type=jnp.float32)
            out = out[:rows] + out[rows:]
            for tile in range(2):
                start = part * piece + tile * LANES
                add = out[:, tile * LANES:(tile + 1) * LANES]
                if start == 0:
                    add = add + lower
                if start == width - LANES:
                    add = add + upper
                for c in range(4):
                    write(c, start, read(c, start) + add[c * length:(c + 1) * length])

    def along_k():
        count = 3 * length
        parts = []
        for step in range(chunks):
            at = slice(step * chunk, (step + 1) * chunk)
            parts.append(jnp.concatenate([split[:rows, at], split[rows:, at]], axis=1))
        velocity = jnp.concatenate([part[:count] for part in parts], axis=0)
        pressure = jnp.concatenate([part[count:] for part in parts], axis=0)
        slope = jnp.dot(velocity, k_slope_uvw[...], preferred_element_type=jnp.float32)
        bend = jnp.dot(velocity, k_bend[...], preferred_element_type=jnp.float32)
        slope_p = jnp.dot(pressure, k_slope_p[...], preferred_element_type=jnp.float32)
        for step in range(chunks):
            at = slice(step * chunk, (step + 1) * chunk)
            slope_k[:3, :, at] = slope[step * count:(step + 1) * count].reshape(3, length, chunk)
            bend_k[:, :, at] = bend[step * count:(step + 1) * count].reshape(3, length, chunk)
            slope_k[3, :, at] = slope_p[step * length:(step + 1) * length]

    def chain_copies(padded, turn):
        to_before = pltpu.make_async_remote_copy(
            padded.at[:, 0:2, inner], ghost_rows.at[turn, :, 6:8], chain_send.at[turn, 0], chain_recv.at[turn, 0],
            device_id={"blk": before}, device_id_type=MESH)
        to_after = pltpu.make_async_remote_copy(
            padded.at[:, length - 2:length, inner], ghost_rows.at[turn, :, 0:2],
            chain_send.at[turn, 1], chain_recv.at[turn, 1], device_id={"blk": after}, device_id_type=MESH)
        return to_before, to_after

    def face_copies(turn):
        return [pltpu.make_async_remote_copy(
            face_out.at[turn], face_in.at[turn, offset - 1], face_send.at[turn, offset - 1],
            face_recv.at[turn, offset - 1], device_id={"seg": to_seg(offset)}, device_id_type=MESH)
            for offset in order]

    def start_chain(padded, turn):
        to_before, to_after = chain_copies(padded, turn)

        @pl.when(has_before)
        def _():
            to_before.start()

        @pl.when(has_after)
        def _():
            to_after.start()

        @pl.when(jnp.logical_not(has_before))
        def _():
            for c in range(4):
                ghost_rows[turn, c, 0:1, :] = -WALL[c] * padded[c, 1:2, inner]
                ghost_rows[turn, c, 1:2, :] = -WALL[c] * padded[c, 0:1, inner]

        @pl.when(jnp.logical_not(has_after))
        def _():
            for c in range(4):
                ghost_rows[turn, c, 6:7, :] = -WALL[c] * padded[c, length - 1:length, inner]
                ghost_rows[turn, c, 7:8, :] = -WALL[c] * padded[c, length - 2:length - 1, inner]

    def await_chain(padded, turn):
        to_before, to_after = chain_copies(padded, turn)

        @pl.when(has_before)
        def _():
            to_after.wait_recv()

        @pl.when(has_after)
        def _():
            to_before.wait_recv()

    def sent_chain(padded, turn):
        to_before, to_after = chain_copies(padded, turn)

        @pl.when(has_before)
        def _():
            to_before.wait_send()

        @pl.when(has_after)
        def _():
            to_after.wait_send()

    lane = lax.broadcasted_iota(jnp.int32, (length, chunk), 1)
    row_of = lax.broadcasted_iota(jnp.int32, (length, chunk), 0)

    def central(value, minus2, minus1, plus1, plus2, bent):
        slope = (minus2 - plus2) + 8.0 * (plus1 - minus1)
        if not bent:
            return slope, None
        return slope, 16.0 * (minus1 + plus1) - (minus2 + plus2) - 30.0 * value

    def along(value, bent):
        def moved(step):
            rolled = pltpu.roll(value, step % length, 0)
            inside = row_of >= step if step > 0 else row_of < length + step
            return jnp.where(inside, rolled, 0.0)
        return central(value, moved(2), moved(1), moved(-1), moved(-2), bent)

    def along_j(wide, value, wall, is_first, is_last, bent):
        def moved(step):
            if step > 0:
                return pltpu.roll(wide[:, :LANES + chunk], step, 1)[:, LANES:]
            return pltpu.roll(wide[:, LANES:], LANES + chunk + step, 1)[:, :chunk]
        minus2, minus1, plus1, plus2 = moved(2 * cross), moved(cross), moved(-cross), moved(-2 * cross)
        m1, m2, p1, p2 = minus1, minus2, plus1, plus2
        if is_first:
            m1 = jnp.where(lane < cross, wall * value, minus1)
            m2 = jnp.where(lane < cross, wall * plus1, jnp.where(lane < 2 * cross, wall * minus1, minus2))
        if is_last:
            p1 = jnp.where(lane >= chunk - cross, wall * value, plus1)
            p2 = jnp.where(lane >= chunk - cross, wall * minus1,
                           jnp.where(lane >= chunk - 2 * cross, wall * plus1, plus2))
        return central(value, m2, m1, p1, p2, bent)

    def rates_of(metric, values, slopes, bends):
        carried = metric[0] * values[0] + metric[1] * values[1] + metric[2] * values[2]
        norm = viscosity * (metric[0] * metric[0] + metric[1] * metric[1] + metric[2] * metric[2])
        parts = [norm * bends[c] - carried * slopes[c] - metric[c] * slopes[3] for c in range(3)]
        parts.append(-compress * (metric[0] * slopes[0] + metric[1] * slopes[1] + metric[2] * slopes[2]))
        return parts

    def inside_rates(padded, finish):
        def at_chunk(start, is_first, is_last):
            at = pl.ds(start, chunk)
            wide = [padded[c, :, pl.ds(start, chunk + 2 * LANES)] for c in range(4)]
            values = [w[:, LANES:LANES + chunk] for w in wide]
            sums = None
            for direction in range(3):
                metric = [geometry[3 * direction + b, :, at] for b in range(3)]
                if direction == 2:
                    slopes = [slope_k[c, :, at] for c in range(4)]
                    bends = [bend_k[c, :, at] for c in range(3)]
                else:
                    slopes, bends = [], []
                    for c in range(4):
                        if direction == 0:
                            slope, bend = along(values[c], c < 3)
                        else:
                            slope, bend = along_j(wide[c], values[c], WALL[c], is_first, is_last, c < 3)
                        slopes.append(slope)
                        bends.append(bend)
                parts = rates_of(metric, values, slopes, bends)
                sums = parts if sums is None else [a + b for a, b in zip(sums, parts)]
            for c in range(4):
                finish(c, start, values[c], sums[c])

        at_chunk(0, True, chunks == 1)
        if chunks > 2:
            @pl.loop(1, chunks - 1)
            def _(step):
                at_chunk(pl.multiple_of(step * chunk, LANES), False, False)
        if chunks > 1:
            at_chunk((chunks - 1) * chunk, False, True)

    sub = lax.broadcasted_iota(jnp.int32, (8, chunk), 0)
    near_row = jnp.where(jnp.logical_or(sub == 0, sub == 7), 1.0, 0.0)
    row_sign = jnp.where(sub < 4, 1.0, -1.0)

    def chain_rates(padded, turn, scale, read, write):
        def body(step, carry):
            start = pl.multiple_of(step * chunk, LANES)
            at = pl.ds(start, chunk)

            def ends(low, high):
                return jnp.where(sub < 4, low, high)

            inside = pl.ds(pl.multiple_of(start + LANES, LANES), chunk)
            values = [ends(padded[c, :8, inside], padded[c, length - 8:, inside]) for c in range(3)]
            metric = [ends(geometry[b, :8, at], geometry[b, length - 8:, at]) for b in range(3)]
            moved = [ghost_rows[turn, c, :, at] for c in range(4)]
            ghosts = [ends(pltpu.roll(m, 7, 0), pltpu.roll(m, 1, 0)) for m in moved]
            sums = ghost_rates(near_row, ghost_terms(scale, row_sign, near_row, metric, values), ghosts, moved)
            for c in range(4):
                write(c, pl.ds(0, 8), start, read(c, pl.ds(0, 8), start) + jnp.where(sub < 2, sums[c], 0.0))
                high = pl.ds(length - 8, 8)
                write(c, high, start, read(c, high, start) + jnp.where(sub >= 6, sums[c], 0.0))
            return carry

        lax.fori_loop(0, chunks, body, 0)

    def at_part(value, c):
        return value[c * length:(c + 1) * length]

    def prepare_terms(scale, metric, own):
        edge, outer, pull = ghost_terms(scale, face_sign, near_lane, [at_part(metric, b) for b in range(3)],
                                        [at_part(own, b) for b in range(3)])
        terms_ref[0] = edge
        terms_ref[1] = outer
        for b in range(3):
            terms_ref[2 + b] = pull[b]

    def face_rates(turn, own):
        received = face_in[turn, order[-1] - 1]
        for offset in order[:-1]:
            received = jnp.where(comes_from[offset], face_in[turn, offset - 1], received)
        ghosts = [at_part(received, c) - WALL[c] * at_part(own, c) for c in range(4)]
        moved = [pltpu.roll(g, HALF, 1) for g in ghosts]
        terms = (terms_ref[0], terms_ref[1], [terms_ref[2 + b] for b in range(3)])
        return jnp.concatenate(ghost_rates(near_lane, terms, ghosts, moved), axis=0)

    def inside_second(start, size):
        return pl.ds(start + LANES if isinstance(start, int) else pl.multiple_of(start + LANES, LANES), size)

    step_one, step_two = time_step / 12.0, 0.5 * time_step / 12.0

    def finish_first(c, start, value, rate):
        second[c, :, inside_second(start, chunk)] = value + step_one * rate

    def finish_second(c, start, value, rate):
        base = first[c, :, inside_second(start, chunk)]
        out_ref[c, :, pl.ds(start, chunk)] = 0.5 * (base + value) + step_two * rate

    def read_second(c, which, start):
        return second[c, which, inside_second(start, chunk)]

    def write_second(c, which, start, value):
        second[c, which, inside_second(start, chunk)] = value

    def read_out(c, which, start):
        return out_ref[c, which, pl.ds(start, chunk)]

    def write_out(c, which, start, value):
        out_ref[c, which, pl.ds(start, chunk)] = value

    def tile_second(c, start):
        return second[c, :, start + LANES:start + 2 * LANES]

    def put_second(c, start, value):
        second[c, :, start + LANES:start + 2 * LANES] = value

    def tile_out(c, start):
        return out_ref[c, :, start:start + LANES]

    def put_out(c, start, value):
        out_ref[c, :, start:start + LANES] = value

    build_faces()
    load_state.wait()
    split_up(first[:, :, inner].reshape(rows, width))
    face_out[0] = gather_face(first)
    pl.semaphore_wait(barrier, segs - 1 + has_before.astype(jnp.int32) + has_after.astype(jnp.int32))
    for copy in face_copies(0):
        copy.start()
    start_chain(first, 0)

    build_flips()
    along_k()
    load_metric.wait()
    inside_rates(first, finish_first)
    metric = jnp.where(on_first, geometry[3:6], geometry[6:9]).reshape(3 * length, width)
    split_up(metric)
    valid = jnp.where(jnp.logical_and(in_face, any_join), 1.0, 0.0)
    own_metric[...] = valid * gathered(metric[:, :LANES], metric[:, width - LANES:], 3 * length)
    own_face[...] = flipped(face_out[0])
    prepare_terms(step_one, flipped(own_metric[...]), own_face[...])

    await_chain(first, 0)
    chain_rates(first, 0, step_one, read_second, write_second)
    split_up(second[:, :, inner].reshape(rows, width))
    part_ref[...] = flipped(gather_face(second))
    for copy in face_copies(0):
        copy.wait_recv()
    added = face_rates(0, own_face[...])
    finished = part_ref[...] + added
    face_out[1] = finished
    for copy in face_copies(1):
        copy.start()

    spread(flipped(added), tile_second, put_second)
    start_chain(second, 1)
    own_face[...] = flipped(finished)
    split_up(second[:, :, inner].reshape(rows, width))
    along_k()
    inside_rates(second, finish_second)
    prepare_terms(step_two, own_metric[...], own_face[...])
    await_chain(second, 1)
    chain_rates(second, 1, step_two, read_out, write_out)
    for copy in face_copies(1):
        copy.wait_recv()
    spread(face_rates(1, own_face[...]), tile_out, put_out)

    for turn, padded in ((0, first), (1, second)):
        for copy in face_copies(turn):
            copy.wait_send()
        sent_chain(padded, turn)


def on_device(state, metric, block_map, links):
    segs, chain = lax.axis_size("seg"), lax.axis_size("blk")
    _, parts, length, width = state.shape
    cross = math.isqrt(width)
    assert cross <= HALF and length == 16
    chunk = math.lcm(cross, LANES)
    links = links.transpose(1, 2, 0)
    f32, bf16, dma = jnp.float32, jnp.bfloat16, pltpu.SemaphoreType.DMA
    result = pl.pallas_call(
        functools.partial(kernel, segs, chain, cross),
        out_shape=pltpu.VMEM((parts, length, width), f32),
        in_specs=[pl.BlockSpec(memory_space=pl.ANY)] * 4,
        out_specs=pl.BlockSpec(memory_space=pltpu.VMEM),
        scratch_shapes=[
            pltpu.VMEM((parts, length, width + 2 * LANES), f32),
            pltpu.VMEM((parts, length, width + 2 * LANES), f32),
            pltpu.VMEM((9, length, width), f32),
            pltpu.VMEM((width, LANES), bf16),
            pltpu.VMEM((2 * parts * length, width), bf16),
            pltpu.VMEM((2 * chunk, chunk), bf16),
            pltpu.VMEM((2 * chunk, chunk), bf16),
            pltpu.VMEM((2 * chunk, chunk), bf16),
            pltpu.VMEM((parts, length, width), f32),
            pltpu.VMEM((parts - 1, length, width), f32),
            pltpu.VMEM((parts * length, parts * length), bf16),
            pltpu.VMEM((2 * LANES, LANES), bf16),
            pltpu.VMEM((parts * length, LANES), f32),
            pltpu.VMEM(((parts - 1) * length, LANES), f32),
            pltpu.VMEM((5, length, LANES), f32),
            pltpu.VMEM((parts * length, LANES), f32),
            pltpu.VMEM((2, parts, 8, width), f32),
            pltpu.VMEM((2, parts * length, LANES), f32),
            pltpu.VMEM((2, segs - 1, parts * length, LANES), f32),
            pltpu.SMEM(block_map.shape, jnp.int32),
            pltpu.SMEM(links.shape, jnp.int32),
            dma((4,)), dma((2, 2)), dma((2, 2)), dma((2, segs - 1)), dma((2, segs - 1)),
        ],
        compiler_params=pltpu.CompilerParams(collective_id=0, has_side_effects=True),
    )(state, metric, block_map, links)
    return result.reshape(state.shape)


def solution(mesh):
    in_specs = (P(("seg", "blk"), None, None, None), P(("seg", "blk"), None, None, None), P(), P())
    out_specs = P(("seg", "blk"), None, None, None)
    return jax.shard_map(
        on_device, mesh=mesh, in_specs=in_specs, out_specs=out_specs, check_vma=False
    )
```

```python
import functools
import math

import jax
import jax.numpy as jnp
from jax import lax
from jax.experimental import pallas as pl
from jax.experimental.pallas import tpu as pltpu
from jax.sharding import PartitionSpec as P

time_step = 0.05
viscosity = 0.2
compress = 1.0
MESH = pl.DeviceIdType.MESH
LANES = 128
HALF = LANES // 2
WALL = (-1.0, -1.0, -1.0, 1.0)


def split_index(index, size, count):
    quotient = jnp.zeros_like(index)
    for step in range(1, count):
        quotient += (index >= size * step).astype(jnp.int32)
    return quotient, index - size * quotient


def flipped_bits(index, bits):
    bit = 1
    while bit <= bits:
        if bits & bit:
            index = index + bit - 2 * bit * lax.rem(lax.div(index, bit), 2)
        bit *= 2
    return index


def halves(value):
    lead = value.astype(jnp.bfloat16)
    return lead, (value - lead.astype(jnp.float32)).astype(jnp.bfloat16)


def select(flag, yes, no):
    return jnp.where(flag, yes, no)


def ghost_terms(scale, sign, near, metric, values):
    carried = sign * (metric[0] * values[0] + metric[1] * values[1] + metric[2] * values[2])
    norm = viscosity * (metric[0] * metric[0] + metric[1] * metric[1] + metric[2] * metric[2])
    edge = (8.0 * scale) * (2.0 * norm + carried) * near
    outer = scale * (norm + carried)
    return edge, outer, [(scale * sign) * m for m in metric]


def ghost_rates(near, terms, ghosts, moved):
    edge, outer, pull = terms
    eight = 8.0 * near
    slopes = [m - eight * g for g, m in zip(ghosts, moved)]
    parts = [edge * ghosts[c] - outer * moved[c] - pull[c] * slopes[3] for c in range(3)]
    parts.append(-compress * (pull[0] * slopes[0] + pull[1] * slopes[1] + pull[2] * slopes[2]))
    return parts


def kernel(segs, chain, cross, state_hbm, metric_hbm, block_map_hbm, links_hbm, out_ref,
           first, second, geometry, side_matrix, face_matrix, split, metric_split,
           k_slope_uvw, k_slope_p, k_bend, slope_k, bend_k,
           row_flip, lane_flip, terms_ref, added_ref, theirs_ref, turned_ref,
           ghost_rows, end_rows, delta_out, delta_in, face_out, face_in, block_map, links,
           load_sem, chain_send, chain_recv, face_send, face_recv):
    length, width = out_ref.shape[1], out_ref.shape[2]
    rows = 4 * length
    chunk = math.lcm(cross, LANES)
    chunks = width // chunk
    inner = pl.ds(LANES, width)
    seg, pos = lax.axis_index("seg"), lax.axis_index("blk")
    me = seg * chain + pos
    has_before, has_after = pos > 0, pos < chain - 1
    before, after = lax.rem(pos + chain - 1, chain), lax.rem(pos + 1, chain)
    paired = segs & (segs - 1) == 0
    order = range(segs - 1, 0, -1)

    def to_seg(offset):
        return flipped_bits(seg, offset) if paired else lax.rem(seg + offset, segs)

    def from_seg(offset):
        return flipped_bits(seg, offset) if paired else lax.rem(seg + segs - offset, segs)

    barrier = pltpu.get_barrier_semaphore()
    for offset in order:
        pl.semaphore_signal(barrier, inc=1, device_id={"seg": to_seg(offset)}, device_id_type=MESH)

    @pl.when(has_before)
    def _():
        pl.semaphore_signal(barrier, inc=1, device_id={"blk": before}, device_id_type=MESH)

    @pl.when(has_after)
    def _():
        pl.semaphore_signal(barrier, inc=1, device_id={"blk": after}, device_id_type=MESH)

    load_map = pltpu.make_async_copy(block_map_hbm, block_map, load_sem.at[2])
    load_links = pltpu.make_async_copy(links_hbm, links, load_sem.at[3])
    load_state = pltpu.make_async_copy(state_hbm.at[0], first.at[:, :, inner], load_sem.at[0])
    load_metric = pltpu.make_async_copy(metric_hbm.at[0], geometry, load_sem.at[1])
    load_map.start()
    load_links.start()
    load_state.start()
    load_metric.start()

    lane_row = lax.broadcasted_iota(jnp.int32, (1, LANES), 1)
    face_layer = (lane_row >= HALF).astype(jnp.int32)
    face_place = lane_row - HALF * face_layer
    in_face = face_place < cross
    near_lane = (lane_row < HALF).astype(jnp.float32)

    def build_k():
        here = lax.broadcasted_iota(jnp.int32, (cross, LANES), 0)
        column = lax.broadcasted_iota(jnp.int32, (cross, LANES), 1)
        for group in range(chunk // cross):
            first_row = group * cross
            for tile in range(chunk // LANES):
                lanes = slice(tile * LANES, (tile + 1) * LANES)
                if not first_row // LANES <= tile <= (first_row + cross - 1) // LANES:
                    for matrix in (k_slope_uvw, k_slope_p, k_bend):
                        for top in (first_row, chunk + first_row):
                            matrix[top:top + cross, lanes] = jnp.zeros((cross, LANES), jnp.bfloat16)
                    continue
                there = column + (tile * LANES - first_row)
                there = jnp.where(jnp.logical_and(there >= 0, there < cross), there, 4 * width)
                offset, mirrored = here - there, here + there

                def at(index, value, factor):
                    return jnp.where(index == value, factor, 0.0)

                slope = at(offset, -2, 1.0) + at(offset, -1, -8.0) + at(offset, 1, 8.0) + at(offset, 2, -1.0)
                bend = (at(offset, -2, -1.0) + at(offset, -1, 16.0) + at(offset, 0, -30.0)
                        + at(offset, 1, 16.0) + at(offset, 2, -1.0))
                end = 2 * cross - 2
                wall_slope = (at(mirrored, 0, -8.0) + at(mirrored, 1, 1.0)
                              + at(mirrored, end, 8.0) + at(mirrored, end - 1, -1.0))
                wall_bend = (at(mirrored, 0, 16.0) + at(mirrored, 1, -1.0)
                             + at(mirrored, end, 16.0) + at(mirrored, end - 1, -1.0))
                for matrix, value in ((k_slope_uvw, slope + WALL[0] * wall_slope),
                                      (k_slope_p, slope + WALL[3] * wall_slope),
                                      (k_bend, bend + WALL[0] * wall_bend)):
                    value = value.astype(jnp.bfloat16)
                    matrix[first_row:first_row + cross, lanes] = value
                    matrix[chunk + first_row:chunk + first_row + cross, lanes] = value

    pads = jnp.zeros((4, length, LANES), jnp.float32)
    for padded in (first, second):
        padded[:, :, :LANES] = pads
        padded[:, :, LANES + width:] = pads
    build_k()

    def build_sides():
        piece = 2 * LANES
        cells = lax.broadcasted_iota(jnp.int32, (piece, LANES), 0)
        place = jnp.where(in_face, face_place, 0)
        for side, spot in enumerate((face_layer, cross - 1 - face_layer)):
            source = jnp.where(in_face, place * cross + spot, -1)
            for part in range(width // piece):
                hit = (cells == source - part * piece).astype(jnp.float32).astype(jnp.bfloat16)
                side_matrix[part * piece:(part + 1) * piece, side * LANES:(side + 1) * LANES] = hit

    build_sides()

    load_map.wait()
    load_links.wait()
    block = block_map[me]

    def joined_side(number):
        return [links[2 + side, 0, number] >= 0 for side in range(4)]

    joins = joined_side(block)
    partner, partner_face = jnp.int32(-1), jnp.int32(0)
    flip_along, flip_across = jnp.int32(0), jnp.int32(0)
    for side in range(4):
        partner = select(joins[side], links[2 + side, 0, block], partner)
        partner_face = select(joins[side], links[2 + side, 1, block], partner_face)
        flip_along = select(joins[side], links[2 + side, 2, block], flip_along)
        flip_across = select(joins[side], links[2 + side, 3, block], flip_across)
    any_join = partner >= 0
    on_first = jnp.logical_or(joins[0], joins[1])
    on_second = jnp.logical_or(joins[2], joins[3])
    on_high = jnp.logical_or(joins[1], joins[3])
    joins_before = joined_side(block_map[seg * chain + before])
    joins_after = joined_side(block_map[seg * chain + after])
    comes_from = {offset: block_map[from_seg(offset) * chain + pos] == partner for offset in order}
    face_sign = select(on_high, -1.0, 1.0)
    partner_sign = select(jnp.logical_or(partner_face == 3, partner_face == 5), -1.0, 1.0)

    def build_faces():
        use_low = select(jnp.logical_and(on_second, jnp.logical_not(on_high)), 1.0, 0.0)
        use_high = select(jnp.logical_and(on_second, on_high), 1.0, 0.0)
        low = jnp.full((1, LANES), use_low).astype(jnp.bfloat16)
        high = jnp.full((1, LANES), use_high).astype(jnp.bfloat16)
        face_matrix[...] = side_matrix[:, :LANES] * low + side_matrix[:, LANES:] * high

    def build_flips():
        target = lax.broadcasted_iota(jnp.int32, (rows, 1), 0)
        component, along_index = split_index(target, length, 4)
        along_index = select(flip_along == 1, length - 1 - along_index, along_index)
        target = component * length + along_index
        hit = lax.broadcasted_iota(jnp.int32, (rows, rows), 1) == target
        row_flip[...] = hit.astype(jnp.float32).astype(jnp.bfloat16)
        place = select(flip_across == 1, cross - 1 - face_place, face_place)
        origin = jnp.where(in_face, face_layer * HALF + place, -1)
        hit = lax.broadcasted_iota(jnp.int32, (LANES, LANES), 0) == origin
        hit = hit.astype(jnp.float32).astype(jnp.bfloat16)
        lane_flip[:LANES, :] = hit
        lane_flip[LANES:, :] = hit

    def flipped(value):
        count = value.shape[0]
        both = jnp.concatenate(halves(value), axis=1)
        both = jnp.dot(row_flip[:count, :count], both, preferred_element_type=jnp.float32)
        return jnp.dot(both.astype(jnp.bfloat16), lane_flip[...], preferred_element_type=jnp.float32)

    def split_up(value, into):
        count = value.shape[0]
        lead, trail = halves(value)
        into[:count] = lead
        into[count:2 * count] = trail

    def gathered(low, high, count, source):
        packed = jnp.dot(source[...], face_matrix[...], preferred_element_type=jnp.float32)
        packed = packed[:count] + packed[count:]
        near, far = LANES - cross, LANES - 2 * cross
        lower = jnp.where(lane_row < HALF, low, pltpu.roll(low, HALF - cross, 1))
        upper = jnp.where(lane_row < HALF, pltpu.roll(high, LANES - near, 1), pltpu.roll(high, HALF - far, 1))
        return jnp.where(on_first, jnp.where(on_high, upper, lower), packed)

    def gather_face(padded):
        low = padded[:, :, LANES:2 * LANES].reshape(rows, LANES)
        high = padded[:, :, width:width + LANES].reshape(rows, LANES)
        return gathered(low, high, rows, split)

    near, far = LANES - cross, LANES - 2 * cross

    def to_lower(value):
        return jnp.where(lane_row < cross, value, pltpu.roll(value, LANES - (HALF - cross), 1))

    def to_upper(value):
        return jnp.where(lane_row >= near, pltpu.roll(value, near, 1), pltpu.roll(value, LANES - (HALF - far), 1))

    def spread(value, both, matrix, lower, upper, write):
        count = value.shape[0]
        lead, trail = halves(both)
        both = jnp.concatenate([lead, trail], axis=0)
        piece = 2 * LANES
        for part in range(width // piece):
            out = lax.dot_general(both, matrix[part * piece:(part + 1) * piece, :],
                                  (((1,), (1,)), ((), ())), preferred_element_type=jnp.float32)
            out = out[:count] + out[count:]
            for tile in range(2):
                start = part * piece + tile * LANES
                add = out[:, tile * LANES:(tile + 1) * LANES]
                if start == 0:
                    add = add + lower
                if start == width - LANES:
                    add = add + upper
                write(start, add)

    def spread_face(value, read, write):
        on_low = jnp.logical_not(on_high)
        lower = jnp.where(jnp.logical_and(lane_row < 2 * cross, jnp.logical_and(on_first, on_low)), to_lower(value), 0.0)
        upper = jnp.where(jnp.logical_and(lane_row >= far, jnp.logical_and(on_first, on_high)), to_upper(value), 0.0)

        def put(start, add):
            for c in range(4):
                write(c, start, read(c, start) + add[c * length:(c + 1) * length])

        spread(value, value, face_matrix, lower, upper, put)

    def spread_delta():
        end_row = lax.broadcasted_iota(jnp.int32, (8, LANES), 0)
        wanted = jnp.logical_or(jnp.logical_and(end_row < 2, has_before), jnp.logical_and(end_row >= 6, has_after))
        value = jnp.concatenate([jnp.where(wanted, delta_in[c], 0.0) for c in range(4)], axis=0)

        def mask(side):
            flag = [select(flags[side], 1.0, 0.0) for flags in (joins_before, joins_after)]
            one = jnp.where(end_row < 4, flag[0], flag[1])
            return jnp.concatenate([one] * 4, axis=0)

        lower = jnp.where(lane_row < 2 * cross, to_lower(value) * mask(0), 0.0)
        upper = jnp.where(lane_row >= far, to_upper(value) * mask(1), 0.0)
        both = jnp.concatenate([value * mask(2), value * mask(3)], axis=1)

        def put(start, add):
            for c in range(4):
                at = slice(start, start + LANES)
                ghost_rows[1, c, :, at] = ghost_rows[1, c, :, at] + add[c * 8:(c + 1) * 8]

        spread(value, both, side_matrix, lower, upper, put)

    def along_k():
        count = 3 * length
        parts = []
        for step in range(chunks):
            at = slice(step * chunk, (step + 1) * chunk)
            parts.append(jnp.concatenate([split[:rows, at], split[rows:, at]], axis=1))
        velocity = jnp.concatenate([part[:count] for part in parts], axis=0)
        pressure = jnp.concatenate([part[count:] for part in parts], axis=0)
        slope = jnp.dot(velocity, k_slope_uvw[...], preferred_element_type=jnp.float32)
        bend = jnp.dot(velocity, k_bend[...], preferred_element_type=jnp.float32)
        slope_p = jnp.dot(pressure, k_slope_p[...], preferred_element_type=jnp.float32)
        for step in range(chunks):
            at = slice(step * chunk, (step + 1) * chunk)
            slope_k[:3, :, at] = slope[step * count:(step + 1) * count].reshape(3, length, chunk)
            bend_k[:, :, at] = bend[step * count:(step + 1) * count].reshape(3, length, chunk)
            slope_k[3, :, at] = slope_p[step * length:(step + 1) * length]

    def chain_copies(kind):
        if kind == 0:
            low, high = first.at[:, 0:2, inner], first.at[:, length - 2:length, inner]
        else:
            source = end_rows if kind == 1 else delta_out
            low, high = source.at[:, 0:2], source.at[:, 6:8]
        target = delta_in if kind == 2 else ghost_rows.at[kind]
        to_before = pltpu.make_async_remote_copy(
            low, target.at[:, 6:8], chain_send.at[kind, 0], chain_recv.at[kind, 0],
            device_id={"blk": before}, device_id_type=MESH)
        to_after = pltpu.make_async_remote_copy(
            high, target.at[:, 0:2], chain_send.at[kind, 1], chain_recv.at[kind, 1],
            device_id={"blk": after}, device_id_type=MESH)
        return to_before, to_after

    def face_copies(kind):
        used = pl.ds(0, 3 * length if kind == 1 else rows)
        return [pltpu.make_async_remote_copy(
            face_out.at[kind, used], face_in.at[kind, offset - 1, used], face_send.at[kind, offset - 1],
            face_recv.at[kind, offset - 1], device_id={"seg": to_seg(offset)}, device_id_type=MESH)
            for offset in order]

    def start_faces(kind):
        for copy in face_copies(kind):
            copy.start()

    def await_faces(kind):
        for copy in face_copies(kind):
            copy.wait_recv()

    def start_chain(kind):
        to_before, to_after = chain_copies(kind)

        @pl.when(has_before)
        def _():
            to_before.start()

        @pl.when(has_after)
        def _():
            to_after.start()

    def open_ends(padded, turn):
        @pl.when(jnp.logical_not(has_before))
        def _():
            for c in range(4):
                ghost_rows[turn, c, 0:1, :] = -WALL[c] * padded[c, 1:2, inner]
                ghost_rows[turn, c, 1:2, :] = -WALL[c] * padded[c, 0:1, inner]

        @pl.when(jnp.logical_not(has_after))
        def _():
            for c in range(4):
                ghost_rows[turn, c, 6:7, :] = -WALL[c] * padded[c, length - 1:length, inner]
                ghost_rows[turn, c, 7:8, :] = -WALL[c] * padded[c, length - 2:length - 1, inner]

    def await_chain(kind):
        to_before, to_after = chain_copies(kind)

        @pl.when(has_before)
        def _():
            to_after.wait_recv()

        @pl.when(has_after)
        def _():
            to_before.wait_recv()

    def sent_chain(kind):
        to_before, to_after = chain_copies(kind)

        @pl.when(has_before)
        def _():
            to_before.wait_send()

        @pl.when(has_after)
        def _():
            to_after.wait_send()

    lane = lax.broadcasted_iota(jnp.int32, (length, chunk), 1)
    row_of = lax.broadcasted_iota(jnp.int32, (length, chunk), 0)

    def central(value, minus2, minus1, plus1, plus2, bent):
        slope = (minus2 - plus2) + 8.0 * (plus1 - minus1)
        if not bent:
            return slope, None
        return slope, 16.0 * (minus1 + plus1) - (minus2 + plus2) - 30.0 * value

    def along(value, bent):
        def moved(step):
            rolled = pltpu.roll(value, step % length, 0)
            inside = row_of >= step if step > 0 else row_of < length + step
            return jnp.where(inside, rolled, 0.0)
        return central(value, moved(2), moved(1), moved(-1), moved(-2), bent)

    def along_j(wide, value, wall, is_first, is_last, bent):
        def moved(step):
            if step > 0:
                return pltpu.roll(wide[:, :LANES + chunk], step, 1)[:, LANES:]
            return pltpu.roll(wide[:, LANES:], LANES + chunk + step, 1)[:, :chunk]
        minus2, minus1, plus1, plus2 = moved(2 * cross), moved(cross), moved(-cross), moved(-2 * cross)
        m1, m2, p1, p2 = minus1, minus2, plus1, plus2
        if is_first:
            m1 = jnp.where(lane < cross, wall * value, minus1)
            m2 = jnp.where(lane < cross, wall * plus1, jnp.where(lane < 2 * cross, wall * minus1, minus2))
        if is_last:
            p1 = jnp.where(lane >= chunk - cross, wall * value, plus1)
            p2 = jnp.where(lane >= chunk - cross, wall * minus1,
                           jnp.where(lane >= chunk - 2 * cross, wall * plus1, plus2))
        return central(value, m2, m1, p1, p2, bent)

    def rates_of(metric, values, slopes, bends):
        carried = metric[0] * values[0] + metric[1] * values[1] + metric[2] * values[2]
        norm = viscosity * (metric[0] * metric[0] + metric[1] * metric[1] + metric[2] * metric[2])
        parts = [norm * bends[c] - carried * slopes[c] - metric[c] * slopes[3] for c in range(3)]
        parts.append(-compress * (metric[0] * slopes[0] + metric[1] * slopes[1] + metric[2] * slopes[2]))
        return parts

    def inside_rates(padded, finish):
        def at_chunk(start, is_first, is_last):
            at = pl.ds(start, chunk)
            wide = [padded[c, :, pl.ds(start, chunk + 2 * LANES)] for c in range(4)]
            values = [w[:, LANES:LANES + chunk] for w in wide]
            sums = None
            for direction in range(3):
                metric = [geometry[3 * direction + b, :, at] for b in range(3)]
                if direction == 2:
                    slopes = [slope_k[c, :, at] for c in range(4)]
                    bends = [bend_k[c, :, at] for c in range(3)]
                else:
                    slopes, bends = [], []
                    for c in range(4):
                        if direction == 0:
                            slope, bend = along(values[c], c < 3)
                        else:
                            slope, bend = along_j(wide[c], values[c], WALL[c], is_first, is_last, c < 3)
                        slopes.append(slope)
                        bends.append(bend)
                parts = rates_of(metric, values, slopes, bends)
                sums = parts if sums is None else [a + b for a, b in zip(sums, parts)]
            for c in range(4):
                finish(c, start, values[c], sums[c])

        at_chunk(0, True, chunks == 1)
        if chunks > 2:
            @pl.loop(1, chunks - 1)
            def _(step):
                at_chunk(pl.multiple_of(step * chunk, LANES), False, False)
        if chunks > 1:
            at_chunk((chunks - 1) * chunk, False, True)

    sub = lax.broadcasted_iota(jnp.int32, (8, chunk), 0)
    near_row = jnp.where(jnp.logical_or(sub == 0, sub == 7), 1.0, 0.0)
    row_sign = jnp.where(sub < 4, 1.0, -1.0)

    def chain_rates(padded, turn, scale, read, write, keep=None):
        def body(step, carry):
            start = pl.multiple_of(step * chunk, LANES)
            at = pl.ds(start, chunk)

            def ends(low, high):
                return jnp.where(sub < 4, low, high)

            inside = pl.ds(pl.multiple_of(start + LANES, LANES), chunk)
            values = [ends(padded[c, :8, inside], padded[c, length - 8:, inside]) for c in range(3)]
            metric = [ends(geometry[b, :8, at], geometry[b, length - 8:, at]) for b in range(3)]
            moved = [ghost_rows[turn, c, :, at] for c in range(4)]
            ghosts = [ends(pltpu.roll(m, 7, 0), pltpu.roll(m, 1, 0)) for m in moved]
            sums = ghost_rates(near_row, ghost_terms(scale, row_sign, near_row, metric, values), ghosts, moved)
            low, high = pl.ds(0, 8), pl.ds(length - 8, 8)
            for c in range(4):
                low_new = read(c, low, start) + jnp.where(sub < 2, sums[c], 0.0)
                high_new = read(c, high, start) + jnp.where(sub >= 6, sums[c], 0.0)
                write(c, low, start, low_new)
                write(c, high, start, high_new)
                if keep is not None:
                    keep[c, :, at] = ends(low_new, high_new)
            return carry

        lax.fori_loop(0, chunks, body, 0)

    def at_part(value, c):
        return value[c * length:(c + 1) * length]

    def terms_of(scale, sign, metric, own):
        return ghost_terms(scale, sign, near_lane, [at_part(metric, b) for b in range(3)],
                           [at_part(own, b) for b in range(3)])

    def prepare_terms(scale, metric, own):
        edge, outer, pull = terms_of(scale, face_sign, metric, own)
        terms_ref[0] = edge
        terms_ref[1] = outer
        for b in range(3):
            terms_ref[2 + b] = pull[b]

    def own_terms():
        return terms_ref[0], terms_ref[1], [terms_ref[2 + b] for b in range(3)]

    def received(kind, count):
        value = face_in[kind, order[-1] - 1, :count]
        for offset in order[:-1]:
            value = jnp.where(comes_from[offset], face_in[kind, offset - 1, :count], value)
        return value

    def face_rates(terms, theirs, own):
        ghosts = [at_part(theirs, c) - WALL[c] * at_part(own, c) for c in range(4)]
        moved = [pltpu.roll(g, HALF, 1) for g in ghosts]
        return jnp.concatenate(ghost_rates(near_lane, terms, ghosts, moved), axis=0)

    def inside_second(start, size):
        return pl.ds(start + LANES if isinstance(start, int) else pl.multiple_of(start + LANES, LANES), size)

    step_one, step_two = time_step / 12.0, 0.5 * time_step / 12.0

    def finish_first(c, start, value, rate):
        second[c, :, inside_second(start, chunk)] = value + step_one * rate

    def finish_second(c, start, value, rate):
        base = first[c, :, inside_second(start, chunk)]
        out_ref[c, :, pl.ds(start, chunk)] = 0.5 * (base + value) + step_two * rate

    def read_second(c, which, start):
        return second[c, which, inside_second(start, chunk)]

    def write_second(c, which, start, value):
        second[c, which, inside_second(start, chunk)] = value

    def read_out(c, which, start):
        return out_ref[c, which, pl.ds(start, chunk)]

    def write_out(c, which, start, value):
        out_ref[c, which, pl.ds(start, chunk)] = value

    def tile_second(c, start):
        return second[c, :, start + LANES:start + 2 * LANES]

    def put_second(c, start, value):
        second[c, :, start + LANES:start + 2 * LANES] = value

    def tile_out(c, start):
        return out_ref[c, :, start:start + LANES]

    def put_out(c, start, value):
        out_ref[c, :, start:start + LANES] = value

    build_faces()
    load_state.wait()
    split_up(first[:, :, inner].reshape(rows, width), split)
    face_out[0] = gather_face(first)
    pl.semaphore_wait(barrier, segs - 1 + has_before.astype(jnp.int32) + has_after.astype(jnp.int32))
    start_faces(0)
    start_chain(0)

    load_metric.wait()
    metric = jnp.where(on_first, geometry[3:6], geometry[6:9]).reshape(3 * length, width)
    split_up(metric, metric_split)
    valid = jnp.where(jnp.logical_and(in_face, any_join), 1.0, 0.0)
    own_metric = valid * gathered(metric[:, :LANES], metric[:, width - LANES:], 3 * length, metric_split)
    face_out[1, :3 * length] = own_metric
    start_faces(1)
    open_ends(first, 0)
    build_flips()
    prepare_terms(step_one, own_metric, face_out[0])
    along_k()
    inside_rates(first, finish_first)

    await_chain(0)
    chain_rates(first, 0, step_one, read_second, write_second, end_rows)
    start_chain(1)
    split_up(second[:, :, inner].reshape(rows, width), split)
    face_out[2] = gather_face(second)
    start_faces(2)

    turned_ref[...] = flipped(face_out[0])
    await_faces(0)
    added = face_rates(own_terms(), flipped(received(0, rows)), face_out[0])
    for c in range(4):
        delta_out[c] = jnp.where(lax.broadcasted_iota(jnp.int32, (8, LANES), 0) < 4,
                                 added[c * length:c * length + 8], added[(c + 1) * length - 8:(c + 1) * length])
    start_chain(2)
    added_ref[...] = face_out[2] + added
    spread_face(added, tile_second, put_second)
    open_ends(second, 1)
    split_up(second[:, :, inner].reshape(rows, width), split)
    along_k()
    inside_rates(second, finish_second)
    prepare_terms(step_two, face_out[1, :3 * length], added_ref[...])
    await_faces(1)
    their_face = received(0, rows)
    their_terms = terms_of(step_one, partner_sign, received(1, 3 * length), their_face)
    theirs_ref[...] = face_rates(their_terms, turned_ref[...], their_face)

    await_chain(1)
    await_chain(2)
    spread_delta()
    chain_rates(second, 1, step_two, read_out, write_out)
    await_faces(2)
    their_face = flipped(received(2, rows) + theirs_ref[...])
    spread_face(face_rates(own_terms(), their_face, added_ref[...]), tile_out, put_out)

    for kind in range(3):
        for copy in face_copies(kind):
            copy.wait_send()
        sent_chain(kind)


def on_device(state, metric, block_map, links):
    segs, chain = lax.axis_size("seg"), lax.axis_size("blk")
    _, parts, length, width = state.shape
    cross = math.isqrt(width)
    assert cross <= HALF and length == 16
    chunk = math.lcm(cross, LANES)
    links = links.transpose(1, 2, 0)
    f32, bf16, dma = jnp.float32, jnp.bfloat16, pltpu.SemaphoreType.DMA
    result = pl.pallas_call(
        functools.partial(kernel, segs, chain, cross),
        out_shape=pltpu.VMEM((parts, length, width), f32),
        in_specs=[pl.BlockSpec(memory_space=pl.ANY)] * 4,
        out_specs=pl.BlockSpec(memory_space=pltpu.VMEM),
        scratch_shapes=[
            pltpu.VMEM((parts, length, width + 2 * LANES), f32),
            pltpu.VMEM((parts, length, width + 2 * LANES), f32),
            pltpu.VMEM((9, length, width), f32),
            pltpu.VMEM((width, 2 * LANES), bf16),
            pltpu.VMEM((width, LANES), bf16),
            pltpu.VMEM((2 * parts * length, width), bf16),
            pltpu.VMEM((2 * (parts - 1) * length, width), bf16),
            pltpu.VMEM((2 * chunk, chunk), bf16),
            pltpu.VMEM((2 * chunk, chunk), bf16),
            pltpu.VMEM((2 * chunk, chunk), bf16),
            pltpu.VMEM((parts, length, width), f32),
            pltpu.VMEM((parts - 1, length, width), f32),
            pltpu.VMEM((parts * length, parts * length), bf16),
            pltpu.VMEM((2 * LANES, LANES), bf16),
            pltpu.VMEM((5, length, LANES), f32),
            pltpu.VMEM((parts * length, LANES), f32),
            pltpu.VMEM((parts * length, LANES), f32),
            pltpu.VMEM((parts * length, LANES), f32),
            pltpu.VMEM((2, parts, 8, width), f32),
            pltpu.VMEM((parts, 8, width), f32),
            pltpu.VMEM((parts, 8, LANES), f32),
            pltpu.VMEM((parts, 8, LANES), f32),
            pltpu.VMEM((3, parts * length, LANES), f32),
            pltpu.VMEM((3, segs - 1, parts * length, LANES), f32),
            pltpu.SMEM(block_map.shape, jnp.int32),
            pltpu.SMEM(links.shape, jnp.int32),
            dma((4,)), dma((3, 2)), dma((3, 2)), dma((3, segs - 1)), dma((3, segs - 1)),
        ],
        compiler_params=pltpu.CompilerParams(collective_id=0, has_side_effects=True),
    )(state, metric, block_map, links)
    return result.reshape(state.shape)


def solution(mesh):
    in_specs = (P(("seg", "blk"), None, None, None), P(("seg", "blk"), None, None, None), P(), P())
    out_specs = P(("seg", "blk"), None, None, None)
    return jax.shard_map(
        on_device, mesh=mesh, in_specs=in_specs, out_specs=out_specs, check_vma=False
    )
```

```python
import functools
import math

import jax
import jax.numpy as jnp
from jax import lax
from jax.experimental import pallas as pl
from jax.experimental.pallas import tpu as pltpu
from jax.sharding import PartitionSpec as P

time_step = 0.05
viscosity = 0.2
compress = 1.0
MESH = pl.DeviceIdType.MESH
LANES = 128
HALF = LANES // 2
WALL = (-1.0, -1.0, -1.0, 1.0)


def split_index(index, size, count):
    quotient = jnp.zeros_like(index)
    for step in range(1, count):
        quotient += (index >= size * step).astype(jnp.int32)
    return quotient, index - size * quotient


def take(value, index, axis):
    numbers = lax.GatherDimensionNumbers(
        offset_dims=(), collapsed_slice_dims=(axis,), start_index_map=(axis,),
        operand_batching_dims=(1 - axis,), start_indices_batching_dims=(1 - axis,))
    return lax.gather(value, index[..., None], numbers, slice_sizes=(1, 1),
                      mode=lax.GatherScatterMode.PROMISE_IN_BOUNDS)


def flipped_bits(index, bits):
    bit = 1
    while bit <= bits:
        if bits & bit:
            index = index + bit - 2 * bit * lax.rem(lax.div(index, bit), 2)
        bit *= 2
    return index


def halves(value):
    lead = value.astype(jnp.bfloat16)
    return lead, (value - lead.astype(jnp.float32)).astype(jnp.bfloat16)


def select(flag, yes, no):
    return jnp.where(flag, yes, no)


def ghost_terms(scale, sign, near, metric, values):
    carried = sign * (metric[0] * values[0] + metric[1] * values[1] + metric[2] * values[2])
    norm = viscosity * (metric[0] * metric[0] + metric[1] * metric[1] + metric[2] * metric[2])
    edge = (8.0 * scale) * (2.0 * norm + carried) * near
    outer = scale * (norm + carried)
    return edge, outer, [(scale * sign) * m for m in metric]


def ghost_rates(near, terms, ghosts, moved):
    edge, outer, pull = terms
    eight = 8.0 * near
    slopes = [m - eight * g for g, m in zip(ghosts, moved)]
    parts = [edge * ghosts[c] - outer * moved[c] - pull[c] * slopes[3] for c in range(3)]
    parts.append(-compress * (pull[0] * slopes[0] + pull[1] * slopes[1] + pull[2] * slopes[2]))
    return parts


def kernel(segs, chain, cross, state_hbm, metric_hbm, block_map_hbm, links_hbm, out_ref,
           first, second, geometry, face_index, face_mask, delta_index, delta_mask, split,
           k_slope_uvw, k_slope_p, k_bend, slope_k, bend_k,
           terms_ref, added_ref, theirs_ref, turned_ref,
           ghost_rows, end_rows, delta_out, delta_in, face_out, face_in, block_map, links,
           load_sem, chain_send, chain_recv, face_send, face_recv):
    length, width = out_ref.shape[1], out_ref.shape[2]
    rows = 4 * length
    chunk = math.lcm(cross, LANES)
    chunks = width // chunk
    inner = pl.ds(LANES, width)
    seg, pos = lax.axis_index("seg"), lax.axis_index("blk")
    me = seg * chain + pos
    has_before, has_after = pos > 0, pos < chain - 1
    before, after = lax.rem(pos + chain - 1, chain), lax.rem(pos + 1, chain)
    paired = segs & (segs - 1) == 0
    order = range(segs - 1, 0, -1)

    def to_seg(offset):
        return flipped_bits(seg, offset) if paired else lax.rem(seg + offset, segs)

    def from_seg(offset):
        return flipped_bits(seg, offset) if paired else lax.rem(seg + segs - offset, segs)

    barrier = pltpu.get_barrier_semaphore()
    for offset in order:
        pl.semaphore_signal(barrier, inc=1, device_id={"seg": to_seg(offset)}, device_id_type=MESH)

    @pl.when(has_before)
    def _():
        pl.semaphore_signal(barrier, inc=1, device_id={"blk": before}, device_id_type=MESH)

    @pl.when(has_after)
    def _():
        pl.semaphore_signal(barrier, inc=1, device_id={"blk": after}, device_id_type=MESH)

    load_map = pltpu.make_async_copy(block_map_hbm, block_map, load_sem.at[2])
    load_links = pltpu.make_async_copy(links_hbm, links, load_sem.at[3])
    load_state = pltpu.make_async_copy(state_hbm.at[0], first.at[:, :, inner], load_sem.at[0])
    load_metric = pltpu.make_async_copy(metric_hbm.at[0], geometry, load_sem.at[1])
    load_map.start()
    load_links.start()
    load_state.start()
    load_metric.start()

    lane_row = lax.broadcasted_iota(jnp.int32, (1, LANES), 1)
    face_layer = (lane_row >= HALF).astype(jnp.int32)
    face_place = lane_row - HALF * face_layer
    in_face = face_place < cross
    near_lane = (lane_row < HALF).astype(jnp.float32)

    def build_k():
        here = lax.broadcasted_iota(jnp.int32, (cross, LANES), 0)
        column = lax.broadcasted_iota(jnp.int32, (cross, LANES), 1)
        for group in range(chunk // cross):
            first_row = group * cross
            for tile in range(chunk // LANES):
                lanes = slice(tile * LANES, (tile + 1) * LANES)
                if not first_row // LANES <= tile <= (first_row + cross - 1) // LANES:
                    for matrix in (k_slope_uvw, k_slope_p, k_bend):
                        for top in (first_row, chunk + first_row):
                            matrix[top:top + cross, lanes] = jnp.zeros((cross, LANES), jnp.bfloat16)
                    continue
                there = column + (tile * LANES - first_row)
                there = jnp.where(jnp.logical_and(there >= 0, there < cross), there, 4 * width)
                offset, mirrored = here - there, here + there

                def at(index, value, factor):
                    return jnp.where(index == value, factor, 0.0)

                slope = at(offset, -2, 1.0) + at(offset, -1, -8.0) + at(offset, 1, 8.0) + at(offset, 2, -1.0)
                bend = (at(offset, -2, -1.0) + at(offset, -1, 16.0) + at(offset, 0, -30.0)
                        + at(offset, 1, 16.0) + at(offset, 2, -1.0))
                end = 2 * cross - 2
                wall_slope = (at(mirrored, 0, -8.0) + at(mirrored, 1, 1.0)
                              + at(mirrored, end, 8.0) + at(mirrored, end - 1, -1.0))
                wall_bend = (at(mirrored, 0, 16.0) + at(mirrored, 1, -1.0)
                             + at(mirrored, end, 16.0) + at(mirrored, end - 1, -1.0))
                for matrix, value in ((k_slope_uvw, slope + WALL[0] * wall_slope),
                                      (k_slope_p, slope + WALL[3] * wall_slope),
                                      (k_bend, bend + WALL[0] * wall_bend)):
                    value = value.astype(jnp.bfloat16)
                    matrix[first_row:first_row + cross, lanes] = value
                    matrix[chunk + first_row:chunk + first_row + cross, lanes] = value

    pads = jnp.zeros((4, length, LANES), jnp.float32)
    for padded in (first, second):
        padded[:, :, :LANES] = pads
        padded[:, :, LANES + width:] = pads
    build_k()

    load_map.wait()
    load_links.wait()
    block = block_map[me]

    def joined_side(number):
        return [links[2 + side, 0, number] >= 0 for side in range(4)]

    joins = joined_side(block)
    partner, partner_face = jnp.int32(-1), jnp.int32(0)
    flip_along, flip_across = jnp.int32(0), jnp.int32(0)
    for side in range(4):
        partner = select(joins[side], links[2 + side, 0, block], partner)
        partner_face = select(joins[side], links[2 + side, 1, block], partner_face)
        flip_along = select(joins[side], links[2 + side, 2, block], flip_along)
        flip_across = select(joins[side], links[2 + side, 3, block], flip_across)
    any_join = partner >= 0
    on_first = jnp.logical_or(joins[0], joins[1])
    on_second = jnp.logical_or(joins[2], joins[3])
    on_high = jnp.logical_or(joins[1], joins[3])
    joins_before = joined_side(block_map[seg * chain + before])
    joins_after = joined_side(block_map[seg * chain + after])
    comes_from = {offset: block_map[from_seg(offset) * chain + pos] == partner for offset in order}
    face_sign = select(on_high, -1.0, 1.0)
    partner_sign = select(jnp.logical_or(partner_face == 3, partner_face == 5), -1.0, 1.0)

    lane_of = lax.broadcasted_iota(jnp.int32, (8, LANES), 1)
    row_in = lax.broadcasted_iota(jnp.int32, (8, LANES), 0)
    layer_of = (lane_of >= HALF).astype(jnp.int32)
    place_of = lane_of - HALF * layer_of
    face_lane = place_of < cross

    def spread_index(tile, high):
        start = tile * LANES
        row = start // cross
        spot = lane_of + (start - row * cross)
        place = jnp.full((8, LANES), row, jnp.int32)
        for step in range(1, LANES // cross + 2):
            past = spot >= step * cross
            place = place + past.astype(jnp.int32)
        spot = lane_of + start - place * cross
        layer = jnp.where(high, cross - 1 - spot, spot)
        return jnp.where(layer < 2, place + HALF * layer, -1)

    def build_spread(index_ref, mask_ref, high, used):
        for tile in range(width // LANES):
            index = jnp.where(used, spread_index(tile, high), -1)
            mask_ref[tile] = jnp.where(index >= 0, 1.0, 0.0)
            index_ref[tile] = jnp.maximum(index, 0)

    def build_faces():
        build_spread(face_index, face_mask, jnp.full((8, LANES), select(on_high, 1, 0)) > 0,
                     jnp.full((8, LANES), select(on_second, 1, 0)) > 0)

    def build_delta():
        def chosen(sides):
            flags = [select(jnp.logical_or(near_joins[sides[0]], near_joins[sides[1]]), 1, 0)
                     for near_joins in (joins_before, joins_after)]
            return jnp.where(row_in < 4, flags[0], flags[1]) > 0

        build_spread(delta_index, delta_mask, chosen((1, 3)), chosen((2, 3)))

    source_of = jnp.where(face_lane, place_of, 0) * cross + select(on_high, cross - 1 - layer_of, layer_of)
    source_tile, source_lane = split_index(source_of, LANES, width // LANES)
    flip_rows = select(flip_along == 1, 7 - row_in, row_in)
    flip_lanes = jnp.where(face_lane, layer_of * HALF + select(flip_across == 1, cross - 1 - place_of, place_of), lane_of)

    def by_rows(value, function):
        return jnp.concatenate([function(value[at:at + 8]) for at in range(0, value.shape[0], 8)], axis=0)

    def flipped(value):
        parts = []
        for at in range(0, value.shape[0], length):
            low, high = value[at:at + 8], value[at + 8:at + 16]
            for half in (select(flip_along == 1, high, low), select(flip_along == 1, low, high)):
                parts.append(take(take(half, flip_rows, 0), flip_lanes, 1))
        return jnp.concatenate(parts, axis=0)

    def split_up(value, into):
        count = value.shape[0]
        lead, trail = halves(value)
        into[:count] = lead
        into[count:2 * count] = trail

    def gathered(low, high, tile_of):
        packed = None
        for tile in range(width // LANES):
            part = by_rows(tile_of(tile), lambda x: take(x, source_lane, 1))
            here = jnp.concatenate([source_tile == tile] * (part.shape[0] // 8), axis=0)
            packed = part if packed is None else jnp.where(here, part, packed)
        near, far = LANES - cross, LANES - 2 * cross
        lower = jnp.where(lane_row < HALF, low, pltpu.roll(low, HALF - cross, 1))
        upper = jnp.where(lane_row < HALF, pltpu.roll(high, LANES - near, 1), pltpu.roll(high, HALF - far, 1))
        return jnp.where(on_first, jnp.where(on_high, upper, lower), packed)

    def gather_face(padded):
        def tile_of(tile):
            start = LANES + tile * LANES
            return padded[:, :, start:start + LANES].reshape(rows, LANES)

        return gathered(tile_of(0), tile_of(width // LANES - 1), tile_of)

    def gather_metric():
        def tile_of(tile, base=6):
            return geometry[base:base + 3, :, tile * LANES:(tile + 1) * LANES].reshape(3 * length, LANES)

        return gathered(tile_of(0, 3), tile_of(width // LANES - 1, 3), tile_of)

    near, far = LANES - cross, LANES - 2 * cross

    def to_lower(value):
        return jnp.where(lane_row < cross, value, pltpu.roll(value, LANES - (HALF - cross), 1))

    def to_upper(value):
        return jnp.where(lane_row >= near, pltpu.roll(value, near, 1), pltpu.roll(value, LANES - (HALF - far), 1))

    def spread(value, index_ref, mask_ref, lower, upper, write):
        for tile in range(width // LANES):
            index, mask = index_ref[tile], mask_ref[tile]
            add = by_rows(value, lambda x: take(x, index, 1) * mask)
            if tile == 0:
                add = add + lower
            if tile == width // LANES - 1:
                add = add + upper
            write(tile * LANES, add)

    def spread_face(value, read, write):
        on_low = jnp.logical_not(on_high)
        lower = jnp.where(jnp.logical_and(lane_row < 2 * cross, jnp.logical_and(on_first, on_low)), to_lower(value), 0.0)
        upper = jnp.where(jnp.logical_and(lane_row >= far, jnp.logical_and(on_first, on_high)), to_upper(value), 0.0)

        def put(start, add):
            for c in range(4):
                write(c, start, read(c, start) + add[c * length:(c + 1) * length])

        spread(value, face_index, face_mask, lower, upper, put)

    def spread_delta():
        end_row = lax.broadcasted_iota(jnp.int32, (8, LANES), 0)
        wanted = jnp.logical_or(jnp.logical_and(end_row < 2, has_before), jnp.logical_and(end_row >= 6, has_after))
        value = jnp.concatenate([jnp.where(wanted, delta_in[c], 0.0) for c in range(4)], axis=0)

        def mask(side):
            flag = [select(flags[side], 1.0, 0.0) for flags in (joins_before, joins_after)]
            one = jnp.where(end_row < 4, flag[0], flag[1])
            return jnp.concatenate([one] * 4, axis=0)

        lower = jnp.where(lane_row < 2 * cross, to_lower(value) * mask(0), 0.0)
        upper = jnp.where(lane_row >= far, to_upper(value) * mask(1), 0.0)
        def put(start, add):
            for c in range(4):
                at = slice(start, start + LANES)
                ghost_rows[1, c, :, at] = ghost_rows[1, c, :, at] + add[c * 8:(c + 1) * 8]

        spread(value, delta_index, delta_mask, lower, upper, put)

    def along_k():
        count = 3 * length
        parts = []
        for step in range(chunks):
            at = slice(step * chunk, (step + 1) * chunk)
            parts.append(jnp.concatenate([split[:rows, at], split[rows:, at]], axis=1))
        velocity = jnp.concatenate([part[:count] for part in parts], axis=0)
        pressure = jnp.concatenate([part[count:] for part in parts], axis=0)
        slope = jnp.dot(velocity, k_slope_uvw[...], preferred_element_type=jnp.float32)
        bend = jnp.dot(velocity, k_bend[...], preferred_element_type=jnp.float32)
        slope_p = jnp.dot(pressure, k_slope_p[...], preferred_element_type=jnp.float32)
        for step in range(chunks):
            at = slice(step * chunk, (step + 1) * chunk)
            slope_k[:3, :, at] = slope[step * count:(step + 1) * count].reshape(3, length, chunk)
            bend_k[:, :, at] = bend[step * count:(step + 1) * count].reshape(3, length, chunk)
            slope_k[3, :, at] = slope_p[step * length:(step + 1) * length]

    def chain_copies(kind):
        if kind == 0:
            low, high = first.at[:, 0:2, inner], first.at[:, length - 2:length, inner]
        else:
            source = end_rows if kind == 1 else delta_out
            low, high = source.at[:, 0:2], source.at[:, 6:8]
        target = delta_in if kind == 2 else ghost_rows.at[kind]
        to_before = pltpu.make_async_remote_copy(
            low, target.at[:, 6:8], chain_send.at[kind, 0], chain_recv.at[kind, 0],
            device_id={"blk": before}, device_id_type=MESH)
        to_after = pltpu.make_async_remote_copy(
            high, target.at[:, 0:2], chain_send.at[kind, 1], chain_recv.at[kind, 1],
            device_id={"blk": after}, device_id_type=MESH)
        return to_before, to_after

    def face_copies(kind):
        used = pl.ds(0, 3 * length if kind == 1 else rows)
        return [pltpu.make_async_remote_copy(
            face_out.at[kind, used], face_in.at[kind, offset - 1, used], face_send.at[kind, offset - 1],
            face_recv.at[kind, offset - 1], device_id={"seg": to_seg(offset)}, device_id_type=MESH)
            for offset in order]

    def start_faces(kind):
        for copy in face_copies(kind):
            copy.start()

    def await_faces(kind):
        for copy in face_copies(kind):
            copy.wait_recv()

    def start_chain(kind):
        to_before, to_after = chain_copies(kind)

        @pl.when(has_before)
        def _():
            to_before.start()

        @pl.when(has_after)
        def _():
            to_after.start()

    def open_ends(padded, turn):
        @pl.when(jnp.logical_not(has_before))
        def _():
            for c in range(4):
                ghost_rows[turn, c, 0:1, :] = -WALL[c] * padded[c, 1:2, inner]
                ghost_rows[turn, c, 1:2, :] = -WALL[c] * padded[c, 0:1, inner]

        @pl.when(jnp.logical_not(has_after))
        def _():
            for c in range(4):
                ghost_rows[turn, c, 6:7, :] = -WALL[c] * padded[c, length - 1:length, inner]
                ghost_rows[turn, c, 7:8, :] = -WALL[c] * padded[c, length - 2:length - 1, inner]

    def await_chain(kind):
        to_before, to_after = chain_copies(kind)

        @pl.when(has_before)
        def _():
            to_after.wait_recv()

        @pl.when(has_after)
        def _():
            to_before.wait_recv()

    def sent_chain(kind):
        to_before, to_after = chain_copies(kind)

        @pl.when(has_before)
        def _():
            to_before.wait_send()

        @pl.when(has_after)
        def _():
            to_after.wait_send()

    lane = lax.broadcasted_iota(jnp.int32, (length, chunk), 1)
    row_of = lax.broadcasted_iota(jnp.int32, (length, chunk), 0)

    def central(value, minus2, minus1, plus1, plus2, bent):
        slope = (minus2 - plus2) + 8.0 * (plus1 - minus1)
        if not bent:
            return slope, None
        return slope, 16.0 * (minus1 + plus1) - (minus2 + plus2) - 30.0 * value

    def along(value, bent):
        def moved(step):
            rolled = pltpu.roll(value, step % length, 0)
            inside = row_of >= step if step > 0 else row_of < length + step
            return jnp.where(inside, rolled, 0.0)
        return central(value, moved(2), moved(1), moved(-1), moved(-2), bent)

    def along_j(wide, value, wall, is_first, is_last, bent):
        def moved(step):
            if step > 0:
                return pltpu.roll(wide[:, :LANES + chunk], step, 1)[:, LANES:]
            return pltpu.roll(wide[:, LANES:], LANES + chunk + step, 1)[:, :chunk]
        minus2, minus1, plus1, plus2 = moved(2 * cross), moved(cross), moved(-cross), moved(-2 * cross)
        m1, m2, p1, p2 = minus1, minus2, plus1, plus2
        if is_first:
            m1 = jnp.where(lane < cross, wall * value, minus1)
            m2 = jnp.where(lane < cross, wall * plus1, jnp.where(lane < 2 * cross, wall * minus1, minus2))
        if is_last:
            p1 = jnp.where(lane >= chunk - cross, wall * value, plus1)
            p2 = jnp.where(lane >= chunk - cross, wall * minus1,
                           jnp.where(lane >= chunk - 2 * cross, wall * plus1, plus2))
        return central(value, m2, m1, p1, p2, bent)

    def rates_of(metric, values, slopes, bends):
        carried = metric[0] * values[0] + metric[1] * values[1] + metric[2] * values[2]
        norm = viscosity * (metric[0] * metric[0] + metric[1] * metric[1] + metric[2] * metric[2])
        parts = [norm * bends[c] - carried * slopes[c] - metric[c] * slopes[3] for c in range(3)]
        parts.append(-compress * (metric[0] * slopes[0] + metric[1] * slopes[1] + metric[2] * slopes[2]))
        return parts

    def inside_rates(padded, finish):
        def at_chunk(start, is_first, is_last):
            at = pl.ds(start, chunk)
            wide = [padded[c, :, pl.ds(start, chunk + 2 * LANES)] for c in range(4)]
            values = [w[:, LANES:LANES + chunk] for w in wide]
            sums = None
            for direction in range(3):
                metric = [geometry[3 * direction + b, :, at] for b in range(3)]
                if direction == 2:
                    slopes = [slope_k[c, :, at] for c in range(4)]
                    bends = [bend_k[c, :, at] for c in range(3)]
                else:
                    slopes, bends = [], []
                    for c in range(4):
                        if direction == 0:
                            slope, bend = along(values[c], c < 3)
                        else:
                            slope, bend = along_j(wide[c], values[c], WALL[c], is_first, is_last, c < 3)
                        slopes.append(slope)
                        bends.append(bend)
                parts = rates_of(metric, values, slopes, bends)
                sums = parts if sums is None else [a + b for a, b in zip(sums, parts)]
            for c in range(4):
                finish(c, start, values[c], sums[c])

        at_chunk(0, True, chunks == 1)
        if chunks > 2:
            @pl.loop(1, chunks - 1)
            def _(step):
                at_chunk(pl.multiple_of(step * chunk, LANES), False, False)
        if chunks > 1:
            at_chunk((chunks - 1) * chunk, False, True)

    sub = lax.broadcasted_iota(jnp.int32, (8, chunk), 0)
    near_row = jnp.where(jnp.logical_or(sub == 0, sub == 7), 1.0, 0.0)
    row_sign = jnp.where(sub < 4, 1.0, -1.0)

    def chain_rates(padded, turn, scale, read, write, keep=None):
        def body(step, carry):
            start = pl.multiple_of(step * chunk, LANES)
            at = pl.ds(start, chunk)

            def ends(low, high):
                return jnp.where(sub < 4, low, high)

            inside = pl.ds(pl.multiple_of(start + LANES, LANES), chunk)
            values = [ends(padded[c, :8, inside], padded[c, length - 8:, inside]) for c in range(3)]
            metric = [ends(geometry[b, :8, at], geometry[b, length - 8:, at]) for b in range(3)]
            moved = [ghost_rows[turn, c, :, at] for c in range(4)]
            ghosts = [ends(pltpu.roll(m, 7, 0), pltpu.roll(m, 1, 0)) for m in moved]
            sums = ghost_rates(near_row, ghost_terms(scale, row_sign, near_row, metric, values), ghosts, moved)
            low, high = pl.ds(0, 8), pl.ds(length - 8, 8)
            for c in range(4):
                low_new = read(c, low, start) + jnp.where(sub < 2, sums[c], 0.0)
                high_new = read(c, high, start) + jnp.where(sub >= 6, sums[c], 0.0)
                write(c, low, start, low_new)
                write(c, high, start, high_new)
                if keep is not None:
                    keep[c, :, at] = ends(low_new, high_new)
            return carry

        lax.fori_loop(0, chunks, body, 0)

    def at_part(value, c):
        return value[c * length:(c + 1) * length]

    def terms_of(scale, sign, metric, own):
        return ghost_terms(scale, sign, near_lane, [at_part(metric, b) for b in range(3)],
                           [at_part(own, b) for b in range(3)])

    def prepare_terms(scale, metric, own):
        edge, outer, pull = terms_of(scale, face_sign, metric, own)
        terms_ref[0] = edge
        terms_ref[1] = outer
        for b in range(3):
            terms_ref[2 + b] = pull[b]

    def own_terms():
        return terms_ref[0], terms_ref[1], [terms_ref[2 + b] for b in range(3)]

    def received(kind, count):
        value = face_in[kind, order[-1] - 1, :count]
        for offset in order[:-1]:
            value = jnp.where(comes_from[offset], face_in[kind, offset - 1, :count], value)
        return value

    def face_rates(terms, theirs, own):
        ghosts = [at_part(theirs, c) - WALL[c] * at_part(own, c) for c in range(4)]
        moved = [pltpu.roll(g, HALF, 1) for g in ghosts]
        return jnp.concatenate(ghost_rates(near_lane, terms, ghosts, moved), axis=0)

    def inside_second(start, size):
        return pl.ds(start + LANES if isinstance(start, int) else pl.multiple_of(start + LANES, LANES), size)

    step_one, step_two = time_step / 12.0, 0.5 * time_step / 12.0

    def finish_first(c, start, value, rate):
        second[c, :, inside_second(start, chunk)] = value + step_one * rate

    def finish_second(c, start, value, rate):
        base = first[c, :, inside_second(start, chunk)]
        out_ref[c, :, pl.ds(start, chunk)] = 0.5 * (base + value) + step_two * rate

    def read_second(c, which, start):
        return second[c, which, inside_second(start, chunk)]

    def write_second(c, which, start, value):
        second[c, which, inside_second(start, chunk)] = value

    def read_out(c, which, start):
        return out_ref[c, which, pl.ds(start, chunk)]

    def write_out(c, which, start, value):
        out_ref[c, which, pl.ds(start, chunk)] = value

    def tile_second(c, start):
        return second[c, :, start + LANES:start + 2 * LANES]

    def put_second(c, start, value):
        second[c, :, start + LANES:start + 2 * LANES] = value

    def tile_out(c, start):
        return out_ref[c, :, start:start + LANES]

    def put_out(c, start, value):
        out_ref[c, :, start:start + LANES] = value

    load_state.wait()
    face_out[0] = gather_face(first)
    pl.semaphore_wait(barrier, segs - 1 + has_before.astype(jnp.int32) + has_after.astype(jnp.int32))
    start_faces(0)
    start_chain(0)

    load_metric.wait()
    valid = jnp.where(jnp.logical_and(in_face, any_join), 1.0, 0.0)
    own_metric = valid * gather_metric()
    face_out[1, :3 * length] = own_metric
    start_faces(1)
    open_ends(first, 0)
    build_faces()
    build_delta()
    prepare_terms(step_one, own_metric, face_out[0])
    split_up(first[:, :, inner].reshape(rows, width), split)
    along_k()
    inside_rates(first, finish_first)

    await_chain(0)
    chain_rates(first, 0, step_one, read_second, write_second, end_rows)
    start_chain(1)
    face_out[2] = gather_face(second)
    start_faces(2)

    turned_ref[...] = flipped(face_out[0])
    await_faces(0)
    added = face_rates(own_terms(), flipped(received(0, rows)), face_out[0])
    for c in range(4):
        delta_out[c] = jnp.where(lax.broadcasted_iota(jnp.int32, (8, LANES), 0) < 4,
                                 added[c * length:c * length + 8], added[(c + 1) * length - 8:(c + 1) * length])
    start_chain(2)
    added_ref[...] = face_out[2] + added
    spread_face(added, tile_second, put_second)
    open_ends(second, 1)
    split_up(second[:, :, inner].reshape(rows, width), split)
    along_k()
    inside_rates(second, finish_second)
    prepare_terms(step_two, face_out[1, :3 * length], added_ref[...])
    await_faces(1)
    their_face = received(0, rows)
    their_terms = terms_of(step_one, partner_sign, received(1, 3 * length), their_face)
    theirs_ref[...] = face_rates(their_terms, turned_ref[...], their_face)

    await_chain(1)
    await_chain(2)
    spread_delta()
    chain_rates(second, 1, step_two, read_out, write_out)
    await_faces(2)
    their_face = flipped(received(2, rows) + theirs_ref[...])
    spread_face(face_rates(own_terms(), their_face, added_ref[...]), tile_out, put_out)

    for kind in range(3):
        for copy in face_copies(kind):
            copy.wait_send()
        sent_chain(kind)


def on_device(state, metric, block_map, links):
    segs, chain = lax.axis_size("seg"), lax.axis_size("blk")
    _, parts, length, width = state.shape
    cross = math.isqrt(width)
    assert cross <= HALF and length == 16
    chunk = math.lcm(cross, LANES)
    links = links.transpose(1, 2, 0)
    f32, bf16, dma = jnp.float32, jnp.bfloat16, pltpu.SemaphoreType.DMA
    result = pl.pallas_call(
        functools.partial(kernel, segs, chain, cross),
        out_shape=pltpu.VMEM((parts, length, width), f32),
        in_specs=[pl.BlockSpec(memory_space=pl.ANY)] * 4,
        out_specs=pl.BlockSpec(memory_space=pltpu.VMEM),
        scratch_shapes=[
            pltpu.VMEM((parts, length, width + 2 * LANES), f32),
            pltpu.VMEM((parts, length, width + 2 * LANES), f32),
            pltpu.VMEM((9, length, width), f32),
            pltpu.VMEM((width // LANES, 8, LANES), jnp.int32),
            pltpu.VMEM((width // LANES, 8, LANES), f32),
            pltpu.VMEM((width // LANES, 8, LANES), jnp.int32),
            pltpu.VMEM((width // LANES, 8, LANES), f32),
            pltpu.VMEM((2 * parts * length, width), bf16),
            pltpu.VMEM((2 * chunk, chunk), bf16),
            pltpu.VMEM((2 * chunk, chunk), bf16),
            pltpu.VMEM((2 * chunk, chunk), bf16),
            pltpu.VMEM((parts, length, width), f32),
            pltpu.VMEM((parts - 1, length, width), f32),
            pltpu.VMEM((5, length, LANES), f32),
            pltpu.VMEM((parts * length, LANES), f32),
            pltpu.VMEM((parts * length, LANES), f32),
            pltpu.VMEM((parts * length, LANES), f32),
            pltpu.VMEM((2, parts, 8, width), f32),
            pltpu.VMEM((parts, 8, width), f32),
            pltpu.VMEM((parts, 8, LANES), f32),
            pltpu.VMEM((parts, 8, LANES), f32),
            pltpu.VMEM((3, parts * length, LANES), f32),
            pltpu.VMEM((3, segs - 1, parts * length, LANES), f32),
            pltpu.SMEM(block_map.shape, jnp.int32),
            pltpu.SMEM(links.shape, jnp.int32),
            dma((4,)), dma((3, 2)), dma((3, 2)), dma((3, segs - 1)), dma((3, segs - 1)),
        ],
        compiler_params=pltpu.CompilerParams(collective_id=0, has_side_effects=True),
    )(state, metric, block_map, links)
    return result.reshape(state.shape)


def solution(mesh):
    in_specs = (P(("seg", "blk"), None, None, None), P(("seg", "blk"), None, None, None), P(), P())
    out_specs = P(("seg", "blk"), None, None, None)
    return jax.shard_map(
        on_device, mesh=mesh, in_specs=in_specs, out_specs=out_specs, check_vma=False
    )
```

```python
import functools
import math

import jax
import jax.numpy as jnp
from jax import lax
from jax.experimental import pallas as pl
from jax.experimental.pallas import tpu as pltpu
from jax.sharding import PartitionSpec as P

time_step = 0.05
viscosity = 0.2
compress = 1.0
MESH = pl.DeviceIdType.MESH
LANES = 128
HALF = LANES // 2
WALL = (-1.0, -1.0, -1.0, 1.0)


def split_index(index, size, count):
    quotient = jnp.zeros_like(index)
    for step in range(1, count):
        quotient += (index >= size * step).astype(jnp.int32)
    return quotient, index - size * quotient


def take(value, index, axis):
    numbers = lax.GatherDimensionNumbers(
        offset_dims=(), collapsed_slice_dims=(axis,), start_index_map=(axis,),
        operand_batching_dims=(1 - axis,), start_indices_batching_dims=(1 - axis,))
    return lax.gather(value, index[..., None], numbers, slice_sizes=(1, 1),
                      mode=lax.GatherScatterMode.PROMISE_IN_BOUNDS)


def flipped_bits(index, bits):
    bit = 1
    while bit <= bits:
        if bits & bit:
            index = index + bit - 2 * bit * lax.rem(lax.div(index, bit), 2)
        bit *= 2
    return index


def halves(value):
    lead = value.astype(jnp.bfloat16)
    return lead, (value - lead.astype(jnp.float32)).astype(jnp.bfloat16)


def select(flag, yes, no):
    return jnp.where(flag, yes, no)


def ghost_terms(scale, sign, near, metric, values):
    carried = sign * (metric[0] * values[0] + metric[1] * values[1] + metric[2] * values[2])
    norm = viscosity * (metric[0] * metric[0] + metric[1] * metric[1] + metric[2] * metric[2])
    edge = (8.0 * scale) * (2.0 * norm + carried) * near
    outer = scale * (norm + carried)
    return edge, outer, [(scale * sign) * m for m in metric]


def ghost_rates(near, terms, ghosts, moved):
    edge, outer, pull = terms
    eight = 8.0 * near
    slopes = [m - eight * g for g, m in zip(ghosts, moved)]
    parts = [edge * ghosts[c] - outer * moved[c] - pull[c] * slopes[3] for c in range(3)]
    parts.append(-compress * (pull[0] * slopes[0] + pull[1] * slopes[1] + pull[2] * slopes[2]))
    return parts


def kernel(segs, chain, cross, state_hbm, metric_hbm, block_map_hbm, links_hbm, out_ref,
           first, second, geometry, face_index, face_mask, delta_index, delta_mask, split,
           k_slope_uvw, k_slope_p, k_bend, i_matrix, slope_k, bend_k, slope_i, bend_i, norms,
           terms_ref, added_ref, theirs_ref, turned_ref,
           ghost_rows, end_rows, delta_out, delta_in, face_out, face_in, block_map, links,
           load_sem, chain_send, chain_recv, face_send, face_recv):
    length, width = out_ref.shape[1], out_ref.shape[2]
    rows = 4 * length
    chunk = math.lcm(cross, LANES)
    chunks = width // chunk
    inner = pl.ds(LANES, width)
    seg, pos = lax.axis_index("seg"), lax.axis_index("blk")
    me = seg * chain + pos
    has_before, has_after = pos > 0, pos < chain - 1
    before, after = lax.rem(pos + chain - 1, chain), lax.rem(pos + 1, chain)
    paired = segs & (segs - 1) == 0
    order = range(segs - 1, 0, -1)

    def to_seg(offset):
        return flipped_bits(seg, offset) if paired else lax.rem(seg + offset, segs)

    def from_seg(offset):
        return flipped_bits(seg, offset) if paired else lax.rem(seg + segs - offset, segs)

    barrier = pltpu.get_barrier_semaphore()
    for offset in order:
        pl.semaphore_signal(barrier, inc=1, device_id={"seg": to_seg(offset)}, device_id_type=MESH)

    @pl.when(has_before)
    def _():
        pl.semaphore_signal(barrier, inc=1, device_id={"blk": before}, device_id_type=MESH)

    @pl.when(has_after)
    def _():
        pl.semaphore_signal(barrier, inc=1, device_id={"blk": after}, device_id_type=MESH)

    load_map = pltpu.make_async_copy(block_map_hbm, block_map, load_sem.at[2])
    load_links = pltpu.make_async_copy(links_hbm, links, load_sem.at[3])
    load_state = pltpu.make_async_copy(state_hbm.at[0], first.at[:, :, inner], load_sem.at[0])
    load_metric = pltpu.make_async_copy(metric_hbm.at[0], geometry, load_sem.at[1])
    load_map.start()
    load_links.start()
    load_state.start()
    load_metric.start()

    lane_row = lax.broadcasted_iota(jnp.int32, (1, LANES), 1)
    face_layer = (lane_row >= HALF).astype(jnp.int32)
    face_place = lane_row - HALF * face_layer
    in_face = face_place < cross
    near_lane = (lane_row < HALF).astype(jnp.float32)

    def build_k():
        here = lax.broadcasted_iota(jnp.int32, (cross, LANES), 0)
        column = lax.broadcasted_iota(jnp.int32, (cross, LANES), 1)
        for group in range(chunk // cross):
            first_row = group * cross
            for tile in range(chunk // LANES):
                lanes = slice(tile * LANES, (tile + 1) * LANES)
                if not first_row // LANES <= tile <= (first_row + cross - 1) // LANES:
                    for matrix in (k_slope_uvw, k_slope_p, k_bend):
                        for top in (first_row, chunk + first_row):
                            matrix[top:top + cross, lanes] = jnp.zeros((cross, LANES), jnp.bfloat16)
                    continue
                there = column + (tile * LANES - first_row)
                there = jnp.where(jnp.logical_and(there >= 0, there < cross), there, 4 * width)
                offset, mirrored = here - there, here + there

                def at(index, value, factor):
                    return jnp.where(index == value, factor, 0.0)

                slope = at(offset, -2, 1.0) + at(offset, -1, -8.0) + at(offset, 1, 8.0) + at(offset, 2, -1.0)
                bend = at(offset, -2, -1.0) + at(offset, -1, 16.0) + at(offset, 1, 16.0) + at(offset, 2, -1.0)
                end = 2 * cross - 2
                wall_slope = (at(mirrored, 0, -8.0) + at(mirrored, 1, 1.0)
                              + at(mirrored, end, 8.0) + at(mirrored, end - 1, -1.0))
                wall_bend = (at(mirrored, 0, 16.0) + at(mirrored, 1, -1.0)
                             + at(mirrored, end, 16.0) + at(mirrored, end - 1, -1.0))
                for matrix, value in ((k_slope_uvw, slope + WALL[0] * wall_slope),
                                      (k_slope_p, slope + WALL[3] * wall_slope),
                                      (k_bend, bend + WALL[0] * wall_bend)):
                    value = value.astype(jnp.bfloat16)
                    matrix[first_row:first_row + cross, lanes] = value
                    matrix[chunk + first_row:chunk + first_row + cross, lanes] = value

    pads = jnp.zeros((4, length, LANES), jnp.float32)
    for padded in (first, second):
        padded[:, :, :LANES] = pads
        padded[:, :, LANES + width:] = pads
    build_k()

    def build_i():
        count = 7 * length
        term, here = split_index(lax.broadcasted_iota(jnp.int32, (count, LANES), 0), length, 7)
        part, there = split_index(lax.broadcasted_iota(jnp.int32, (count, LANES), 1), length, 8)
        part = jnp.where(part >= 4, part - 4, part)
        offset = there - here

        def at(index, factor):
            return jnp.where(offset == index, factor, 0.0)

        slope = at(-2, 1.0) + at(-1, -8.0) + at(1, 8.0) + at(2, -1.0)
        bend = at(-2, -1.0) + at(-1, 16.0) + at(1, 16.0) + at(2, -1.0)
        value = jnp.where(term == part, slope, jnp.where(term == part + 4, bend, 0.0))
        i_matrix[...] = value.astype(jnp.bfloat16)

    build_i()

    load_map.wait()
    load_links.wait()
    block = block_map[me]

    def joined_side(number):
        return [links[2 + side, 0, number] >= 0 for side in range(4)]

    joins = joined_side(block)
    partner, partner_face = jnp.int32(-1), jnp.int32(0)
    flip_along, flip_across = jnp.int32(0), jnp.int32(0)
    for side in range(4):
        partner = select(joins[side], links[2 + side, 0, block], partner)
        partner_face = select(joins[side], links[2 + side, 1, block], partner_face)
        flip_along = select(joins[side], links[2 + side, 2, block], flip_along)
        flip_across = select(joins[side], links[2 + side, 3, block], flip_across)
    any_join = partner >= 0
    on_first = jnp.logical_or(joins[0], joins[1])
    on_second = jnp.logical_or(joins[2], joins[3])
    on_high = jnp.logical_or(joins[1], joins[3])
    joins_before = joined_side(block_map[seg * chain + before])
    joins_after = joined_side(block_map[seg * chain + after])
    comes_from = {offset: block_map[from_seg(offset) * chain + pos] == partner for offset in order}
    face_sign = select(on_high, -1.0, 1.0)
    partner_sign = select(jnp.logical_or(partner_face == 3, partner_face == 5), -1.0, 1.0)

    lane_of = lax.broadcasted_iota(jnp.int32, (8, LANES), 1)
    row_in = lax.broadcasted_iota(jnp.int32, (8, LANES), 0)
    layer_of = (lane_of >= HALF).astype(jnp.int32)
    place_of = lane_of - HALF * layer_of
    face_lane = place_of < cross

    def spread_index(tile, high):
        start = tile * LANES
        row = start // cross
        spot = lane_of + (start - row * cross)
        place = jnp.full((8, LANES), row, jnp.int32)
        for step in range(1, LANES // cross + 2):
            past = spot >= step * cross
            place = place + past.astype(jnp.int32)
        spot = lane_of + start - place * cross
        layer = jnp.where(high, cross - 1 - spot, spot)
        return jnp.where(layer < 2, place + HALF * layer, -1)

    def build_spread(index_ref, mask_ref, high, used):
        for tile in range(width // LANES):
            index = jnp.where(used, spread_index(tile, high), -1)
            mask_ref[tile] = jnp.where(index >= 0, 1.0, 0.0)
            index_ref[tile] = jnp.maximum(index, 0)

    def build_faces():
        build_spread(face_index, face_mask, jnp.full((8, LANES), select(on_high, 1, 0)) > 0,
                     jnp.full((8, LANES), select(on_second, 1, 0)) > 0)

    def build_delta():
        def chosen(sides):
            flags = [select(jnp.logical_or(near_joins[sides[0]], near_joins[sides[1]]), 1, 0)
                     for near_joins in (joins_before, joins_after)]
            return jnp.where(row_in < 4, flags[0], flags[1]) > 0

        build_spread(delta_index, delta_mask, chosen((1, 3)), chosen((2, 3)))

    source_of = jnp.where(face_lane, place_of, 0) * cross + select(on_high, cross - 1 - layer_of, layer_of)
    source_tile, source_lane = split_index(source_of, LANES, width // LANES)
    flip_rows = select(flip_along == 1, 7 - row_in, row_in)
    flip_lanes = jnp.where(face_lane, layer_of * HALF + select(flip_across == 1, cross - 1 - place_of, place_of), lane_of)

    def by_rows(value, function):
        return jnp.concatenate([function(value[at:at + 8]) for at in range(0, value.shape[0], 8)], axis=0)

    def flipped(value):
        parts = []
        for at in range(0, value.shape[0], length):
            low, high = value[at:at + 8], value[at + 8:at + 16]
            for half in (select(flip_along == 1, high, low), select(flip_along == 1, low, high)):
                parts.append(take(take(half, flip_rows, 0), flip_lanes, 1))
        return jnp.concatenate(parts, axis=0)

    def split_up(value, into):
        count = value.shape[0]
        lead, trail = halves(value)
        into[:count] = lead
        into[count:2 * count] = trail

    def gathered(low, high, tile_of):
        packed = None
        for tile in range(width // LANES):
            part = by_rows(tile_of(tile), lambda x: take(x, source_lane, 1))
            here = jnp.concatenate([source_tile == tile] * (part.shape[0] // 8), axis=0)
            packed = part if packed is None else jnp.where(here, part, packed)
        near, far = LANES - cross, LANES - 2 * cross
        lower = jnp.where(lane_row < HALF, low, pltpu.roll(low, HALF - cross, 1))
        upper = jnp.where(lane_row < HALF, pltpu.roll(high, LANES - near, 1), pltpu.roll(high, HALF - far, 1))
        return jnp.where(on_first, jnp.where(on_high, upper, lower), packed)

    def gather_face(padded):
        def tile_of(tile):
            start = LANES + tile * LANES
            return padded[:, :, start:start + LANES].reshape(rows, LANES)

        return gathered(tile_of(0), tile_of(width // LANES - 1), tile_of)

    def gather_metric():
        def tile_of(tile, base=6):
            return geometry[base:base + 3, :, tile * LANES:(tile + 1) * LANES].reshape(3 * length, LANES)

        return gathered(tile_of(0, 3), tile_of(width // LANES - 1, 3), tile_of)

    near, far = LANES - cross, LANES - 2 * cross

    def to_lower(value):
        return jnp.where(lane_row < cross, value, pltpu.roll(value, LANES - (HALF - cross), 1))

    def to_upper(value):
        return jnp.where(lane_row >= near, pltpu.roll(value, near, 1), pltpu.roll(value, LANES - (HALF - far), 1))

    def spread(value, index_ref, mask_ref, lower, upper, write):
        for tile in range(width // LANES):
            index, mask = index_ref[tile], mask_ref[tile]
            add = by_rows(value, lambda x: take(x, index, 1) * mask)
            if tile == 0:
                add = add + lower
            if tile == width // LANES - 1:
                add = add + upper
            write(tile * LANES, add)

    def spread_face(value, read, write):
        on_low = jnp.logical_not(on_high)
        lower = jnp.where(jnp.logical_and(lane_row < 2 * cross, jnp.logical_and(on_first, on_low)), to_lower(value), 0.0)
        upper = jnp.where(jnp.logical_and(lane_row >= far, jnp.logical_and(on_first, on_high)), to_upper(value), 0.0)

        def put(start, add):
            for c in range(4):
                write(c, start, read(c, start) + add[c * length:(c + 1) * length])

        spread(value, face_index, face_mask, lower, upper, put)

    def spread_delta():
        end_row = lax.broadcasted_iota(jnp.int32, (8, LANES), 0)
        wanted = jnp.logical_or(jnp.logical_and(end_row < 2, has_before), jnp.logical_and(end_row >= 6, has_after))
        value = jnp.concatenate([jnp.where(wanted, delta_in[c], 0.0) for c in range(4)], axis=0)

        def mask(side):
            flag = [select(flags[side], 1.0, 0.0) for flags in (joins_before, joins_after)]
            one = jnp.where(end_row < 4, flag[0], flag[1])
            return jnp.concatenate([one] * 4, axis=0)

        lower = jnp.where(lane_row < 2 * cross, to_lower(value) * mask(0), 0.0)
        upper = jnp.where(lane_row >= far, to_upper(value) * mask(1), 0.0)
        def put(start, add):
            for c in range(4):
                at = slice(start, start + LANES)
                ghost_rows[1, c, :, at] = ghost_rows[1, c, :, at] + add[c * 8:(c + 1) * 8]

        spread(value, delta_index, delta_mask, lower, upper, put)

    def along_i():
        piece = 2 * LANES
        for part in range(width // piece):
            at = slice(part * piece, (part + 1) * piece)
            out = jnp.dot(i_matrix[...], split[:, at], preferred_element_type=jnp.float32)
            slope_i[:, :, at] = out[:rows].reshape(4, length, piece)
            bend_i[:, :, at] = out[rows:].reshape(3, length, piece)

    def along_k():
        count = 3 * length
        parts = []
        for step in range(chunks):
            at = slice(step * chunk, (step + 1) * chunk)
            parts.append(jnp.concatenate([split[:rows, at], split[rows:, at]], axis=1))
        velocity = jnp.concatenate([part[:count] for part in parts], axis=0)
        pressure = jnp.concatenate([part[count:] for part in parts], axis=0)
        slope = jnp.dot(velocity, k_slope_uvw[...], preferred_element_type=jnp.float32)
        bend = jnp.dot(velocity, k_bend[...], preferred_element_type=jnp.float32)
        slope_p = jnp.dot(pressure, k_slope_p[...], preferred_element_type=jnp.float32)
        for step in range(chunks):
            at = slice(step * chunk, (step + 1) * chunk)
            slope_k[:3, :, at] = slope[step * count:(step + 1) * count].reshape(3, length, chunk)
            bend_k[:, :, at] = bend[step * count:(step + 1) * count].reshape(3, length, chunk)
            slope_k[3, :, at] = slope_p[step * length:(step + 1) * length]

    def chain_copies(kind):
        if kind == 0:
            low, high = first.at[:, 0:2, inner], first.at[:, length - 2:length, inner]
        else:
            source = end_rows if kind == 1 else delta_out
            low, high = source.at[:, 0:2], source.at[:, 6:8]
        target = delta_in if kind == 2 else ghost_rows.at[kind]
        to_before = pltpu.make_async_remote_copy(
            low, target.at[:, 6:8], chain_send.at[kind, 0], chain_recv.at[kind, 0],
            device_id={"blk": before}, device_id_type=MESH)
        to_after = pltpu.make_async_remote_copy(
            high, target.at[:, 0:2], chain_send.at[kind, 1], chain_recv.at[kind, 1],
            device_id={"blk": after}, device_id_type=MESH)
        return to_before, to_after

    def face_copies(kind):
        used = pl.ds(0, 3 * length if kind == 1 else rows)
        return [pltpu.make_async_remote_copy(
            face_out.at[kind, used], face_in.at[kind, offset - 1, used], face_send.at[kind, offset - 1],
            face_recv.at[kind, offset - 1], device_id={"seg": to_seg(offset)}, device_id_type=MESH)
            for offset in order]

    def start_faces(kind):
        for copy in face_copies(kind):
            copy.start()

    def await_faces(kind):
        for copy in face_copies(kind):
            copy.wait_recv()

    def start_chain(kind):
        to_before, to_after = chain_copies(kind)

        @pl.when(has_before)
        def _():
            to_before.start()

        @pl.when(has_after)
        def _():
            to_after.start()

    def open_ends(padded, turn):
        @pl.when(jnp.logical_not(has_before))
        def _():
            for c in range(4):
                ghost_rows[turn, c, 0:1, :] = -WALL[c] * padded[c, 1:2, inner]
                ghost_rows[turn, c, 1:2, :] = -WALL[c] * padded[c, 0:1, inner]

        @pl.when(jnp.logical_not(has_after))
        def _():
            for c in range(4):
                ghost_rows[turn, c, 6:7, :] = -WALL[c] * padded[c, length - 1:length, inner]
                ghost_rows[turn, c, 7:8, :] = -WALL[c] * padded[c, length - 2:length - 1, inner]

    def await_chain(kind):
        to_before, to_after = chain_copies(kind)

        @pl.when(has_before)
        def _():
            to_after.wait_recv()

        @pl.when(has_after)
        def _():
            to_before.wait_recv()

    def sent_chain(kind):
        to_before, to_after = chain_copies(kind)

        @pl.when(has_before)
        def _():
            to_before.wait_send()

        @pl.when(has_after)
        def _():
            to_after.wait_send()

    lane = lax.broadcasted_iota(jnp.int32, (length, chunk), 1)

    def central(minus2, minus1, plus1, plus2, bent):
        slope = (minus2 - plus2) + 8.0 * (plus1 - minus1)
        return slope, 16.0 * (minus1 + plus1) - (minus2 + plus2) if bent else None

    def along_j(wide, value, wall, is_first, is_last, bent):
        def moved(step):
            if step > 0:
                return pltpu.roll(wide[:, :LANES + chunk], step, 1)[:, LANES:]
            return pltpu.roll(wide[:, LANES:], LANES + chunk + step, 1)[:, :chunk]
        minus2, minus1, plus1, plus2 = moved(2 * cross), moved(cross), moved(-cross), moved(-2 * cross)
        m1, m2, p1, p2 = minus1, minus2, plus1, plus2
        if is_first:
            m1 = jnp.where(lane < cross, wall * value, minus1)
            m2 = jnp.where(lane < cross, wall * plus1, jnp.where(lane < 2 * cross, wall * minus1, minus2))
        if is_last:
            p1 = jnp.where(lane >= chunk - cross, wall * value, plus1)
            p2 = jnp.where(lane >= chunk - cross, wall * minus1,
                           jnp.where(lane >= chunk - 2 * cross, wall * plus1, plus2))
        return central(m2, m1, p1, p2, bent)

    def inside_rates(padded, fresh, finish):
        def at_chunk(start, is_first, is_last):
            at = pl.ds(start, chunk)
            wide = [padded[c, :, pl.ds(start, chunk + 2 * LANES)] for c in range(4)]
            values = [w[:, LANES:LANES + chunk] for w in wide]
            sums, total = None, None
            for direction in range(3):
                metric = [geometry[3 * direction + b, :, at] for b in range(3)]
                if direction == 1:
                    slopes, bends = [], []
                    for c in range(4):
                        slope, bend = along_j(wide[c], values[c], WALL[c], is_first, is_last, c < 3)
                        slopes.append(slope)
                        bends.append(bend)
                else:
                    slope_ref, bend_ref = (slope_i, bend_i) if direction == 0 else (slope_k, bend_k)
                    slopes = [slope_ref[c, :, at] for c in range(4)]
                    bends = [bend_ref[c, :, at] for c in range(3)]
                if fresh:
                    norm = viscosity * (metric[0] * metric[0] + metric[1] * metric[1] + metric[2] * metric[2])
                    norms[direction, :, at] = norm
                    total = norm if total is None else total + norm
                else:
                    norm = norms[direction, :, at]
                carried = metric[0] * values[0] + metric[1] * values[1] + metric[2] * values[2]
                parts = [norm * bends[c] - carried * slopes[c] - metric[c] * slopes[3] for c in range(3)]
                parts.append(metric[0] * slopes[0] + metric[1] * slopes[1] + metric[2] * slopes[2])
                sums = parts if sums is None else [a + b for a, b in zip(sums, parts)]
            if fresh:
                total = 30.0 * total
                norms[3, :, at] = total
            else:
                total = norms[3, :, at]
            for c in range(4):
                finish(c, start, values[c], sums[c] - total * values[c] if c < 3 else sums[c])

        at_chunk(0, True, chunks == 1)
        if chunks > 2:
            for step in range(1, chunks - 1):
                at_chunk(step * chunk, False, False)
        if chunks > 1:
            at_chunk((chunks - 1) * chunk, False, True)

    sub = lax.broadcasted_iota(jnp.int32, (8, chunk), 0)
    near_row = jnp.where(jnp.logical_or(sub == 0, sub == 7), 1.0, 0.0)
    row_sign = jnp.where(sub < 4, 1.0, -1.0)

    def chain_rates(padded, turn, scale, read, write, keep=None):
        def body(step, carry):
            start = pl.multiple_of(step * chunk, LANES)
            at = pl.ds(start, chunk)

            def ends(low, high):
                return jnp.where(sub < 4, low, high)

            inside = pl.ds(pl.multiple_of(start + LANES, LANES), chunk)
            values = [ends(padded[c, :8, inside], padded[c, length - 8:, inside]) for c in range(3)]
            metric = [ends(geometry[b, :8, at], geometry[b, length - 8:, at]) for b in range(3)]
            moved = [ghost_rows[turn, c, :, at] for c in range(4)]
            ghosts = [ends(pltpu.roll(m, 7, 0), pltpu.roll(m, 1, 0)) for m in moved]
            sums = ghost_rates(near_row, ghost_terms(scale, row_sign, near_row, metric, values), ghosts, moved)
            low, high = pl.ds(0, 8), pl.ds(length - 8, 8)
            for c in range(4):
                low_new = read(c, low, start) + jnp.where(sub < 2, sums[c], 0.0)
                high_new = read(c, high, start) + jnp.where(sub >= 6, sums[c], 0.0)
                write(c, low, start, low_new)
                write(c, high, start, high_new)
                if keep is not None:
                    keep[c, :, at] = ends(low_new, high_new)
            return carry

        lax.fori_loop(0, chunks, body, 0)

    def at_part(value, c):
        return value[c * length:(c + 1) * length]

    def terms_of(scale, sign, metric, own):
        return ghost_terms(scale, sign, near_lane, [at_part(metric, b) for b in range(3)],
                           [at_part(own, b) for b in range(3)])

    def prepare_terms(scale, metric, own):
        edge, outer, pull = terms_of(scale, face_sign, metric, own)
        terms_ref[0] = edge
        terms_ref[1] = outer
        for b in range(3):
            terms_ref[2 + b] = pull[b]

    def own_terms():
        return terms_ref[0], terms_ref[1], [terms_ref[2 + b] for b in range(3)]

    def received(kind, count):
        value = face_in[kind, order[-1] - 1, :count]
        for offset in order[:-1]:
            value = jnp.where(comes_from[offset], face_in[kind, offset - 1, :count], value)
        return value

    def face_rates(terms, theirs, own):
        ghosts = [at_part(theirs, c) - WALL[c] * at_part(own, c) for c in range(4)]
        moved = [pltpu.roll(g, HALF, 1) for g in ghosts]
        return jnp.concatenate(ghost_rates(near_lane, terms, ghosts, moved), axis=0)

    def inside_second(start, size):
        return pl.ds(start + LANES if isinstance(start, int) else pl.multiple_of(start + LANES, LANES), size)

    step_one, step_two = time_step / 12.0, 0.5 * time_step / 12.0

    factor = (1.0, 1.0, 1.0, -compress)

    def finish_first(c, start, value, rate):
        second[c, :, inside_second(start, chunk)] = value + (step_one * factor[c]) * rate

    def finish_second(c, start, value, rate):
        base = first[c, :, inside_second(start, chunk)]
        out_ref[c, :, pl.ds(start, chunk)] = 0.5 * (base + value) + (step_two * factor[c]) * rate

    def read_second(c, which, start):
        return second[c, which, inside_second(start, chunk)]

    def write_second(c, which, start, value):
        second[c, which, inside_second(start, chunk)] = value

    def read_out(c, which, start):
        return out_ref[c, which, pl.ds(start, chunk)]

    def write_out(c, which, start, value):
        out_ref[c, which, pl.ds(start, chunk)] = value

    def tile_second(c, start):
        return second[c, :, start + LANES:start + 2 * LANES]

    def put_second(c, start, value):
        second[c, :, start + LANES:start + 2 * LANES] = value

    def tile_out(c, start):
        return out_ref[c, :, start:start + LANES]

    def put_out(c, start, value):
        out_ref[c, :, start:start + LANES] = value

    load_state.wait()
    face_out[0] = gather_face(first)
    pl.semaphore_wait(barrier, segs - 1 + has_before.astype(jnp.int32) + has_after.astype(jnp.int32))
    start_faces(0)
    start_chain(0)

    load_metric.wait()
    valid = jnp.where(jnp.logical_and(in_face, any_join), 1.0, 0.0)
    own_metric = valid * gather_metric()
    face_out[1, :3 * length] = own_metric
    start_faces(1)
    open_ends(first, 0)
    build_faces()
    build_delta()
    prepare_terms(step_one, own_metric, face_out[0])
    split_up(first[:, :, inner].reshape(rows, width), split)
    along_i()
    along_k()
    inside_rates(first, True, finish_first)

    await_chain(0)
    chain_rates(first, 0, step_one, read_second, write_second, end_rows)
    start_chain(1)
    face_out[2] = gather_face(second)
    start_faces(2)

    turned_ref[...] = flipped(face_out[0])
    await_faces(0)
    added = face_rates(own_terms(), flipped(received(0, rows)), face_out[0])
    for c in range(4):
        delta_out[c] = jnp.where(lax.broadcasted_iota(jnp.int32, (8, LANES), 0) < 4,
                                 added[c * length:c * length + 8], added[(c + 1) * length - 8:(c + 1) * length])
    start_chain(2)
    added_ref[...] = face_out[2] + added
    spread_face(added, tile_second, put_second)
    open_ends(second, 1)
    split_up(second[:, :, inner].reshape(rows, width), split)
    along_i()
    along_k()
    inside_rates(second, False, finish_second)
    prepare_terms(step_two, face_out[1, :3 * length], added_ref[...])
    await_faces(1)
    their_face = received(0, rows)
    their_terms = terms_of(step_one, partner_sign, received(1, 3 * length), their_face)
    theirs_ref[...] = face_rates(their_terms, turned_ref[...], their_face)

    await_chain(1)
    await_chain(2)
    spread_delta()
    chain_rates(second, 1, step_two, read_out, write_out)
    await_faces(2)
    their_face = flipped(received(2, rows) + theirs_ref[...])
    spread_face(face_rates(own_terms(), their_face, added_ref[...]), tile_out, put_out)

    for kind in range(3):
        for copy in face_copies(kind):
            copy.wait_send()
        sent_chain(kind)


def on_device(state, metric, block_map, links):
    segs, chain = lax.axis_size("seg"), lax.axis_size("blk")
    _, parts, length, width = state.shape
    cross = math.isqrt(width)
    assert cross <= HALF and length == 16
    chunk = math.lcm(cross, LANES)
    links = links.transpose(1, 2, 0)
    f32, bf16, dma = jnp.float32, jnp.bfloat16, pltpu.SemaphoreType.DMA
    result = pl.pallas_call(
        functools.partial(kernel, segs, chain, cross),
        out_shape=pltpu.VMEM((parts, length, width), f32),
        in_specs=[pl.BlockSpec(memory_space=pl.ANY)] * 4,
        out_specs=pl.BlockSpec(memory_space=pltpu.VMEM),
        scratch_shapes=[
            pltpu.VMEM((parts, length, width + 2 * LANES), f32),
            pltpu.VMEM((parts, length, width + 2 * LANES), f32),
            pltpu.VMEM((9, length, width), f32),
            pltpu.VMEM((width // LANES, 8, LANES), jnp.int32),
            pltpu.VMEM((width // LANES, 8, LANES), f32),
            pltpu.VMEM((width // LANES, 8, LANES), jnp.int32),
            pltpu.VMEM((width // LANES, 8, LANES), f32),
            pltpu.VMEM((2 * parts * length, width), bf16),
            pltpu.VMEM((2 * chunk, chunk), bf16),
            pltpu.VMEM((2 * chunk, chunk), bf16),
            pltpu.VMEM((2 * chunk, chunk), bf16),
            pltpu.VMEM((7 * length, LANES), bf16),
            pltpu.VMEM((parts, length, width), f32),
            pltpu.VMEM((parts - 1, length, width), f32),
            pltpu.VMEM((parts, length, width), f32),
            pltpu.VMEM((parts - 1, length, width), f32),
            pltpu.VMEM((parts, length, width), f32),
            pltpu.VMEM((5, length, LANES), f32),
            pltpu.VMEM((parts * length, LANES), f32),
            pltpu.VMEM((parts * length, LANES), f32),
            pltpu.VMEM((parts * length, LANES), f32),
            pltpu.VMEM((2, parts, 8, width), f32),
            pltpu.VMEM((parts, 8, width), f32),
            pltpu.VMEM((parts, 8, LANES), f32),
            pltpu.VMEM((parts, 8, LANES), f32),
            pltpu.VMEM((3, parts * length, LANES), f32),
            pltpu.VMEM((3, segs - 1, parts * length, LANES), f32),
            pltpu.SMEM(block_map.shape, jnp.int32),
            pltpu.SMEM(links.shape, jnp.int32),
            dma((4,)), dma((3, 2)), dma((3, 2)), dma((3, segs - 1)), dma((3, segs - 1)),
        ],
        compiler_params=pltpu.CompilerParams(collective_id=0, has_side_effects=True),
    )(state, metric, block_map, links)
    return result.reshape(state.shape)


def solution(mesh):
    in_specs = (P(("seg", "blk"), None, None, None), P(("seg", "blk"), None, None, None), P(), P())
    out_specs = P(("seg", "blk"), None, None, None)
    return jax.shard_map(
        on_device, mesh=mesh, in_specs=in_specs, out_specs=out_specs, check_vma=False
    )
```

```python
import functools
import math

import jax
import jax.numpy as jnp
from jax import lax
from jax.experimental import pallas as pl
from jax.experimental.pallas import tpu as pltpu
from jax.sharding import PartitionSpec as P

time_step = 0.05
viscosity = 0.2
compress = 1.0
MESH = pl.DeviceIdType.MESH
LANES = 128
HALF = LANES // 2
WALL = (-1.0, -1.0, -1.0, 1.0)


def split_index(index, size, count):
    quotient = jnp.zeros_like(index)
    for step in range(1, count):
        quotient += (index >= size * step).astype(jnp.int32)
    return quotient, index - size * quotient


def take(value, index, axis):
    numbers = lax.GatherDimensionNumbers(
        offset_dims=(), collapsed_slice_dims=(axis,), start_index_map=(axis,),
        operand_batching_dims=(1 - axis,), start_indices_batching_dims=(1 - axis,))
    return lax.gather(value, index[..., None], numbers, slice_sizes=(1, 1),
                      mode=lax.GatherScatterMode.PROMISE_IN_BOUNDS)


def flipped_bits(index, bits):
    bit = 1
    while bit <= bits:
        if bits & bit:
            index = index + bit - 2 * bit * lax.rem(lax.div(index, bit), 2)
        bit *= 2
    return index


def halves(value):
    lead = value.astype(jnp.bfloat16)
    return lead, (value - lead.astype(jnp.float32)).astype(jnp.bfloat16)


def select(flag, yes, no):
    return jnp.where(flag, yes, no)


def ghost_terms(scale, sign, near, metric, values):
    carried = sign * (metric[0] * values[0] + metric[1] * values[1] + metric[2] * values[2])
    norm = viscosity * (metric[0] * metric[0] + metric[1] * metric[1] + metric[2] * metric[2])
    edge = (8.0 * scale) * (2.0 * norm + carried) * near
    outer = scale * (norm + carried)
    return edge, outer, [(scale * sign) * m for m in metric]


def ghost_rates(near, terms, ghosts, moved):
    edge, outer, pull = terms
    eight = 8.0 * near
    slopes = [m - eight * g for g, m in zip(ghosts, moved)]
    parts = [edge * ghosts[c] - outer * moved[c] - pull[c] * slopes[3] for c in range(3)]
    parts.append(-compress * (pull[0] * slopes[0] + pull[1] * slopes[1] + pull[2] * slopes[2]))
    return parts


def kernel(segs, chain, cross, state_hbm, metric_hbm, block_map_hbm, links_hbm, out_ref,
           first, second, geometry, face_index, face_mask, delta_index, delta_mask, split,
           k_slope_uvw, k_slope_p, k_bend, i_matrix, slope_k, bend_k, slope_i, bend_i, norms,
           terms_ref, added_ref, theirs_ref, turned_ref,
           ghost_rows, end_rows, delta_out, delta_in, face_out, face_in, block_map, links,
           load_sem, chain_send, chain_recv, face_send, face_recv):
    length, width = out_ref.shape[1], out_ref.shape[2]
    rows = 4 * length
    chunk = math.lcm(cross, LANES)
    chunks = width // chunk
    inner = pl.ds(LANES, width)
    seg, pos = lax.axis_index("seg"), lax.axis_index("blk")
    me = seg * chain + pos
    has_before, has_after = pos > 0, pos < chain - 1
    before, after = lax.rem(pos + chain - 1, chain), lax.rem(pos + 1, chain)
    paired = segs & (segs - 1) == 0
    order = range(segs - 1, 0, -1)

    def to_seg(offset):
        return flipped_bits(seg, offset) if paired else lax.rem(seg + offset, segs)

    def from_seg(offset):
        return flipped_bits(seg, offset) if paired else lax.rem(seg + segs - offset, segs)

    barrier = pltpu.get_barrier_semaphore()
    for offset in order:
        pl.semaphore_signal(barrier, inc=1, device_id={"seg": to_seg(offset)}, device_id_type=MESH)

    @pl.when(has_before)
    def _():
        pl.semaphore_signal(barrier, inc=1, device_id={"blk": before}, device_id_type=MESH)

    @pl.when(has_after)
    def _():
        pl.semaphore_signal(barrier, inc=1, device_id={"blk": after}, device_id_type=MESH)

    load_map = pltpu.make_async_copy(block_map_hbm, block_map, load_sem.at[2])
    load_links = pltpu.make_async_copy(links_hbm, links, load_sem.at[3])
    load_state = pltpu.make_async_copy(state_hbm.at[0], first.at[:, :, inner], load_sem.at[0])
    load_metric = pltpu.make_async_copy(metric_hbm.at[0], geometry, load_sem.at[1])
    load_map.start()
    load_links.start()
    load_state.start()
    load_metric.start()

    lane_row = lax.broadcasted_iota(jnp.int32, (1, LANES), 1)
    face_layer = (lane_row >= HALF).astype(jnp.int32)
    face_place = lane_row - HALF * face_layer
    in_face = face_place < cross
    near_lane = (lane_row < HALF).astype(jnp.float32)

    def build_k():
        here = lax.broadcasted_iota(jnp.int32, (cross, LANES), 0)
        column = lax.broadcasted_iota(jnp.int32, (cross, LANES), 1)
        for group in range(chunk // cross):
            first_row = group * cross
            for tile in range(chunk // LANES):
                lanes = slice(tile * LANES, (tile + 1) * LANES)
                if not first_row // LANES <= tile <= (first_row + cross - 1) // LANES:
                    for matrix in (k_slope_uvw, k_slope_p, k_bend):
                        for top in (first_row, chunk + first_row):
                            matrix[top:top + cross, lanes] = jnp.zeros((cross, LANES), jnp.bfloat16)
                    continue
                there = column + (tile * LANES - first_row)
                there = jnp.where(jnp.logical_and(there >= 0, there < cross), there, 4 * width)
                offset, mirrored = here - there, here + there

                def at(index, value, factor):
                    return jnp.where(index == value, factor, 0.0)

                slope = at(offset, -2, 1.0) + at(offset, -1, -8.0) + at(offset, 1, 8.0) + at(offset, 2, -1.0)
                bend = at(offset, -2, -1.0) + at(offset, -1, 16.0) + at(offset, 1, 16.0) + at(offset, 2, -1.0)
                end = 2 * cross - 2
                wall_slope = (at(mirrored, 0, -8.0) + at(mirrored, 1, 1.0)
                              + at(mirrored, end, 8.0) + at(mirrored, end - 1, -1.0))
                wall_bend = (at(mirrored, 0, 16.0) + at(mirrored, 1, -1.0)
                             + at(mirrored, end, 16.0) + at(mirrored, end - 1, -1.0))
                for matrix, value in ((k_slope_uvw, slope + WALL[0] * wall_slope),
                                      (k_slope_p, slope + WALL[3] * wall_slope),
                                      (k_bend, bend + WALL[0] * wall_bend)):
                    value = value.astype(jnp.bfloat16)
                    matrix[first_row:first_row + cross, lanes] = value
                    matrix[chunk + first_row:chunk + first_row + cross, lanes] = value

    pads = jnp.zeros((4, length, LANES), jnp.float32)
    for padded in (first, second):
        padded[:, :, :LANES] = pads
        padded[:, :, LANES + width:] = pads
    build_k()

    def build_i():
        count = 7 * length
        term, here = split_index(lax.broadcasted_iota(jnp.int32, (count, LANES), 0), length, 7)
        part, there = split_index(lax.broadcasted_iota(jnp.int32, (count, LANES), 1), length, 8)
        part = jnp.where(part >= 4, part - 4, part)
        offset = there - here

        def at(index, factor):
            return jnp.where(offset == index, factor, 0.0)

        slope = at(-2, 1.0) + at(-1, -8.0) + at(1, 8.0) + at(2, -1.0)
        bend = at(-2, -1.0) + at(-1, 16.0) + at(1, 16.0) + at(2, -1.0)
        value = jnp.where(term == part, slope, jnp.where(term == part + 4, bend, 0.0))
        i_matrix[...] = value.astype(jnp.bfloat16)

    build_i()

    load_map.wait()
    load_links.wait()
    block = block_map[me]

    def joined_side(number):
        return [links[2 + side, 0, number] >= 0 for side in range(4)]

    joins = joined_side(block)
    partner, partner_face = jnp.int32(-1), jnp.int32(0)
    flip_along, flip_across = jnp.int32(0), jnp.int32(0)
    for side in range(4):
        partner = select(joins[side], links[2 + side, 0, block], partner)
        partner_face = select(joins[side], links[2 + side, 1, block], partner_face)
        flip_along = select(joins[side], links[2 + side, 2, block], flip_along)
        flip_across = select(joins[side], links[2 + side, 3, block], flip_across)
    any_join = partner >= 0
    on_first = jnp.logical_or(joins[0], joins[1])
    on_second = jnp.logical_or(joins[2], joins[3])
    on_high = jnp.logical_or(joins[1], joins[3])
    joins_before = joined_side(block_map[seg * chain + before])
    joins_after = joined_side(block_map[seg * chain + after])
    comes_from = {offset: block_map[from_seg(offset) * chain + pos] == partner for offset in order}
    face_sign = select(on_high, -1.0, 1.0)
    partner_sign = select(jnp.logical_or(partner_face == 3, partner_face == 5), -1.0, 1.0)

    lane_of = lax.broadcasted_iota(jnp.int32, (8, LANES), 1)
    row_in = lax.broadcasted_iota(jnp.int32, (8, LANES), 0)
    layer_of = (lane_of >= HALF).astype(jnp.int32)
    place_of = lane_of - HALF * layer_of
    face_lane = place_of < cross

    def spread_index(tile, high):
        start = tile * LANES
        row = start // cross
        spot = lane_of + (start - row * cross)
        place = jnp.full((8, LANES), row, jnp.int32)
        for step in range(1, LANES // cross + 2):
            past = spot >= step * cross
            place = place + past.astype(jnp.int32)
        spot = lane_of + start - place * cross
        layer = jnp.where(high, cross - 1 - spot, spot)
        return jnp.where(layer < 2, place + HALF * layer, -1)

    def build_spread(index_ref, mask_ref, high, used):
        for tile in range(width // LANES):
            index = jnp.where(used, spread_index(tile, high), -1)
            mask_ref[tile] = jnp.where(index >= 0, 1.0, 0.0)
            index_ref[tile] = jnp.maximum(index, 0)

    def build_faces():
        build_spread(face_index, face_mask, jnp.full((8, LANES), select(on_high, 1, 0)) > 0,
                     jnp.full((8, LANES), select(on_second, 1, 0)) > 0)

    def build_delta():
        def chosen(sides):
            flags = [select(jnp.logical_or(near_joins[sides[0]], near_joins[sides[1]]), 1, 0)
                     for near_joins in (joins_before, joins_after)]
            return jnp.where(row_in < 4, flags[0], flags[1]) > 0

        build_spread(delta_index, delta_mask, chosen((1, 3)), chosen((2, 3)))

    source_of = jnp.where(face_lane, place_of, 0) * cross + select(on_high, cross - 1 - layer_of, layer_of)
    source_tile, source_lane = split_index(source_of, LANES, width // LANES)
    flip_rows = select(flip_along == 1, 7 - row_in, row_in)
    flip_lanes = jnp.where(face_lane, layer_of * HALF + select(flip_across == 1, cross - 1 - place_of, place_of), lane_of)

    def by_rows(value, function):
        return jnp.concatenate([function(value[at:at + 8]) for at in range(0, value.shape[0], 8)], axis=0)

    def flipped(value):
        parts = []
        for at in range(0, value.shape[0], length):
            low, high = value[at:at + 8], value[at + 8:at + 16]
            for half in (select(flip_along == 1, high, low), select(flip_along == 1, low, high)):
                parts.append(take(take(half, flip_rows, 0), flip_lanes, 1))
        return jnp.concatenate(parts, axis=0)

    def split_up(value, into):
        count = value.shape[0]
        lead, trail = halves(value)
        into[:count] = lead
        into[count:2 * count] = trail

    def gathered(low, high, tile_of):
        packed = None
        for tile in range(width // LANES):
            part = by_rows(tile_of(tile), lambda x: take(x, source_lane, 1))
            here = jnp.concatenate([source_tile == tile] * (part.shape[0] // 8), axis=0)
            packed = part if packed is None else jnp.where(here, part, packed)
        near, far = LANES - cross, LANES - 2 * cross
        lower = jnp.where(lane_row < HALF, low, pltpu.roll(low, HALF - cross, 1))
        upper = jnp.where(lane_row < HALF, pltpu.roll(high, LANES - near, 1), pltpu.roll(high, HALF - far, 1))
        return jnp.where(on_first, jnp.where(on_high, upper, lower), packed)

    def gather_face(padded):
        def tile_of(tile):
            start = LANES + tile * LANES
            return padded[:, :, start:start + LANES].reshape(rows, LANES)

        return gathered(tile_of(0), tile_of(width // LANES - 1), tile_of)

    def gather_metric():
        def tile_of(tile, base=6):
            return geometry[base:base + 3, :, tile * LANES:(tile + 1) * LANES].reshape(3 * length, LANES)

        return gathered(tile_of(0, 3), tile_of(width // LANES - 1, 3), tile_of)

    near, far = LANES - cross, LANES - 2 * cross

    def to_lower(value):
        return jnp.where(lane_row < cross, value, pltpu.roll(value, LANES - (HALF - cross), 1))

    def to_upper(value):
        return jnp.where(lane_row >= near, pltpu.roll(value, near, 1), pltpu.roll(value, LANES - (HALF - far), 1))

    def spread(value, index_ref, mask_ref, lower, upper, write):
        for tile in range(width // LANES):
            index, mask = index_ref[tile], mask_ref[tile]
            add = by_rows(value, lambda x: take(x, index, 1) * mask)
            if tile == 0:
                add = add + lower
            if tile == width // LANES - 1:
                add = add + upper
            write(tile * LANES, add)

    def spread_face(value, read, write):
        on_low = jnp.logical_not(on_high)
        lower = jnp.where(jnp.logical_and(lane_row < 2 * cross, jnp.logical_and(on_first, on_low)), to_lower(value), 0.0)
        upper = jnp.where(jnp.logical_and(lane_row >= far, jnp.logical_and(on_first, on_high)), to_upper(value), 0.0)

        def put(start, add):
            for c in range(4):
                write(c, start, read(c, start) + add[c * length:(c + 1) * length])

        spread(value, face_index, face_mask, lower, upper, put)

    def spread_delta():
        end_row = lax.broadcasted_iota(jnp.int32, (8, LANES), 0)
        wanted = jnp.logical_or(jnp.logical_and(end_row < 2, has_before), jnp.logical_and(end_row >= 6, has_after))
        value = jnp.concatenate([jnp.where(wanted, delta_in[c], 0.0) for c in range(4)], axis=0)

        def mask(side):
            flag = [select(flags[side], 1.0, 0.0) for flags in (joins_before, joins_after)]
            one = jnp.where(end_row < 4, flag[0], flag[1])
            return jnp.concatenate([one] * 4, axis=0)

        lower = jnp.where(lane_row < 2 * cross, to_lower(value) * mask(0), 0.0)
        upper = jnp.where(lane_row >= far, to_upper(value) * mask(1), 0.0)
        def put(start, add):
            for c in range(4):
                at = slice(start, start + LANES)
                ghost_rows[1, c, :, at] = ghost_rows[1, c, :, at] + add[c * 8:(c + 1) * 8]

        spread(value, delta_index, delta_mask, lower, upper, put)

    def along_i():
        piece = 2 * LANES
        for part in range(width // piece):
            at = slice(part * piece, (part + 1) * piece)
            out = jnp.dot(i_matrix[...], split[:, at], preferred_element_type=jnp.float32)
            slope_i[:, :, at] = out[:rows].reshape(4, length, piece)
            bend_i[:, :, at] = out[rows:].reshape(3, length, piece)

    def along_k():
        count = 3 * length
        parts = []
        for step in range(chunks):
            at = slice(step * chunk, (step + 1) * chunk)
            parts.append(jnp.concatenate([split[:rows, at], split[rows:, at]], axis=1))
        velocity = jnp.concatenate([part[:count] for part in parts], axis=0)
        pressure = jnp.concatenate([part[count:] for part in parts], axis=0)
        slope = jnp.dot(velocity, k_slope_uvw[...], preferred_element_type=jnp.float32)
        bend = jnp.dot(velocity, k_bend[...], preferred_element_type=jnp.float32)
        slope_p = jnp.dot(pressure, k_slope_p[...], preferred_element_type=jnp.float32)
        for step in range(chunks):
            at = slice(step * chunk, (step + 1) * chunk)
            slope_k[:3, :, at] = slope[step * count:(step + 1) * count].reshape(3, length, chunk)
            bend_k[:, :, at] = bend[step * count:(step + 1) * count].reshape(3, length, chunk)
            slope_k[3, :, at] = slope_p[step * length:(step + 1) * length]

    def chain_copies(kind):
        if kind == 0:
            low, high = first.at[:, 0:2, inner], first.at[:, length - 2:length, inner]
        else:
            source = end_rows if kind == 1 else delta_out
            low, high = source.at[:, 0:2], source.at[:, 6:8]
        target = delta_in if kind == 2 else ghost_rows.at[kind]
        to_before = pltpu.make_async_remote_copy(
            low, target.at[:, 6:8], chain_send.at[kind, 0], chain_recv.at[kind, 0],
            device_id={"blk": before}, device_id_type=MESH)
        to_after = pltpu.make_async_remote_copy(
            high, target.at[:, 0:2], chain_send.at[kind, 1], chain_recv.at[kind, 1],
            device_id={"blk": after}, device_id_type=MESH)
        return to_before, to_after

    def face_copies(kind):
        used = pl.ds(0, 3 * length if kind == 1 else rows)
        return [pltpu.make_async_remote_copy(
            face_out.at[kind, used], face_in.at[kind, offset - 1, used], face_send.at[kind, offset - 1],
            face_recv.at[kind, offset - 1], device_id={"seg": to_seg(offset)}, device_id_type=MESH)
            for offset in order]

    def start_faces(kind):
        for copy in face_copies(kind):
            copy.start()

    def await_faces(kind):
        for copy in face_copies(kind):
            copy.wait_recv()

    def start_chain(kind):
        to_before, to_after = chain_copies(kind)

        @pl.when(has_before)
        def _():
            to_before.start()

        @pl.when(has_after)
        def _():
            to_after.start()

    def open_ends(padded, turn):
        @pl.when(jnp.logical_not(has_before))
        def _():
            for c in range(4):
                ghost_rows[turn, c, 0:1, :] = -WALL[c] * padded[c, 1:2, inner]
                ghost_rows[turn, c, 1:2, :] = -WALL[c] * padded[c, 0:1, inner]

        @pl.when(jnp.logical_not(has_after))
        def _():
            for c in range(4):
                ghost_rows[turn, c, 6:7, :] = -WALL[c] * padded[c, length - 1:length, inner]
                ghost_rows[turn, c, 7:8, :] = -WALL[c] * padded[c, length - 2:length - 1, inner]

    def await_chain(kind):
        to_before, to_after = chain_copies(kind)

        @pl.when(has_before)
        def _():
            to_after.wait_recv()

        @pl.when(has_after)
        def _():
            to_before.wait_recv()

    def sent_chain(kind):
        to_before, to_after = chain_copies(kind)

        @pl.when(has_before)
        def _():
            to_before.wait_send()

        @pl.when(has_after)
        def _():
            to_after.wait_send()

    lane = lax.broadcasted_iota(jnp.int32, (length, chunk), 1)

    def central(minus2, minus1, plus1, plus2, bent):
        slope = (minus2 - plus2) + 8.0 * (plus1 - minus1)
        return slope, 16.0 * (minus1 + plus1) - (minus2 + plus2) if bent else None

    def along_j(wide, value, wall, is_first, is_last, bent):
        def moved(step):
            if step > 0:
                return pltpu.roll(wide[:, :LANES + chunk], step, 1)[:, LANES:]
            return pltpu.roll(wide[:, LANES:], LANES + chunk + step, 1)[:, :chunk]
        minus2, minus1, plus1, plus2 = moved(2 * cross), moved(cross), moved(-cross), moved(-2 * cross)
        m1, m2, p1, p2 = minus1, minus2, plus1, plus2
        if is_first:
            m1 = jnp.where(lane < cross, wall * value, minus1)
            m2 = jnp.where(lane < cross, wall * plus1, jnp.where(lane < 2 * cross, wall * minus1, minus2))
        if is_last:
            p1 = jnp.where(lane >= chunk - cross, wall * value, plus1)
            p2 = jnp.where(lane >= chunk - cross, wall * minus1,
                           jnp.where(lane >= chunk - 2 * cross, wall * plus1, plus2))
        return central(m2, m1, p1, p2, bent)

    def inside_rates(padded, fresh, finish):
        def at_chunk(start, is_first, is_last):
            at = pl.ds(start, chunk)
            wide = [padded[c, :, pl.ds(start, chunk + 2 * LANES)] for c in range(4)]
            values = [w[:, LANES:LANES + chunk] for w in wide]
            sums, total = None, None
            for direction in range(3):
                metric = [geometry[3 * direction + b, :, at] for b in range(3)]
                if direction == 1:
                    slopes, bends = [], []
                    for c in range(4):
                        slope, bend = along_j(wide[c], values[c], WALL[c], is_first, is_last, c < 3)
                        slopes.append(slope)
                        bends.append(bend)
                else:
                    slope_ref, bend_ref = (slope_i, bend_i) if direction == 0 else (slope_k, bend_k)
                    slopes = [slope_ref[c, :, at] for c in range(4)]
                    bends = [bend_ref[c, :, at] for c in range(3)]
                if fresh:
                    norm = viscosity * (metric[0] * metric[0] + metric[1] * metric[1] + metric[2] * metric[2])
                    norms[direction, :, at] = norm
                    total = norm if total is None else total + norm
                else:
                    norm = norms[direction, :, at]
                carried = metric[0] * values[0] + metric[1] * values[1] + metric[2] * values[2]
                parts = [norm * bends[c] - carried * slopes[c] - metric[c] * slopes[3] for c in range(3)]
                parts.append(metric[0] * slopes[0] + metric[1] * slopes[1] + metric[2] * slopes[2])
                sums = parts if sums is None else [a + b for a, b in zip(sums, parts)]
            if fresh:
                total = 30.0 * total
                norms[3, :, at] = total
            else:
                total = norms[3, :, at]
            for c in range(4):
                finish(c, start, values[c], sums[c] - total * values[c] if c < 3 else sums[c])

        at_chunk(0, True, chunks == 1)
        if chunks > 2:
            for step in range(1, chunks - 1):
                at_chunk(step * chunk, False, False)
        if chunks > 1:
            at_chunk((chunks - 1) * chunk, False, True)

    sub = lax.broadcasted_iota(jnp.int32, (8, chunk), 0)
    near_row = jnp.where(jnp.logical_or(sub == 0, sub == 7), 1.0, 0.0)
    row_sign = jnp.where(sub < 4, 1.0, -1.0)

    def chain_rates(padded, turn, scale, read, write, keep=None):
        for step in range(chunks):
            start = step * chunk
            at = pl.ds(start, chunk)

            def ends(low, high):
                return jnp.where(sub < 4, low, high)

            inside = pl.ds(start + LANES, chunk)
            values = [ends(padded[c, :8, inside], padded[c, length - 8:, inside]) for c in range(3)]
            metric = [ends(geometry[b, :8, at], geometry[b, length - 8:, at]) for b in range(3)]
            moved = [ghost_rows[turn, c, :, at] for c in range(4)]
            ghosts = [ends(pltpu.roll(m, 7, 0), pltpu.roll(m, 1, 0)) for m in moved]
            sums = ghost_rates(near_row, ghost_terms(scale, row_sign, near_row, metric, values), ghosts, moved)
            low, high = pl.ds(0, 8), pl.ds(length - 8, 8)
            for c in range(4):
                low_new = read(c, low, start) + jnp.where(sub < 2, sums[c], 0.0)
                high_new = read(c, high, start) + jnp.where(sub >= 6, sums[c], 0.0)
                write(c, low, start, low_new)
                write(c, high, start, high_new)
                if keep is not None:
                    keep[c, :, at] = ends(low_new, high_new)

    def at_part(value, c):
        return value[c * length:(c + 1) * length]

    def terms_of(scale, sign, metric, own):
        return ghost_terms(scale, sign, near_lane, [at_part(metric, b) for b in range(3)],
                           [at_part(own, b) for b in range(3)])

    def prepare_terms(scale, metric, own):
        edge, outer, pull = terms_of(scale, face_sign, metric, own)
        terms_ref[0] = edge
        terms_ref[1] = outer
        for b in range(3):
            terms_ref[2 + b] = pull[b]

    def own_terms():
        return terms_ref[0], terms_ref[1], [terms_ref[2 + b] for b in range(3)]

    def received(kind, count):
        value = face_in[kind, order[-1] - 1, :count]
        for offset in order[:-1]:
            value = jnp.where(comes_from[offset], face_in[kind, offset - 1, :count], value)
        return value

    def face_rates(terms, theirs, own):
        ghosts = [at_part(theirs, c) - WALL[c] * at_part(own, c) for c in range(4)]
        moved = [pltpu.roll(g, HALF, 1) for g in ghosts]
        return jnp.concatenate(ghost_rates(near_lane, terms, ghosts, moved), axis=0)

    def inside_second(start, size):
        return pl.ds(start + LANES if isinstance(start, int) else pl.multiple_of(start + LANES, LANES), size)

    step_one, step_two = time_step / 12.0, 0.5 * time_step / 12.0

    factor = (1.0, 1.0, 1.0, -compress)

    def finish_first(c, start, value, rate):
        second[c, :, inside_second(start, chunk)] = value + (step_one * factor[c]) * rate

    def finish_second(c, start, value, rate):
        base = first[c, :, inside_second(start, chunk)]
        out_ref[c, :, pl.ds(start, chunk)] = 0.5 * (base + value) + (step_two * factor[c]) * rate

    def read_second(c, which, start):
        return second[c, which, inside_second(start, chunk)]

    def write_second(c, which, start, value):
        second[c, which, inside_second(start, chunk)] = value

    def read_out(c, which, start):
        return out_ref[c, which, pl.ds(start, chunk)]

    def write_out(c, which, start, value):
        out_ref[c, which, pl.ds(start, chunk)] = value

    def tile_second(c, start):
        return second[c, :, start + LANES:start + 2 * LANES]

    def put_second(c, start, value):
        second[c, :, start + LANES:start + 2 * LANES] = value

    def tile_out(c, start):
        return out_ref[c, :, start:start + LANES]

    def put_out(c, start, value):
        out_ref[c, :, start:start + LANES] = value

    load_state.wait()
    face_out[0] = gather_face(first)
    pl.semaphore_wait(barrier, segs - 1 + has_before.astype(jnp.int32) + has_after.astype(jnp.int32))
    start_faces(0)
    start_chain(0)

    load_metric.wait()
    valid = jnp.where(jnp.logical_and(in_face, any_join), 1.0, 0.0)
    own_metric = valid * gather_metric()
    face_out[1, :3 * length] = own_metric
    start_faces(1)
    open_ends(first, 0)
    build_faces()
    build_delta()
    prepare_terms(step_one, own_metric, face_out[0])
    split_up(first[:, :, inner].reshape(rows, width), split)
    along_i()
    along_k()
    inside_rates(first, True, finish_first)

    await_chain(0)
    chain_rates(first, 0, step_one, read_second, write_second, end_rows)
    start_chain(1)
    face_out[2] = gather_face(second)
    start_faces(2)

    turned_ref[...] = flipped(face_out[0])
    await_faces(0)
    added = face_rates(own_terms(), flipped(received(0, rows)), face_out[0])
    for c in range(4):
        delta_out[c] = jnp.where(lax.broadcasted_iota(jnp.int32, (8, LANES), 0) < 4,
                                 added[c * length:c * length + 8], added[(c + 1) * length - 8:(c + 1) * length])
    start_chain(2)
    added_ref[...] = face_out[2] + added
    spread_face(added, tile_second, put_second)
    open_ends(second, 1)
    split_up(second[:, :, inner].reshape(rows, width), split)
    along_i()
    along_k()
    inside_rates(second, False, finish_second)
    prepare_terms(step_two, face_out[1, :3 * length], added_ref[...])
    await_faces(1)
    their_face = received(0, rows)
    their_terms = terms_of(step_one, partner_sign, received(1, 3 * length), their_face)
    theirs_ref[...] = face_rates(their_terms, turned_ref[...], their_face)

    await_chain(1)
    await_chain(2)
    spread_delta()
    chain_rates(second, 1, step_two, read_out, write_out)
    await_faces(2)
    their_face = flipped(received(2, rows) + theirs_ref[...])
    spread_face(face_rates(own_terms(), their_face, added_ref[...]), tile_out, put_out)

    for kind in range(3):
        for copy in face_copies(kind):
            copy.wait_send()
        sent_chain(kind)


def on_device(state, metric, block_map, links):
    segs, chain = lax.axis_size("seg"), lax.axis_size("blk")
    _, parts, length, width = state.shape
    cross = math.isqrt(width)
    assert cross <= HALF and length == 16
    chunk = math.lcm(cross, LANES)
    links = links.transpose(1, 2, 0)
    f32, bf16, dma = jnp.float32, jnp.bfloat16, pltpu.SemaphoreType.DMA
    result = pl.pallas_call(
        functools.partial(kernel, segs, chain, cross),
        out_shape=pltpu.VMEM((parts, length, width), f32),
        in_specs=[pl.BlockSpec(memory_space=pl.ANY)] * 4,
        out_specs=pl.BlockSpec(memory_space=pltpu.VMEM),
        scratch_shapes=[
            pltpu.VMEM((parts, length, width + 2 * LANES), f32),
            pltpu.VMEM((parts, length, width + 2 * LANES), f32),
            pltpu.VMEM((9, length, width), f32),
            pltpu.VMEM((width // LANES, 8, LANES), jnp.int32),
            pltpu.VMEM((width // LANES, 8, LANES), f32),
            pltpu.VMEM((width // LANES, 8, LANES), jnp.int32),
            pltpu.VMEM((width // LANES, 8, LANES), f32),
            pltpu.VMEM((2 * parts * length, width), bf16),
            pltpu.VMEM((2 * chunk, chunk), bf16),
            pltpu.VMEM((2 * chunk, chunk), bf16),
            pltpu.VMEM((2 * chunk, chunk), bf16),
            pltpu.VMEM((7 * length, LANES), bf16),
            pltpu.VMEM((parts, length, width), f32),
            pltpu.VMEM((parts - 1, length, width), f32),
            pltpu.VMEM((parts, length, width), f32),
            pltpu.VMEM((parts - 1, length, width), f32),
            pltpu.VMEM((parts, length, width), f32),
            pltpu.VMEM((5, length, LANES), f32),
            pltpu.VMEM((parts * length, LANES), f32),
            pltpu.VMEM((parts * length, LANES), f32),
            pltpu.VMEM((parts * length, LANES), f32),
            pltpu.VMEM((2, parts, 8, width), f32),
            pltpu.VMEM((parts, 8, width), f32),
            pltpu.VMEM((parts, 8, LANES), f32),
            pltpu.VMEM((parts, 8, LANES), f32),
            pltpu.VMEM((3, parts * length, LANES), f32),
            pltpu.VMEM((3, segs - 1, parts * length, LANES), f32),
            pltpu.SMEM(block_map.shape, jnp.int32),
            pltpu.SMEM(links.shape, jnp.int32),
            dma((4,)), dma((3, 2)), dma((3, 2)), dma((3, segs - 1)), dma((3, segs - 1)),
        ],
        compiler_params=pltpu.CompilerParams(collective_id=0, has_side_effects=True),
    )(state, metric, block_map, links)
    return result.reshape(state.shape)


def solution(mesh):
    in_specs = (P(("seg", "blk"), None, None, None), P(("seg", "blk"), None, None, None), P(), P())
    out_specs = P(("seg", "blk"), None, None, None)
    return jax.shard_map(
        on_device, mesh=mesh, in_specs=in_specs, out_specs=out_specs, check_vma=False
    )
```

```python
import functools
import math

import jax
import jax.numpy as jnp
from jax import lax
from jax.experimental import pallas as pl
from jax.experimental.pallas import tpu as pltpu
from jax.sharding import PartitionSpec as P

time_step = 0.05
viscosity = 0.2
compress = 1.0
MESH = pl.DeviceIdType.MESH
LANES = 128
HALF = LANES // 2
WALL = (-1.0, -1.0, -1.0, 1.0)


def split_index(index, size, count):
    quotient = jnp.zeros_like(index)
    for step in range(1, count):
        quotient += (index >= size * step).astype(jnp.int32)
    return quotient, index - size * quotient


def take(value, index, axis):
    numbers = lax.GatherDimensionNumbers(
        offset_dims=(), collapsed_slice_dims=(axis,), start_index_map=(axis,),
        operand_batching_dims=(1 - axis,), start_indices_batching_dims=(1 - axis,))
    return lax.gather(value, index[..., None], numbers, slice_sizes=(1, 1),
                      mode=lax.GatherScatterMode.PROMISE_IN_BOUNDS)


def flipped_bits(index, bits):
    bit = 1
    while bit <= bits:
        if bits & bit:
            index = index + bit - 2 * bit * lax.rem(lax.div(index, bit), 2)
        bit *= 2
    return index


def halves(value):
    lead = value.astype(jnp.bfloat16)
    return lead, (value - lead.astype(jnp.float32)).astype(jnp.bfloat16)


def select(flag, yes, no):
    return jnp.where(flag, yes, no)


def ghost_terms(scale, sign, near, metric, values):
    carried = sign * (metric[0] * values[0] + metric[1] * values[1] + metric[2] * values[2])
    norm = viscosity * (metric[0] * metric[0] + metric[1] * metric[1] + metric[2] * metric[2])
    edge = (8.0 * scale) * (2.0 * norm + carried) * near
    outer = scale * (norm + carried)
    return edge, outer, [(scale * sign) * m for m in metric]


def ghost_rates(near, terms, ghosts, moved):
    edge, outer, pull = terms
    eight = 8.0 * near
    slopes = [m - eight * g for g, m in zip(ghosts, moved)]
    parts = [edge * ghosts[c] - outer * moved[c] - pull[c] * slopes[3] for c in range(3)]
    parts.append(-compress * (pull[0] * slopes[0] + pull[1] * slopes[1] + pull[2] * slopes[2]))
    return parts


def kernel(segs, chain, cross, state_hbm, metric_hbm, block_map_hbm, links_hbm, out_ref,
           first, second, geometry, face_index, face_mask, delta_index, delta_mask, face_hot, split,
           k_slope_uvw, k_slope_p, k_bend, i_matrix, slope_k, bend_k, slope_i, bend_i, norms,
           terms_ref, added_ref, theirs_ref, turned_ref,
           ghost_rows, end_rows, delta_out, delta_in, face_out, face_in, block_map, links,
           load_sem, chain_send, chain_recv, face_send, face_recv):
    length, width = out_ref.shape[1], out_ref.shape[2]
    rows = 4 * length
    chunk = math.lcm(cross, LANES)
    chunks = width // chunk
    inner = pl.ds(LANES, width)
    seg, pos = lax.axis_index("seg"), lax.axis_index("blk")
    me = seg * chain + pos
    has_before, has_after = pos > 0, pos < chain - 1
    before, after = lax.rem(pos + chain - 1, chain), lax.rem(pos + 1, chain)
    paired = segs & (segs - 1) == 0
    order = range(segs - 1, 0, -1)

    def to_seg(offset):
        return flipped_bits(seg, offset) if paired else lax.rem(seg + offset, segs)

    def from_seg(offset):
        return flipped_bits(seg, offset) if paired else lax.rem(seg + segs - offset, segs)

    barrier = pltpu.get_barrier_semaphore()
    for offset in order:
        pl.semaphore_signal(barrier, inc=1, device_id={"seg": to_seg(offset)}, device_id_type=MESH)

    @pl.when(has_before)
    def _():
        pl.semaphore_signal(barrier, inc=1, device_id={"blk": before}, device_id_type=MESH)

    @pl.when(has_after)
    def _():
        pl.semaphore_signal(barrier, inc=1, device_id={"blk": after}, device_id_type=MESH)

    load_map = pltpu.make_async_copy(block_map_hbm, block_map, load_sem.at[2])
    load_links = pltpu.make_async_copy(links_hbm, links, load_sem.at[3])
    load_state = pltpu.make_async_copy(state_hbm.at[0], first.at[:, :, inner], load_sem.at[0])
    load_metric = pltpu.make_async_copy(metric_hbm.at[0], geometry, load_sem.at[1])
    load_map.start()
    load_links.start()
    load_state.start()
    load_metric.start()

    lane_row = lax.broadcasted_iota(jnp.int32, (1, LANES), 1)
    face_layer = (lane_row >= HALF).astype(jnp.int32)
    face_place = lane_row - HALF * face_layer
    in_face = face_place < cross
    near_lane = (lane_row < HALF).astype(jnp.float32)

    def build_k():
        here = lax.broadcasted_iota(jnp.int32, (cross, LANES), 0)
        column = lax.broadcasted_iota(jnp.int32, (cross, LANES), 1)
        for group in range(chunk // cross):
            first_row = group * cross
            for tile in range(chunk // LANES):
                lanes = slice(tile * LANES, (tile + 1) * LANES)
                if not first_row // LANES <= tile <= (first_row + cross - 1) // LANES:
                    for matrix in (k_slope_uvw, k_slope_p, k_bend):
                        for top in (first_row, chunk + first_row):
                            matrix[top:top + cross, lanes] = jnp.zeros((cross, LANES), jnp.bfloat16)
                    continue
                there = column + (tile * LANES - first_row)
                there = jnp.where(jnp.logical_and(there >= 0, there < cross), there, 4 * width)
                offset, mirrored = here - there, here + there

                def at(index, value, factor):
                    return jnp.where(index == value, factor, 0.0)

                slope = at(offset, -2, 1.0) + at(offset, -1, -8.0) + at(offset, 1, 8.0) + at(offset, 2, -1.0)
                bend = at(offset, -2, -1.0) + at(offset, -1, 16.0) + at(offset, 1, 16.0) + at(offset, 2, -1.0)
                end = 2 * cross - 2
                wall_slope = (at(mirrored, 0, -8.0) + at(mirrored, 1, 1.0)
                              + at(mirrored, end, 8.0) + at(mirrored, end - 1, -1.0))
                wall_bend = (at(mirrored, 0, 16.0) + at(mirrored, 1, -1.0)
                             + at(mirrored, end, 16.0) + at(mirrored, end - 1, -1.0))
                for matrix, value in ((k_slope_uvw, slope + WALL[0] * wall_slope),
                                      (k_slope_p, slope + WALL[3] * wall_slope),
                                      (k_bend, bend + WALL[0] * wall_bend)):
                    value = value.astype(jnp.bfloat16)
                    matrix[first_row:first_row + cross, lanes] = value
                    matrix[chunk + first_row:chunk + first_row + cross, lanes] = value

    pads = jnp.zeros((4, length, LANES), jnp.float32)
    for padded in (first, second):
        padded[:, :, :LANES] = pads
        padded[:, :, LANES + width:] = pads
    build_k()

    def build_i():
        count = 7 * length
        term, here = split_index(lax.broadcasted_iota(jnp.int32, (count, LANES), 0), length, 7)
        part, there = split_index(lax.broadcasted_iota(jnp.int32, (count, LANES), 1), length, 8)
        part = jnp.where(part >= 4, part - 4, part)
        offset = there - here

        def at(index, factor):
            return jnp.where(offset == index, factor, 0.0)

        slope = at(-2, 1.0) + at(-1, -8.0) + at(1, 8.0) + at(2, -1.0)
        bend = at(-2, -1.0) + at(-1, 16.0) + at(1, 16.0) + at(2, -1.0)
        value = jnp.where(term == part, slope, jnp.where(term == part + 4, bend, 0.0))
        i_matrix[...] = value.astype(jnp.bfloat16)

    build_i()

    load_map.wait()
    load_links.wait()
    block = block_map[me]

    def joined_side(number):
        return [links[2 + side, 0, number] >= 0 for side in range(4)]

    joins = joined_side(block)
    partner, partner_face = jnp.int32(-1), jnp.int32(0)
    flip_along, flip_across = jnp.int32(0), jnp.int32(0)
    for side in range(4):
        partner = select(joins[side], links[2 + side, 0, block], partner)
        partner_face = select(joins[side], links[2 + side, 1, block], partner_face)
        flip_along = select(joins[side], links[2 + side, 2, block], flip_along)
        flip_across = select(joins[side], links[2 + side, 3, block], flip_across)
    any_join = partner >= 0
    on_first = jnp.logical_or(joins[0], joins[1])
    on_second = jnp.logical_or(joins[2], joins[3])
    on_high = jnp.logical_or(joins[1], joins[3])
    joins_before = joined_side(block_map[seg * chain + before])
    joins_after = joined_side(block_map[seg * chain + after])
    comes_from = {offset: block_map[from_seg(offset) * chain + pos] == partner for offset in order}
    face_sign = select(on_high, -1.0, 1.0)
    partner_sign = select(jnp.logical_or(partner_face == 3, partner_face == 5), -1.0, 1.0)

    lane_of = lax.broadcasted_iota(jnp.int32, (8, LANES), 1)
    row_in = lax.broadcasted_iota(jnp.int32, (8, LANES), 0)
    layer_of = (lane_of >= HALF).astype(jnp.int32)
    place_of = lane_of - HALF * layer_of
    face_lane = place_of < cross

    tiles = width // LANES
    split_tile = tiles // 4 * 2

    def spread_index(tile, high):
        start = tile * LANES
        row = start // cross
        spot = lane_of + (start - row * cross)
        place = jnp.full((8, LANES), row, jnp.int32)
        for step in range(1, LANES // cross + 2):
            past = spot >= step * cross
            place = place + past.astype(jnp.int32)
        spot = lane_of + start - place * cross
        layer = jnp.where(high, cross - 1 - spot, spot)
        return jnp.where(layer < 2, place + HALF * layer, -1)

    def build_spread(index_ref, mask_ref, high, used):
        for tile in range(width // LANES):
            index = jnp.where(used, spread_index(tile, high), -1)
            mask_ref[tile] = jnp.where(index >= 0, 1.0, 0.0)
            index_ref[tile] = jnp.maximum(index, 0)

    def build_faces():
        build_spread(face_index, face_mask, jnp.full((8, LANES), select(on_high, 1, 0)) > 0,
                     jnp.full((8, LANES), select(on_second, 1, 0)) > 0)

        cells = lax.broadcasted_iota(jnp.int32, (2 * LANES, LANES), 0)
        source = jnp.where(face_lane, source_of, -1)[0:1]
        source = source - (1 - select(on_second, 1, 0)) * (2 * width)
        for piece in range((tiles - split_tile) // 2):
            start = (split_tile + 2 * piece) * LANES
            hit = (cells == source - start).astype(jnp.float32).astype(jnp.bfloat16)
            face_hot[piece * 2 * LANES:(piece + 1) * 2 * LANES, :] = hit

    def build_delta():
        def chosen(sides):
            flags = [select(jnp.logical_or(near_joins[sides[0]], near_joins[sides[1]]), 1, 0)
                     for near_joins in (joins_before, joins_after)]
            return jnp.where(row_in < 4, flags[0], flags[1]) > 0

        build_spread(delta_index, delta_mask, chosen((1, 3)), chosen((2, 3)))

    source_of = jnp.where(face_lane, place_of, 0) * cross + select(on_high, cross - 1 - layer_of, layer_of)
    source_tile, source_lane = split_index(source_of, LANES, width // LANES)
    flip_rows = select(flip_along == 1, 7 - row_in, row_in)
    flip_lanes = jnp.where(face_lane, layer_of * HALF + select(flip_across == 1, cross - 1 - place_of, place_of), lane_of)

    def by_rows(value, function):
        return jnp.concatenate([function(value[at:at + 8]) for at in range(0, value.shape[0], 8)], axis=0)

    def flipped(value):
        parts = []
        for at in range(0, value.shape[0], length):
            low, high = value[at:at + 8], value[at + 8:at + 16]
            for half in (select(flip_along == 1, high, low), select(flip_along == 1, low, high)):
                parts.append(take(take(half, flip_rows, 0), flip_lanes, 1))
        return jnp.concatenate(parts, axis=0)

    def split_up(value, into):
        count = value.shape[0]
        lead, trail = halves(value)
        into[:count] = lead
        into[count:2 * count] = trail

    def gathered(low, high, tile_of, rest=None):
        packed = None if rest is None else rest
        for tile in range(tiles if rest is None else split_tile):
            part = by_rows(tile_of(tile), lambda x: take(x, source_lane, 1))
            here = jnp.concatenate([source_tile == tile] * (part.shape[0] // 8), axis=0)
            packed = part if packed is None else jnp.where(here, part, packed)
        near, far = LANES - cross, LANES - 2 * cross
        lower = jnp.where(lane_row < HALF, low, pltpu.roll(low, HALF - cross, 1))
        upper = jnp.where(lane_row < HALF, pltpu.roll(high, LANES - near, 1), pltpu.roll(high, HALF - far, 1))
        return jnp.where(on_first, jnp.where(on_high, upper, lower), packed)

    def gather_face(padded, shared):
        def tile_of(tile):
            start = LANES + tile * LANES
            return padded[:, :, start:start + LANES].reshape(rows, LANES)

        if not shared:
            return gathered(tile_of(0), tile_of(tiles - 1), tile_of)
        value = padded[:, :, LANES + split_tile * LANES:LANES + width].reshape(rows, (tiles - split_tile) * LANES)
        both = jnp.concatenate(halves(value), axis=0)
        rest = jnp.dot(both, face_hot[...], preferred_element_type=jnp.float32)
        return gathered(tile_of(0), tile_of(tiles - 1), tile_of, rest[:rows] + rest[rows:])

    def gather_metric():
        def tile_of(tile, base=6):
            return geometry[base:base + 3, :, tile * LANES:(tile + 1) * LANES].reshape(3 * length, LANES)

        return gathered(tile_of(0, 3), tile_of(width // LANES - 1, 3), tile_of)

    near, far = LANES - cross, LANES - 2 * cross

    def to_lower(value):
        return jnp.where(lane_row < cross, value, pltpu.roll(value, LANES - (HALF - cross), 1))

    def to_upper(value):
        return jnp.where(lane_row >= near, pltpu.roll(value, near, 1), pltpu.roll(value, LANES - (HALF - far), 1))

    def spread(value, index_ref, mask_ref, lower, upper, write, shared):
        last = split_tile if shared else tiles
        if shared:
            both = jnp.concatenate(halves(value), axis=0)
            for piece in range((tiles - last) // 2):
                add = lax.dot_general(both, face_hot[piece * 2 * LANES:(piece + 1) * 2 * LANES, :],
                                      (((1,), (1,)), ((), ())), preferred_element_type=jnp.float32)
                add = add[:rows] + add[rows:]
                for side in range(2):
                    tile = last + 2 * piece + side
                    part = add[:, side * LANES:(side + 1) * LANES]
                    write(tile * LANES, part + upper if tile == tiles - 1 else part)
        for tile in range(last):
            index, mask = index_ref[tile], mask_ref[tile]
            add = by_rows(value, lambda x: take(x, index, 1) * mask)
            if tile == 0:
                add = add + lower
            if tile == width // LANES - 1:
                add = add + upper
            write(tile * LANES, add)

    def spread_face(value, read, write):
        on_low = jnp.logical_not(on_high)
        lower = jnp.where(jnp.logical_and(lane_row < 2 * cross, jnp.logical_and(on_first, on_low)), to_lower(value), 0.0)
        upper = jnp.where(jnp.logical_and(lane_row >= far, jnp.logical_and(on_first, on_high)), to_upper(value), 0.0)

        def put(start, add):
            for c in range(4):
                write(c, start, read(c, start) + add[c * length:(c + 1) * length])

        spread(value, face_index, face_mask, lower, upper, put, True)

    def spread_delta():
        end_row = lax.broadcasted_iota(jnp.int32, (8, LANES), 0)
        wanted = jnp.logical_or(jnp.logical_and(end_row < 2, has_before), jnp.logical_and(end_row >= 6, has_after))
        value = jnp.concatenate([jnp.where(wanted, delta_in[c], 0.0) for c in range(4)], axis=0)

        def mask(side):
            flag = [select(flags[side], 1.0, 0.0) for flags in (joins_before, joins_after)]
            one = jnp.where(end_row < 4, flag[0], flag[1])
            return jnp.concatenate([one] * 4, axis=0)

        lower = jnp.where(lane_row < 2 * cross, to_lower(value) * mask(0), 0.0)
        upper = jnp.where(lane_row >= far, to_upper(value) * mask(1), 0.0)
        def put(start, add):
            for c in range(4):
                at = slice(start, start + LANES)
                ghost_rows[1, c, :, at] = ghost_rows[1, c, :, at] + add[c * 8:(c + 1) * 8]

        spread(value, delta_index, delta_mask, lower, upper, put, False)

    def along_i():
        piece = 2 * LANES
        for part in range(width // piece):
            at = slice(part * piece, (part + 1) * piece)
            out = jnp.dot(i_matrix[...], split[:, at], preferred_element_type=jnp.float32)
            slope_i[:, :, at] = out[:rows].reshape(4, length, piece)
            bend_i[:, :, at] = out[rows:].reshape(3, length, piece)

    def along_k():
        count = 3 * length
        parts = []
        for step in range(chunks):
            at = slice(step * chunk, (step + 1) * chunk)
            parts.append(jnp.concatenate([split[:rows, at], split[rows:, at]], axis=1))
        velocity = jnp.concatenate([part[:count] for part in parts], axis=0)
        pressure = jnp.concatenate([part[count:] for part in parts], axis=0)
        slope = jnp.dot(velocity, k_slope_uvw[...], preferred_element_type=jnp.float32)
        bend = jnp.dot(velocity, k_bend[...], preferred_element_type=jnp.float32)
        slope_p = jnp.dot(pressure, k_slope_p[...], preferred_element_type=jnp.float32)
        for step in range(chunks):
            at = slice(step * chunk, (step + 1) * chunk)
            slope_k[:3, :, at] = slope[step * count:(step + 1) * count].reshape(3, length, chunk)
            bend_k[:, :, at] = bend[step * count:(step + 1) * count].reshape(3, length, chunk)
            slope_k[3, :, at] = slope_p[step * length:(step + 1) * length]

    def chain_copies(kind):
        if kind == 0:
            low, high = first.at[:, 0:2, inner], first.at[:, length - 2:length, inner]
        else:
            source = end_rows if kind == 1 else delta_out
            low, high = source.at[:, 0:2], source.at[:, 6:8]
        target = delta_in if kind == 2 else ghost_rows.at[kind]
        to_before = pltpu.make_async_remote_copy(
            low, target.at[:, 6:8], chain_send.at[kind, 0], chain_recv.at[kind, 0],
            device_id={"blk": before}, device_id_type=MESH)
        to_after = pltpu.make_async_remote_copy(
            high, target.at[:, 0:2], chain_send.at[kind, 1], chain_recv.at[kind, 1],
            device_id={"blk": after}, device_id_type=MESH)
        return to_before, to_after

    def face_copies(kind):
        used = pl.ds(0, 3 * length if kind == 1 else rows)
        return [pltpu.make_async_remote_copy(
            face_out.at[kind, used], face_in.at[kind, offset - 1, used], face_send.at[kind, offset - 1],
            face_recv.at[kind, offset - 1], device_id={"seg": to_seg(offset)}, device_id_type=MESH)
            for offset in order]

    def start_faces(kind):
        for copy in face_copies(kind):
            copy.start()

    def await_faces(kind):
        for copy in face_copies(kind):
            copy.wait_recv()

    def start_chain(kind):
        to_before, to_after = chain_copies(kind)

        @pl.when(has_before)
        def _():
            to_before.start()

        @pl.when(has_after)
        def _():
            to_after.start()

    def open_ends(padded, turn):
        @pl.when(jnp.logical_not(has_before))
        def _():
            for c in range(4):
                ghost_rows[turn, c, 0:1, :] = -WALL[c] * padded[c, 1:2, inner]
                ghost_rows[turn, c, 1:2, :] = -WALL[c] * padded[c, 0:1, inner]

        @pl.when(jnp.logical_not(has_after))
        def _():
            for c in range(4):
                ghost_rows[turn, c, 6:7, :] = -WALL[c] * padded[c, length - 1:length, inner]
                ghost_rows[turn, c, 7:8, :] = -WALL[c] * padded[c, length - 2:length - 1, inner]

    def await_chain(kind):
        to_before, to_after = chain_copies(kind)

        @pl.when(has_before)
        def _():
            to_after.wait_recv()

        @pl.when(has_after)
        def _():
            to_before.wait_recv()

    def sent_chain(kind):
        to_before, to_after = chain_copies(kind)

        @pl.when(has_before)
        def _():
            to_before.wait_send()

        @pl.when(has_after)
        def _():
            to_after.wait_send()

    lane = lax.broadcasted_iota(jnp.int32, (length, chunk), 1)

    def central(minus2, minus1, plus1, plus2, bent):
        slope = (minus2 - plus2) + 8.0 * (plus1 - minus1)
        return slope, 16.0 * (minus1 + plus1) - (minus2 + plus2) if bent else None

    def along_j(wide, value, wall, is_first, is_last, bent):
        def moved(step):
            if step > 0:
                return pltpu.roll(wide[:, :LANES + chunk], step, 1)[:, LANES:]
            return pltpu.roll(wide[:, LANES:], LANES + chunk + step, 1)[:, :chunk]
        minus2, minus1, plus1, plus2 = moved(2 * cross), moved(cross), moved(-cross), moved(-2 * cross)
        m1, m2, p1, p2 = minus1, minus2, plus1, plus2
        if is_first:
            m1 = jnp.where(lane < cross, wall * value, minus1)
            m2 = jnp.where(lane < cross, wall * plus1, jnp.where(lane < 2 * cross, wall * minus1, minus2))
        if is_last:
            p1 = jnp.where(lane >= chunk - cross, wall * value, plus1)
            p2 = jnp.where(lane >= chunk - cross, wall * minus1,
                           jnp.where(lane >= chunk - 2 * cross, wall * plus1, plus2))
        return central(m2, m1, p1, p2, bent)

    def inside_rates(padded, fresh, finish):
        def at_chunk(start, is_first, is_last):
            at = pl.ds(start, chunk)
            wide = [padded[c, :, pl.ds(start, chunk + 2 * LANES)] for c in range(4)]
            values = [w[:, LANES:LANES + chunk] for w in wide]
            sums, total = None, None
            for direction in range(3):
                metric = [geometry[3 * direction + b, :, at] for b in range(3)]
                if direction == 1:
                    slopes, bends = [], []
                    for c in range(4):
                        slope, bend = along_j(wide[c], values[c], WALL[c], is_first, is_last, c < 3)
                        slopes.append(slope)
                        bends.append(bend)
                else:
                    slope_ref, bend_ref = (slope_i, bend_i) if direction == 0 else (slope_k, bend_k)
                    slopes = [slope_ref[c, :, at] for c in range(4)]
                    bends = [bend_ref[c, :, at] for c in range(3)]
                if fresh:
                    norm = viscosity * (metric[0] * metric[0] + metric[1] * metric[1] + metric[2] * metric[2])
                    norms[direction, :, at] = norm
                    total = norm if total is None else total + norm
                else:
                    norm = norms[direction, :, at]
                carried = metric[0] * values[0] + metric[1] * values[1] + metric[2] * values[2]
                parts = [norm * bends[c] - carried * slopes[c] - metric[c] * slopes[3] for c in range(3)]
                parts.append(metric[0] * slopes[0] + metric[1] * slopes[1] + metric[2] * slopes[2])
                sums = parts if sums is None else [a + b for a, b in zip(sums, parts)]
            if fresh:
                total = 30.0 * total
                norms[3, :, at] = total
            else:
                total = norms[3, :, at]
            for c in range(4):
                finish(c, start, values[c], sums[c] - total * values[c] if c < 3 else sums[c])

        at_chunk(0, True, chunks == 1)
        if chunks > 2:
            for step in range(1, chunks - 1):
                at_chunk(step * chunk, False, False)
        if chunks > 1:
            at_chunk((chunks - 1) * chunk, False, True)

    sub = lax.broadcasted_iota(jnp.int32, (8, chunk), 0)
    near_row = jnp.where(jnp.logical_or(sub == 0, sub == 7), 1.0, 0.0)
    row_sign = jnp.where(sub < 4, 1.0, -1.0)

    def chain_rates(padded, turn, scale, read, write, keep=None):
        for step in range(chunks):
            start = step * chunk
            at = pl.ds(start, chunk)

            def ends(low, high):
                return jnp.where(sub < 4, low, high)

            inside = pl.ds(start + LANES, chunk)
            values = [ends(padded[c, :8, inside], padded[c, length - 8:, inside]) for c in range(3)]
            metric = [ends(geometry[b, :8, at], geometry[b, length - 8:, at]) for b in range(3)]
            moved = [ghost_rows[turn, c, :, at] for c in range(4)]
            ghosts = [ends(pltpu.roll(m, 7, 0), pltpu.roll(m, 1, 0)) for m in moved]
            sums = ghost_rates(near_row, ghost_terms(scale, row_sign, near_row, metric, values), ghosts, moved)
            low, high = pl.ds(0, 8), pl.ds(length - 8, 8)
            for c in range(4):
                low_new = read(c, low, start) + jnp.where(sub < 2, sums[c], 0.0)
                high_new = read(c, high, start) + jnp.where(sub >= 6, sums[c], 0.0)
                write(c, low, start, low_new)
                write(c, high, start, high_new)
                if keep is not None:
                    keep[c, :, at] = ends(low_new, high_new)

    def at_part(value, c):
        return value[c * length:(c + 1) * length]

    def terms_of(scale, sign, metric, own):
        return ghost_terms(scale, sign, near_lane, [at_part(metric, b) for b in range(3)],
                           [at_part(own, b) for b in range(3)])

    def prepare_terms(scale, metric, own):
        edge, outer, pull = terms_of(scale, face_sign, metric, own)
        terms_ref[0] = edge
        terms_ref[1] = outer
        for b in range(3):
            terms_ref[2 + b] = pull[b]

    def own_terms():
        return terms_ref[0], terms_ref[1], [terms_ref[2 + b] for b in range(3)]

    def received(kind, count):
        value = face_in[kind, order[-1] - 1, :count]
        for offset in order[:-1]:
            value = jnp.where(comes_from[offset], face_in[kind, offset - 1, :count], value)
        return value

    def face_rates(terms, theirs, own):
        ghosts = [at_part(theirs, c) - WALL[c] * at_part(own, c) for c in range(4)]
        moved = [pltpu.roll(g, HALF, 1) for g in ghosts]
        return jnp.concatenate(ghost_rates(near_lane, terms, ghosts, moved), axis=0)

    def inside_second(start, size):
        return pl.ds(start + LANES if isinstance(start, int) else pl.multiple_of(start + LANES, LANES), size)

    step_one, step_two = time_step / 12.0, 0.5 * time_step / 12.0

    factor = (1.0, 1.0, 1.0, -compress)

    def finish_first(c, start, value, rate):
        second[c, :, inside_second(start, chunk)] = value + (step_one * factor[c]) * rate

    def finish_second(c, start, value, rate):
        base = first[c, :, inside_second(start, chunk)]
        out_ref[c, :, pl.ds(start, chunk)] = 0.5 * (base + value) + (step_two * factor[c]) * rate

    def read_second(c, which, start):
        return second[c, which, inside_second(start, chunk)]

    def write_second(c, which, start, value):
        second[c, which, inside_second(start, chunk)] = value

    def read_out(c, which, start):
        return out_ref[c, which, pl.ds(start, chunk)]

    def write_out(c, which, start, value):
        out_ref[c, which, pl.ds(start, chunk)] = value

    def tile_second(c, start):
        return second[c, :, start + LANES:start + 2 * LANES]

    def put_second(c, start, value):
        second[c, :, start + LANES:start + 2 * LANES] = value

    def tile_out(c, start):
        return out_ref[c, :, start:start + LANES]

    def put_out(c, start, value):
        out_ref[c, :, start:start + LANES] = value

    load_state.wait()
    face_out[0] = gather_face(first, False)
    pl.semaphore_wait(barrier, segs - 1 + has_before.astype(jnp.int32) + has_after.astype(jnp.int32))
    start_faces(0)
    start_chain(0)

    load_metric.wait()
    valid = jnp.where(jnp.logical_and(in_face, any_join), 1.0, 0.0)
    own_metric = valid * gather_metric()
    face_out[1, :3 * length] = own_metric
    start_faces(1)
    open_ends(first, 0)
    build_faces()
    build_delta()
    prepare_terms(step_one, own_metric, face_out[0])
    split_up(first[:, :, inner].reshape(rows, width), split)
    along_i()
    along_k()
    inside_rates(first, True, finish_first)

    await_chain(0)
    chain_rates(first, 0, step_one, read_second, write_second, end_rows)
    start_chain(1)
    face_out[2] = gather_face(second, False)
    start_faces(2)

    turned_ref[...] = flipped(face_out[0])
    await_faces(0)
    added = face_rates(own_terms(), flipped(received(0, rows)), face_out[0])
    for c in range(4):
        delta_out[c] = jnp.where(lax.broadcasted_iota(jnp.int32, (8, LANES), 0) < 4,
                                 added[c * length:c * length + 8], added[(c + 1) * length - 8:(c + 1) * length])
    start_chain(2)
    added_ref[...] = face_out[2] + added
    spread_face(added, tile_second, put_second)
    open_ends(second, 1)
    split_up(second[:, :, inner].reshape(rows, width), split)
    along_i()
    along_k()
    inside_rates(second, False, finish_second)
    prepare_terms(step_two, face_out[1, :3 * length], added_ref[...])
    await_faces(1)
    their_face = received(0, rows)
    their_terms = terms_of(step_one, partner_sign, received(1, 3 * length), their_face)
    theirs_ref[...] = face_rates(their_terms, turned_ref[...], their_face)

    await_chain(1)
    await_chain(2)
    spread_delta()
    chain_rates(second, 1, step_two, read_out, write_out)
    for kind in range(3):
        for copy in face_copies(kind):
            copy.wait_send()
        sent_chain(kind)
    await_faces(2)
    their_face = flipped(received(2, rows) + theirs_ref[...])
    spread_face(face_rates(own_terms(), their_face, added_ref[...]), tile_out, put_out)


def on_device(state, metric, block_map, links):
    segs, chain = lax.axis_size("seg"), lax.axis_size("blk")
    _, parts, length, width = state.shape
    cross = math.isqrt(width)
    assert cross <= HALF and length == 16
    chunk = math.lcm(cross, LANES)
    links = links.transpose(1, 2, 0)
    f32, bf16, dma = jnp.float32, jnp.bfloat16, pltpu.SemaphoreType.DMA
    result = pl.pallas_call(
        functools.partial(kernel, segs, chain, cross),
        out_shape=pltpu.VMEM((parts, length, width), f32),
        in_specs=[pl.BlockSpec(memory_space=pl.ANY)] * 4,
        out_specs=pl.BlockSpec(memory_space=pltpu.VMEM),
        scratch_shapes=[
            pltpu.VMEM((parts, length, width + 2 * LANES), f32),
            pltpu.VMEM((parts, length, width + 2 * LANES), f32),
            pltpu.VMEM((9, length, width), f32),
            pltpu.VMEM((width // LANES, 8, LANES), jnp.int32),
            pltpu.VMEM((width // LANES, 8, LANES), f32),
            pltpu.VMEM((width // LANES, 8, LANES), jnp.int32),
            pltpu.VMEM((width // LANES, 8, LANES), f32),
            pltpu.VMEM((width - width // LANES // 4 * 2 * LANES, LANES), bf16),
            pltpu.VMEM((2 * parts * length, width), bf16),
            pltpu.VMEM((2 * chunk, chunk), bf16),
            pltpu.VMEM((2 * chunk, chunk), bf16),
            pltpu.VMEM((2 * chunk, chunk), bf16),
            pltpu.VMEM((7 * length, LANES), bf16),
            pltpu.VMEM((parts, length, width), f32),
            pltpu.VMEM((parts - 1, length, width), f32),
            pltpu.VMEM((parts, length, width), f32),
            pltpu.VMEM((parts - 1, length, width), f32),
            pltpu.VMEM((parts, length, width), f32),
            pltpu.VMEM((5, length, LANES), f32),
            pltpu.VMEM((parts * length, LANES), f32),
            pltpu.VMEM((parts * length, LANES), f32),
            pltpu.VMEM((parts * length, LANES), f32),
            pltpu.VMEM((2, parts, 8, width), f32),
            pltpu.VMEM((parts, 8, width), f32),
            pltpu.VMEM((parts, 8, LANES), f32),
            pltpu.VMEM((parts, 8, LANES), f32),
            pltpu.VMEM((3, parts * length, LANES), f32),
            pltpu.VMEM((3, segs - 1, parts * length, LANES), f32),
            pltpu.SMEM(block_map.shape, jnp.int32),
            pltpu.SMEM(links.shape, jnp.int32),
            dma((4,)), dma((3, 2)), dma((3, 2)), dma((3, segs - 1)), dma((3, segs - 1)),
        ],
        compiler_params=pltpu.CompilerParams(collective_id=0, has_side_effects=True),
    )(state, metric, block_map, links)
    return result.reshape(state.shape)


def solution(mesh):
    in_specs = (P(("seg", "blk"), None, None, None), P(("seg", "blk"), None, None, None), P(), P())
    out_specs = P(("seg", "blk"), None, None, None)
    return jax.shard_map(
        on_device, mesh=mesh, in_specs=in_specs, out_specs=out_specs, check_vma=False
    )
```

```python
import functools
import math

import jax
import jax.numpy as jnp
from jax import lax
from jax.experimental import pallas as pl
from jax.experimental.pallas import tpu as pltpu
from jax.sharding import PartitionSpec as P

time_step = 0.05
viscosity = 0.2
compress = 1.0
MESH = pl.DeviceIdType.MESH
LANES = 128
HALF = LANES // 2
WALL = (-1.0, -1.0, -1.0, 1.0)


def split_index(index, size, count):
    quotient = jnp.zeros_like(index)
    for step in range(1, count):
        quotient += (index >= size * step).astype(jnp.int32)
    return quotient, index - size * quotient


def take(value, index, axis):
    numbers = lax.GatherDimensionNumbers(
        offset_dims=(), collapsed_slice_dims=(axis,), start_index_map=(axis,),
        operand_batching_dims=(1 - axis,), start_indices_batching_dims=(1 - axis,))
    return lax.gather(value, index[..., None], numbers, slice_sizes=(1, 1),
                      mode=lax.GatherScatterMode.PROMISE_IN_BOUNDS)


def flipped_bits(index, bits):
    bit = 1
    while bit <= bits:
        if bits & bit:
            index = index + bit - 2 * bit * lax.rem(lax.div(index, bit), 2)
        bit *= 2
    return index


def halves(value):
    lead = value.astype(jnp.bfloat16)
    return lead, (value - lead.astype(jnp.float32)).astype(jnp.bfloat16)


def select(flag, yes, no):
    return jnp.where(flag, yes, no)


def ghost_terms(scale, sign, near, metric, values):
    carried = sign * (metric[0] * values[0] + metric[1] * values[1] + metric[2] * values[2])
    norm = viscosity * (metric[0] * metric[0] + metric[1] * metric[1] + metric[2] * metric[2])
    edge = (8.0 * scale) * (2.0 * norm + carried) * near
    outer = scale * (norm + carried)
    return edge, outer, [(scale * sign) * m for m in metric]


def ghost_rates(near, terms, ghosts, moved):
    edge, outer, pull = terms
    eight = 8.0 * near
    slopes = [m - eight * g for g, m in zip(ghosts, moved)]
    parts = [edge * ghosts[c] - outer * moved[c] - pull[c] * slopes[3] for c in range(3)]
    parts.append(-compress * (pull[0] * slopes[0] + pull[1] * slopes[1] + pull[2] * slopes[2]))
    return parts


def kernel(segs, chain, cross, state_hbm, metric_hbm, block_map_hbm, links_hbm, out_ref,
           first, second, geometry, face_index, face_mask, delta_index, delta_mask, face_hot, split,
           k_slope_uvw, k_slope_p, k_bend, i_matrix, slope_k, bend_k, slope_i, bend_i, norms,
           terms_ref, added_ref, theirs_ref, turned_ref,
           ghost_rows, end_rows, delta_out, delta_in, face_out, face_in, block_map, links,
           load_sem, chain_send, chain_recv, face_send, face_recv):
    length, width = out_ref.shape[1], out_ref.shape[2]
    rows = 4 * length
    chunk = math.lcm(cross, LANES)
    chunks = width // chunk
    inner = pl.ds(LANES, width)
    seg, pos = lax.axis_index("seg"), lax.axis_index("blk")
    me = seg * chain + pos
    has_before, has_after = pos > 0, pos < chain - 1
    before, after = lax.rem(pos + chain - 1, chain), lax.rem(pos + 1, chain)
    paired = segs & (segs - 1) == 0
    order = range(segs - 1, 0, -1)

    def to_seg(offset):
        return flipped_bits(seg, offset) if paired else lax.rem(seg + offset, segs)

    def from_seg(offset):
        return flipped_bits(seg, offset) if paired else lax.rem(seg + segs - offset, segs)

    barrier = pltpu.get_barrier_semaphore()
    for offset in order:
        pl.semaphore_signal(barrier, inc=1, device_id={"seg": to_seg(offset)}, device_id_type=MESH)

    @pl.when(has_before)
    def _():
        pl.semaphore_signal(barrier, inc=1, device_id={"blk": before}, device_id_type=MESH)

    @pl.when(has_after)
    def _():
        pl.semaphore_signal(barrier, inc=1, device_id={"blk": after}, device_id_type=MESH)

    load_map = pltpu.make_async_copy(block_map_hbm, block_map, load_sem.at[2])
    load_links = pltpu.make_async_copy(links_hbm, links, load_sem.at[3])
    load_state = pltpu.make_async_copy(state_hbm.at[0], first.at[:, :, inner], load_sem.at[0])
    load_metric = pltpu.make_async_copy(metric_hbm.at[0], geometry, load_sem.at[1])
    load_map.start()
    load_links.start()
    load_state.start()
    load_metric.start()

    lane_row = lax.broadcasted_iota(jnp.int32, (1, LANES), 1)
    face_layer = (lane_row >= HALF).astype(jnp.int32)
    face_place = lane_row - HALF * face_layer
    in_face = face_place < cross
    near_lane = (lane_row < HALF).astype(jnp.float32)

    def build_k():
        here = lax.broadcasted_iota(jnp.int32, (cross, LANES), 0)
        column = lax.broadcasted_iota(jnp.int32, (cross, LANES), 1)
        for group in range(chunk // cross):
            first_row = group * cross
            for tile in range(chunk // LANES):
                lanes = slice(tile * LANES, (tile + 1) * LANES)
                if not first_row // LANES <= tile <= (first_row + cross - 1) // LANES:
                    for matrix in (k_slope_uvw, k_slope_p, k_bend):
                        for top in (first_row, chunk + first_row):
                            matrix[top:top + cross, lanes] = jnp.zeros((cross, LANES), jnp.bfloat16)
                    continue
                there = column + (tile * LANES - first_row)
                there = jnp.where(jnp.logical_and(there >= 0, there < cross), there, 4 * width)
                offset, mirrored = here - there, here + there

                def at(index, value, factor):
                    return jnp.where(index == value, factor, 0.0)

                slope = at(offset, -2, 1.0) + at(offset, -1, -8.0) + at(offset, 1, 8.0) + at(offset, 2, -1.0)
                bend = at(offset, -2, -1.0) + at(offset, -1, 16.0) + at(offset, 1, 16.0) + at(offset, 2, -1.0)
                end = 2 * cross - 2
                wall_slope = (at(mirrored, 0, -8.0) + at(mirrored, 1, 1.0)
                              + at(mirrored, end, 8.0) + at(mirrored, end - 1, -1.0))
                wall_bend = (at(mirrored, 0, 16.0) + at(mirrored, 1, -1.0)
                             + at(mirrored, end, 16.0) + at(mirrored, end - 1, -1.0))
                for matrix, value in ((k_slope_uvw, slope + WALL[0] * wall_slope),
                                      (k_slope_p, slope + WALL[3] * wall_slope),
                                      (k_bend, bend + WALL[0] * wall_bend)):
                    value = value.astype(jnp.bfloat16)
                    matrix[first_row:first_row + cross, lanes] = value
                    matrix[chunk + first_row:chunk + first_row + cross, lanes] = value

    pads = jnp.zeros((4, length, LANES), jnp.float32)
    for padded in (first, second):
        padded[:, :, :LANES] = pads
        padded[:, :, LANES + width:] = pads
    build_k()

    def build_i():
        count = 7 * length
        term, here = split_index(lax.broadcasted_iota(jnp.int32, (count, LANES), 0), length, 7)
        part, there = split_index(lax.broadcasted_iota(jnp.int32, (count, LANES), 1), length, 8)
        part = jnp.where(part >= 4, part - 4, part)
        offset = there - here

        def at(index, factor):
            return jnp.where(offset == index, factor, 0.0)

        slope = at(-2, 1.0) + at(-1, -8.0) + at(1, 8.0) + at(2, -1.0)
        bend = at(-2, -1.0) + at(-1, 16.0) + at(1, 16.0) + at(2, -1.0)
        value = jnp.where(term == part, slope, jnp.where(term == part + 4, bend, 0.0))
        i_matrix[...] = value.astype(jnp.bfloat16)

    build_i()

    load_map.wait()
    load_links.wait()
    block = block_map[me]

    def joined_side(number):
        return [links[2 + side, 0, number] >= 0 for side in range(4)]

    joins = joined_side(block)
    partner, partner_face = jnp.int32(-1), jnp.int32(0)
    flip_along, flip_across = jnp.int32(0), jnp.int32(0)
    for side in range(4):
        partner = select(joins[side], links[2 + side, 0, block], partner)
        partner_face = select(joins[side], links[2 + side, 1, block], partner_face)
        flip_along = select(joins[side], links[2 + side, 2, block], flip_along)
        flip_across = select(joins[side], links[2 + side, 3, block], flip_across)
    any_join = partner >= 0
    on_first = jnp.logical_or(joins[0], joins[1])
    on_second = jnp.logical_or(joins[2], joins[3])
    on_high = jnp.logical_or(joins[1], joins[3])
    joins_before = joined_side(block_map[seg * chain + before])
    joins_after = joined_side(block_map[seg * chain + after])
    comes_from = {offset: block_map[from_seg(offset) * chain + pos] == partner for offset in order}
    face_sign = select(on_high, -1.0, 1.0)
    partner_sign = select(jnp.logical_or(partner_face == 3, partner_face == 5), -1.0, 1.0)

    lane_of = lax.broadcasted_iota(jnp.int32, (8, LANES), 1)
    row_in = lax.broadcasted_iota(jnp.int32, (8, LANES), 0)
    layer_of = (lane_of >= HALF).astype(jnp.int32)
    place_of = lane_of - HALF * layer_of
    face_lane = place_of < cross

    tiles = width // LANES
    split_tile = tiles // 6 * 2

    def spread_index(tile, high):
        start = tile * LANES
        row = start // cross
        spot = lane_of + (start - row * cross)
        place = jnp.full((8, LANES), row, jnp.int32)
        for step in range(1, LANES // cross + 2):
            past = spot >= step * cross
            place = place + past.astype(jnp.int32)
        spot = lane_of + start - place * cross
        layer = jnp.where(high, cross - 1 - spot, spot)
        return jnp.where(layer < 2, place + HALF * layer, -1)

    def build_spread(index_ref, mask_ref, high, used):
        for tile in range(width // LANES):
            index = jnp.where(used, spread_index(tile, high), -1)
            mask_ref[tile] = jnp.where(index >= 0, 1.0, 0.0)
            index_ref[tile] = jnp.maximum(index, 0)

    def build_faces():
        build_spread(face_index, face_mask, jnp.full((8, LANES), select(on_high, 1, 0)) > 0,
                     jnp.full((8, LANES), select(on_second, 1, 0)) > 0)

        cells = lax.broadcasted_iota(jnp.int32, (2 * LANES, LANES), 0)
        source = jnp.where(face_lane, source_of, -1)[0:1]
        source = source - (1 - select(on_second, 1, 0)) * (2 * width)
        for piece in range((tiles - split_tile) // 2):
            start = (split_tile + 2 * piece) * LANES
            hit = (cells == source - start).astype(jnp.float32).astype(jnp.bfloat16)
            face_hot[piece * 2 * LANES:(piece + 1) * 2 * LANES, :] = hit

    def build_delta():
        def chosen(sides):
            flags = [select(jnp.logical_or(near_joins[sides[0]], near_joins[sides[1]]), 1, 0)
                     for near_joins in (joins_before, joins_after)]
            return jnp.where(row_in < 4, flags[0], flags[1]) > 0

        build_spread(delta_index, delta_mask, chosen((1, 3)), chosen((2, 3)))

    source_of = jnp.where(face_lane, place_of, 0) * cross + select(on_high, cross - 1 - layer_of, layer_of)
    source_tile, source_lane = split_index(source_of, LANES, width // LANES)
    flip_rows = select(flip_along == 1, 7 - row_in, row_in)
    flip_lanes = jnp.where(face_lane, layer_of * HALF + select(flip_across == 1, cross - 1 - place_of, place_of), lane_of)

    def by_rows(value, function):
        return jnp.concatenate([function(value[at:at + 8]) for at in range(0, value.shape[0], 8)], axis=0)

    def flipped(value):
        parts = []
        for at in range(0, value.shape[0], length):
            low, high = value[at:at + 8], value[at + 8:at + 16]
            for half in (select(flip_along == 1, high, low), select(flip_along == 1, low, high)):
                parts.append(take(take(half, flip_rows, 0), flip_lanes, 1))
        return jnp.concatenate(parts, axis=0)

    def split_up(value, into):
        count = value.shape[0]
        lead, trail = halves(value)
        into[:count] = lead
        into[count:2 * count] = trail

    def gathered(low, high, tile_of, rest=None):
        packed = None if rest is None else rest
        for tile in range(tiles if rest is None else split_tile):
            part = by_rows(tile_of(tile), lambda x: take(x, source_lane, 1))
            here = jnp.concatenate([source_tile == tile] * (part.shape[0] // 8), axis=0)
            packed = part if packed is None else jnp.where(here, part, packed)
        near, far = LANES - cross, LANES - 2 * cross
        lower = jnp.where(lane_row < HALF, low, pltpu.roll(low, HALF - cross, 1))
        upper = jnp.where(lane_row < HALF, pltpu.roll(high, LANES - near, 1), pltpu.roll(high, HALF - far, 1))
        return jnp.where(on_first, jnp.where(on_high, upper, lower), packed)

    def gather_face(padded, shared):
        def tile_of(tile):
            start = LANES + tile * LANES
            return padded[:, :, start:start + LANES].reshape(rows, LANES)

        if not shared:
            return gathered(tile_of(0), tile_of(tiles - 1), tile_of)
        value = padded[:, :, LANES + split_tile * LANES:LANES + width].reshape(rows, (tiles - split_tile) * LANES)
        both = jnp.concatenate(halves(value), axis=0)
        rest = jnp.dot(both, face_hot[...], preferred_element_type=jnp.float32)
        return gathered(tile_of(0), tile_of(tiles - 1), tile_of, rest[:rows] + rest[rows:])

    def gather_metric():
        def tile_of(tile, base=6):
            return geometry[base:base + 3, :, tile * LANES:(tile + 1) * LANES].reshape(3 * length, LANES)

        return gathered(tile_of(0, 3), tile_of(width // LANES - 1, 3), tile_of)

    near, far = LANES - cross, LANES - 2 * cross

    def to_lower(value):
        return jnp.where(lane_row < cross, value, pltpu.roll(value, LANES - (HALF - cross), 1))

    def to_upper(value):
        return jnp.where(lane_row >= near, pltpu.roll(value, near, 1), pltpu.roll(value, LANES - (HALF - far), 1))

    def spread(value, index_ref, mask_ref, lower, upper, write, shared):
        last = split_tile if shared else tiles
        if shared:
            both = jnp.concatenate(halves(value), axis=0)
            for piece in range((tiles - last) // 2):
                add = lax.dot_general(both, face_hot[piece * 2 * LANES:(piece + 1) * 2 * LANES, :],
                                      (((1,), (1,)), ((), ())), preferred_element_type=jnp.float32)
                add = add[:rows] + add[rows:]
                for side in range(2):
                    tile = last + 2 * piece + side
                    part = add[:, side * LANES:(side + 1) * LANES]
                    write(tile * LANES, part + upper if tile == tiles - 1 else part)
        for tile in range(last):
            index, mask = index_ref[tile], mask_ref[tile]
            add = by_rows(value, lambda x: take(x, index, 1) * mask)
            if tile == 0:
                add = add + lower
            if tile == width // LANES - 1:
                add = add + upper
            write(tile * LANES, add)

    def spread_face(value, read, write):
        on_low = jnp.logical_not(on_high)
        lower = jnp.where(jnp.logical_and(lane_row < 2 * cross, jnp.logical_and(on_first, on_low)), to_lower(value), 0.0)
        upper = jnp.where(jnp.logical_and(lane_row >= far, jnp.logical_and(on_first, on_high)), to_upper(value), 0.0)

        def put(start, add):
            for c in range(4):
                write(c, start, read(c, start) + add[c * length:(c + 1) * length])

        spread(value, face_index, face_mask, lower, upper, put, True)

    def spread_delta():
        end_row = lax.broadcasted_iota(jnp.int32, (8, LANES), 0)
        wanted = jnp.logical_or(jnp.logical_and(end_row < 2, has_before), jnp.logical_and(end_row >= 6, has_after))
        value = jnp.concatenate([jnp.where(wanted, delta_in[c], 0.0) for c in range(4)], axis=0)

        def mask(side):
            flag = [select(flags[side], 1.0, 0.0) for flags in (joins_before, joins_after)]
            one = jnp.where(end_row < 4, flag[0], flag[1])
            return jnp.concatenate([one] * 4, axis=0)

        lower = jnp.where(lane_row < 2 * cross, to_lower(value) * mask(0), 0.0)
        upper = jnp.where(lane_row >= far, to_upper(value) * mask(1), 0.0)
        def put(start, add):
            for c in range(4):
                at = slice(start, start + LANES)
                ghost_rows[1, c, :, at] = ghost_rows[1, c, :, at] + add[c * 8:(c + 1) * 8]

        spread(value, delta_index, delta_mask, lower, upper, put, False)

    def along_i():
        piece = 2 * LANES
        for part in range(width // piece):
            at = slice(part * piece, (part + 1) * piece)
            out = jnp.dot(i_matrix[...], split[:, at], preferred_element_type=jnp.float32)
            slope_i[:, :, at] = out[:rows].reshape(4, length, piece)
            bend_i[:, :, at] = out[rows:].reshape(3, length, piece)

    def along_k():
        count = 3 * length
        parts = []
        for step in range(chunks):
            at = slice(step * chunk, (step + 1) * chunk)
            parts.append(jnp.concatenate([split[:rows, at], split[rows:, at]], axis=1))
        velocity = jnp.concatenate([part[:count] for part in parts], axis=0)
        pressure = jnp.concatenate([part[count:] for part in parts], axis=0)
        slope = jnp.dot(velocity, k_slope_uvw[...], preferred_element_type=jnp.float32)
        bend = jnp.dot(velocity, k_bend[...], preferred_element_type=jnp.float32)
        slope_p = jnp.dot(pressure, k_slope_p[...], preferred_element_type=jnp.float32)
        for step in range(chunks):
            at = slice(step * chunk, (step + 1) * chunk)
            slope_k[:3, :, at] = slope[step * count:(step + 1) * count].reshape(3, length, chunk)
            bend_k[:, :, at] = bend[step * count:(step + 1) * count].reshape(3, length, chunk)
            slope_k[3, :, at] = slope_p[step * length:(step + 1) * length]

    def chain_copies(kind):
        if kind == 0:
            low, high = first.at[:, 0:2, inner], first.at[:, length - 2:length, inner]
        else:
            source = end_rows if kind == 1 else delta_out
            low, high = source.at[:, 0:2], source.at[:, 6:8]
        target = delta_in if kind == 2 else ghost_rows.at[kind]
        to_before = pltpu.make_async_remote_copy(
            low, target.at[:, 6:8], chain_send.at[kind, 0], chain_recv.at[kind, 0],
            device_id={"blk": before}, device_id_type=MESH)
        to_after = pltpu.make_async_remote_copy(
            high, target.at[:, 0:2], chain_send.at[kind, 1], chain_recv.at[kind, 1],
            device_id={"blk": after}, device_id_type=MESH)
        return to_before, to_after

    def face_copies(kind):
        used = pl.ds(0, 3 * length if kind == 1 else rows)
        return [pltpu.make_async_remote_copy(
            face_out.at[kind, used], face_in.at[kind, offset - 1, used], face_send.at[kind, offset - 1],
            face_recv.at[kind, offset - 1], device_id={"seg": to_seg(offset)}, device_id_type=MESH)
            for offset in order]

    def start_faces(kind):
        for copy in face_copies(kind):
            copy.start()

    def await_faces(kind):
        for copy in face_copies(kind):
            copy.wait_recv()

    def start_chain(kind):
        to_before, to_after = chain_copies(kind)

        @pl.when(has_before)
        def _():
            to_before.start()

        @pl.when(has_after)
        def _():
            to_after.start()

    def open_ends(padded, turn):
        @pl.when(jnp.logical_not(has_before))
        def _():
            for c in range(4):
                ghost_rows[turn, c, 0:1, :] = -WALL[c] * padded[c, 1:2, inner]
                ghost_rows[turn, c, 1:2, :] = -WALL[c] * padded[c, 0:1, inner]

        @pl.when(jnp.logical_not(has_after))
        def _():
            for c in range(4):
                ghost_rows[turn, c, 6:7, :] = -WALL[c] * padded[c, length - 1:length, inner]
                ghost_rows[turn, c, 7:8, :] = -WALL[c] * padded[c, length - 2:length - 1, inner]

    def await_chain(kind):
        to_before, to_after = chain_copies(kind)

        @pl.when(has_before)
        def _():
            to_after.wait_recv()

        @pl.when(has_after)
        def _():
            to_before.wait_recv()

    def sent_chain(kind):
        to_before, to_after = chain_copies(kind)

        @pl.when(has_before)
        def _():
            to_before.wait_send()

        @pl.when(has_after)
        def _():
            to_after.wait_send()

    lane = lax.broadcasted_iota(jnp.int32, (length, chunk), 1)

    def central(minus2, minus1, plus1, plus2, bent):
        slope = (minus2 - plus2) + 8.0 * (plus1 - minus1)
        return slope, 16.0 * (minus1 + plus1) - (minus2 + plus2) if bent else None

    def along_j(wide, value, wall, is_first, is_last, bent):
        def moved(step):
            if step > 0:
                return pltpu.roll(wide[:, :LANES + chunk], step, 1)[:, LANES:]
            return pltpu.roll(wide[:, LANES:], LANES + chunk + step, 1)[:, :chunk]
        minus2, minus1, plus1, plus2 = moved(2 * cross), moved(cross), moved(-cross), moved(-2 * cross)
        m1, m2, p1, p2 = minus1, minus2, plus1, plus2
        if is_first:
            m1 = jnp.where(lane < cross, wall * value, minus1)
            m2 = jnp.where(lane < cross, wall * plus1, jnp.where(lane < 2 * cross, wall * minus1, minus2))
        if is_last:
            p1 = jnp.where(lane >= chunk - cross, wall * value, plus1)
            p2 = jnp.where(lane >= chunk - cross, wall * minus1,
                           jnp.where(lane >= chunk - 2 * cross, wall * plus1, plus2))
        return central(m2, m1, p1, p2, bent)

    def inside_rates(padded, fresh, finish):
        def at_chunk(start, is_first, is_last):
            at = pl.ds(start, chunk)
            wide = [padded[c, :, pl.ds(start, chunk + 2 * LANES)] for c in range(4)]
            values = [w[:, LANES:LANES + chunk] for w in wide]
            sums, total = None, None
            for direction in range(3):
                metric = [geometry[3 * direction + b, :, at] for b in range(3)]
                if direction == 1:
                    slopes, bends = [], []
                    for c in range(4):
                        slope, bend = along_j(wide[c], values[c], WALL[c], is_first, is_last, c < 3)
                        slopes.append(slope)
                        bends.append(bend)
                else:
                    slope_ref, bend_ref = (slope_i, bend_i) if direction == 0 else (slope_k, bend_k)
                    slopes = [slope_ref[c, :, at] for c in range(4)]
                    bends = [bend_ref[c, :, at] for c in range(3)]
                if fresh:
                    norm = viscosity * (metric[0] * metric[0] + metric[1] * metric[1] + metric[2] * metric[2])
                    norms[direction, :, at] = norm
                    total = norm if total is None else total + norm
                else:
                    norm = norms[direction, :, at]
                carried = metric[0] * values[0] + metric[1] * values[1] + metric[2] * values[2]
                parts = [norm * bends[c] - carried * slopes[c] - metric[c] * slopes[3] for c in range(3)]
                parts.append(metric[0] * slopes[0] + metric[1] * slopes[1] + metric[2] * slopes[2])
                sums = parts if sums is None else [a + b for a, b in zip(sums, parts)]
            if fresh:
                total = 30.0 * total
                norms[3, :, at] = total
            else:
                total = norms[3, :, at]
            for c in range(4):
                finish(c, start, values[c], sums[c] - total * values[c] if c < 3 else sums[c])

        at_chunk(0, True, chunks == 1)
        if chunks > 2:
            for step in range(1, chunks - 1):
                at_chunk(step * chunk, False, False)
        if chunks > 1:
            at_chunk((chunks - 1) * chunk, False, True)

    sub = lax.broadcasted_iota(jnp.int32, (8, chunk), 0)
    near_row = jnp.where(jnp.logical_or(sub == 0, sub == 7), 1.0, 0.0)
    row_sign = jnp.where(sub < 4, 1.0, -1.0)

    def chain_rates(padded, turn, scale, read, write, keep=None):
        for step in range(chunks):
            start = step * chunk
            at = pl.ds(start, chunk)

            def ends(low, high):
                return jnp.where(sub < 4, low, high)

            inside = pl.ds(start + LANES, chunk)
            values = [ends(padded[c, :8, inside], padded[c, length - 8:, inside]) for c in range(3)]
            metric = [ends(geometry[b, :8, at], geometry[b, length - 8:, at]) for b in range(3)]
            moved = [ghost_rows[turn, c, :, at] for c in range(4)]
            ghosts = [ends(pltpu.roll(m, 7, 0), pltpu.roll(m, 1, 0)) for m in moved]
            sums = ghost_rates(near_row, ghost_terms(scale, row_sign, near_row, metric, values), ghosts, moved)
            low, high = pl.ds(0, 8), pl.ds(length - 8, 8)
            for c in range(4):
                low_new = read(c, low, start) + jnp.where(sub < 2, sums[c], 0.0)
                high_new = read(c, high, start) + jnp.where(sub >= 6, sums[c], 0.0)
                write(c, low, start, low_new)
                write(c, high, start, high_new)
                if keep is not None:
                    keep[c, :, at] = ends(low_new, high_new)

    def at_part(value, c):
        return value[c * length:(c + 1) * length]

    def terms_of(scale, sign, metric, own):
        return ghost_terms(scale, sign, near_lane, [at_part(metric, b) for b in range(3)],
                           [at_part(own, b) for b in range(3)])

    def prepare_terms(scale, metric, own):
        edge, outer, pull = terms_of(scale, face_sign, metric, own)
        terms_ref[0] = edge
        terms_ref[1] = outer
        for b in range(3):
            terms_ref[2 + b] = pull[b]

    def own_terms():
        return terms_ref[0], terms_ref[1], [terms_ref[2 + b] for b in range(3)]

    def received(kind, count):
        value = face_in[kind, order[-1] - 1, :count]
        for offset in order[:-1]:
            value = jnp.where(comes_from[offset], face_in[kind, offset - 1, :count], value)
        return value

    def face_rates(terms, theirs, own=None):
        ghosts = [at_part(theirs, c) for c in range(4)]
        if own is not None:
            ghosts = [g - WALL[c] * at_part(own, c) for c, g in enumerate(ghosts)]
        moved = [pltpu.roll(g, HALF, 1) for g in ghosts]
        return jnp.concatenate(ghost_rates(near_lane, terms, ghosts, moved), axis=0)

    def inside_second(start, size):
        return pl.ds(start + LANES if isinstance(start, int) else pl.multiple_of(start + LANES, LANES), size)

    step_one, step_two = time_step / 12.0, 0.5 * time_step / 12.0

    factor = (1.0, 1.0, 1.0, -compress)

    def finish_first(c, start, value, rate):
        second[c, :, inside_second(start, chunk)] = value + (step_one * factor[c]) * rate

    def finish_second(c, start, value, rate):
        base = first[c, :, inside_second(start, chunk)]
        out_ref[c, :, pl.ds(start, chunk)] = 0.5 * (base + value) + (step_two * factor[c]) * rate

    def read_second(c, which, start):
        return second[c, which, inside_second(start, chunk)]

    def write_second(c, which, start, value):
        second[c, which, inside_second(start, chunk)] = value

    def read_out(c, which, start):
        return out_ref[c, which, pl.ds(start, chunk)]

    def write_out(c, which, start, value):
        out_ref[c, which, pl.ds(start, chunk)] = value

    def tile_second(c, start):
        return second[c, :, start + LANES:start + 2 * LANES]

    def put_second(c, start, value):
        second[c, :, start + LANES:start + 2 * LANES] = value

    def tile_out(c, start):
        return out_ref[c, :, start:start + LANES]

    def put_out(c, start, value):
        out_ref[c, :, start:start + LANES] = value

    load_state.wait()
    face_out[0] = gather_face(first, False)
    pl.semaphore_wait(barrier, segs - 1 + has_before.astype(jnp.int32) + has_after.astype(jnp.int32))
    start_faces(0)
    start_chain(0)

    load_metric.wait()
    valid = jnp.where(jnp.logical_and(in_face, any_join), 1.0, 0.0)
    own_metric = valid * gather_metric()
    face_out[1, :3 * length] = own_metric
    start_faces(1)
    open_ends(first, 0)
    build_faces()
    build_delta()
    prepare_terms(step_one, own_metric, face_out[0])
    split_up(first[:, :, inner].reshape(rows, width), split)
    along_i()
    along_k()
    inside_rates(first, True, finish_first)

    await_chain(0)
    chain_rates(first, 0, step_one, read_second, write_second, end_rows)
    start_chain(1)
    face_out[2] = gather_face(second, False)
    start_faces(2)

    await_faces(0)
    added = face_rates(own_terms(), flipped(received(0, rows)), face_out[0])
    for c in range(4):
        delta_out[c] = jnp.where(lax.broadcasted_iota(jnp.int32, (8, LANES), 0) < 4,
                                 added[c * length:c * length + 8], added[(c + 1) * length - 8:(c + 1) * length])
    start_chain(2)
    added_ref[...] = face_out[2] + added
    spread_face(added, tile_second, put_second)
    open_ends(second, 1)
    split_up(second[:, :, inner].reshape(rows, width), split)
    along_i()
    along_k()
    inside_rates(second, False, finish_second)
    prepare_terms(step_two, face_out[1, :3 * length], added_ref[...])
    await_faces(1)
    their_face = received(0, rows)
    their_terms = terms_of(step_one, partner_sign, received(1, 3 * length), their_face)
    theirs = flipped(face_rates(their_terms, flipped(face_out[0]), their_face))
    for c in range(4):
        theirs_ref[c * length:(c + 1) * length] = at_part(theirs, c) - WALL[c] * at_part(added_ref[...], c)

    await_chain(1)
    await_chain(2)
    spread_delta()
    chain_rates(second, 1, step_two, read_out, write_out)
    for kind in range(3):
        for copy in face_copies(kind):
            copy.wait_send()
        sent_chain(kind)
    await_faces(2)
    their_face = flipped(received(2, rows)) + theirs_ref[...]
    spread_face(face_rates(own_terms(), their_face), tile_out, put_out)


def on_device(state, metric, block_map, links):
    segs, chain = lax.axis_size("seg"), lax.axis_size("blk")
    _, parts, length, width = state.shape
    cross = math.isqrt(width)
    assert cross <= HALF and length == 16
    chunk = math.lcm(cross, LANES)
    links = links.transpose(1, 2, 0)
    f32, bf16, dma = jnp.float32, jnp.bfloat16, pltpu.SemaphoreType.DMA
    result = pl.pallas_call(
        functools.partial(kernel, segs, chain, cross),
        out_shape=pltpu.VMEM((parts, length, width), f32),
        in_specs=[pl.BlockSpec(memory_space=pl.ANY)] * 4,
        out_specs=pl.BlockSpec(memory_space=pltpu.VMEM),
        scratch_shapes=[
            pltpu.VMEM((parts, length, width + 2 * LANES), f32),
            pltpu.VMEM((parts, length, width + 2 * LANES), f32),
            pltpu.VMEM((9, length, width), f32),
            pltpu.VMEM((width // LANES, 8, LANES), jnp.int32),
            pltpu.VMEM((width // LANES, 8, LANES), f32),
            pltpu.VMEM((width // LANES, 8, LANES), jnp.int32),
            pltpu.VMEM((width // LANES, 8, LANES), f32),
            pltpu.VMEM((width - width // LANES // 6 * 2 * LANES, LANES), bf16),
            pltpu.VMEM((2 * parts * length, width), bf16),
            pltpu.VMEM((2 * chunk, chunk), bf16),
            pltpu.VMEM((2 * chunk, chunk), bf16),
            pltpu.VMEM((2 * chunk, chunk), bf16),
            pltpu.VMEM((7 * length, LANES), bf16),
            pltpu.VMEM((parts, length, width), f32),
            pltpu.VMEM((parts - 1, length, width), f32),
            pltpu.VMEM((parts, length, width), f32),
            pltpu.VMEM((parts - 1, length, width), f32),
            pltpu.VMEM((parts, length, width), f32),
            pltpu.VMEM((5, length, LANES), f32),
            pltpu.VMEM((parts * length, LANES), f32),
            pltpu.VMEM((parts * length, LANES), f32),
            pltpu.VMEM((parts * length, LANES), f32),
            pltpu.VMEM((2, parts, 8, width), f32),
            pltpu.VMEM((parts, 8, width), f32),
            pltpu.VMEM((parts, 8, LANES), f32),
            pltpu.VMEM((parts, 8, LANES), f32),
            pltpu.VMEM((3, parts * length, LANES), f32),
            pltpu.VMEM((3, segs - 1, parts * length, LANES), f32),
            pltpu.SMEM(block_map.shape, jnp.int32),
            pltpu.SMEM(links.shape, jnp.int32),
            dma((4,)), dma((3, 2)), dma((3, 2)), dma((3, segs - 1)), dma((3, segs - 1)),
        ],
        compiler_params=pltpu.CompilerParams(collective_id=0, has_side_effects=True),
    )(state, metric, block_map, links)
    return result.reshape(state.shape)


def solution(mesh):
    in_specs = (P(("seg", "blk"), None, None, None), P(("seg", "blk"), None, None, None), P(), P())
    out_specs = P(("seg", "blk"), None, None, None)
    return jax.shard_map(
        on_device, mesh=mesh, in_specs=in_specs, out_specs=out_specs, check_vma=False
    )
```
